32 devices in a mesh: grp: 2 (over y), edge: 4 (over z), tx: 2 (over x), rcv: 2 (over core).
Axes of the slice: x: 2, y: 2, z: 4, core: 2. Of those that a mesh axis runs over, the one named last changes fastest.
Arguments:
- fields: bfloat16 [8, 128, 65536], P(('grp', 'tx', 'rcv'), 'edge'), parts along dimension 0, may hold values from -6 to 6
- kblocks: bfloat16 [1024, 12288], P('edge'), may hold values from -0.4375 to 0.4375
- blk_index: int32 [1024, 3], P('edge'), may hold values from 0 to 1023, as said below
- sigma: float32 [131072], P(('grp', 'edge')), parts along dimension 0, may hold values from 0.1 to 3
- rec_edge: int32 [8192, 8], P(('grp', 'edge')), parts along dimension 0, may hold values from 0 to 16383
- rec_weight: float32 [8192, 8], P(('grp', 'edge')), parts along dimension 0, may hold values from -1 to 1
- rec_owner: int32 [8192, 1], P(('grp', 'edge')), parts along dimension 0, may hold values from 0 to 3; in each aligned block of 1024 rows (0 to 1023, 1024 to 2047, ...) at most 256 rows name the same one
- rec_slot: int32 [8192], P(('grp', 'edge')), parts along dimension 0, may hold values from 0 to 1023
Outputs:
- residual: bfloat16 [8, 128, 65536], P(('grp', 'tx', 'rcv'), None, 'edge'), parts along dimension 0
- site_data: float32 [8, 128, 4096], P(('grp', 'tx', 'rcv'), None, 'edge'), parts along dimension 0
The draws below stay inside these ranges and needn't reach their ends.
There are 2 independent parts, one for each index of `grp`. The reference program is written for one: setup_inputs(seed, part) draws one part's arguments, and reference() takes and returns one part's arrays. A program takes and returns all parts, laid end to end along the dimension named above; an argument that names none is the same for every part. Nothing has to cross between parts.
Inputs may be any that keep to these rules, and one draw needn't show every extreme that they name: `blk_index`: entry 0 of row b is b itself; entry 1 is b minus a distance of 1 to 2 and entry 2 is b plus a distance of 1 to 2, each reflected at the ends (a negative index -j becomes j, an index 1023 + j becomes 1024 - 1 - j); the first block row of every edge range takes distance 2 in entry 1 and its last block row takes distance 2 in entry 2. `rec_edge`: receiver r interpolates edges of edge range r // 1024. `rec_owner`: among the 1024 receivers of one edge range at most 256 name the same owner, a bound that some block reaches.
All inputs are finite; a program needn't handle non-finite values.
Results may differ from the reference program's by a relative error of at most 0.001.
Values may be sent and summed in bfloat16 or wider, within the bound.
No kernel may reach another device: no remote copies, remote signals or barrier semaphores. Data moves between devices by JAX's collectives and lax.ppermute only.
A program may use at most 320 MiB of HBM per device.

```python
import math
import jax
import jax.numpy as jnp
import numpy as np
from jax import lax

BS = 64
NNZB = 3
HB = 2
IW = 8
EDEV = 16384
RDEV = 1024
GT = 4
GE = 128
NE = 65536
NB = 1024
NREC = 4096
SDEV = 1024
NSITE = 4096
CAP = 256
N_EDGE = 4


def draw_blk_index(key, part):
    block_ids = jnp.arange(NB, dtype=jnp.int32)
    rows_per = EDEV // BS
    key_one, key_two = jax.random.split(jax.random.fold_in(key, 7))
    below = jax.random.randint(key_one, (NB,), 1, HB + 1, dtype=jnp.int32)
    above = jax.random.randint(key_two, (NB,), 1, HB + 1, dtype=jnp.int32)
    below = jnp.where(block_ids % rows_per == 0, HB, below)
    above = jnp.where(block_ids % rows_per == rows_per - 1, HB, above)

    def reflect(values):
        values = jnp.abs(values)
        return jnp.where(values > NB - 1, 2 * (NB - 1) - values, values)
    return jnp.stack([block_ids, reflect(block_ids - below), reflect(block_ids + above)], axis=1).astype(jnp.int32)


def touch_ends(array, own_key, low, high):
    spot = [jax.random.randint(jax.random.fold_in(own_key, axis), (), 0, length) for axis, length in enumerate(array.shape)]
    main_axis = array.shape.index(max(array.shape))
    beside = spot[:main_axis] + [(spot[main_axis] + 1) % array.shape[main_axis]] + spot[main_axis + 1:]
    return array.at[tuple(spot)].set(low).at[tuple(beside)].set(high)


def levels(stream_key, dims, pieces, smallest, high):
    level, own = 1.0, jax.random.fold_in(stream_key, 6)
    for position, parts in pieces:
        steps = jnp.exp(jax.random.uniform(jax.random.fold_in(own, position), (parts,), jnp.float32, smallest / len(pieces), high / len(pieces)))
        level = level * jnp.repeat(steps, dims[position] // parts).reshape([-1 if axis == position else 1 for axis in range(len(dims))])
    return level


def shared_out(rng, own, number, rows, count, top, limit, lean):
    ranking = jax.random.permutation(rng, count)
    crowded, common = portions_of(count, rows * top, limit, lean, True), portions_of(count, rows * top, limit, lean, False)
    places = jnp.arange(count)

    def named(lengths, rotation):
        used = int((lengths > 0).sum())
        fixed = max(1, used // 4)
        moved = fixed + (places - fixed + rotation * (used - fixed)) % max(1, count - fixed)
        return jnp.zeros((count,), jnp.int32).at[ranking[jnp.where(places < fixed, places, moved)]].set(jnp.asarray(lengths, jnp.int32))

    lengths = jnp.where(number % 4 == 0, named(crowded, number // 4), named(common, number - number // 4 - 1))
    mixed = jax.random.permutation(jax.random.fold_in(own, 3), count)
    giver, receiver = mixed[0:count // 2 * 2:2], mixed[1:count // 2 * 2:2]
    margin = jnp.minimum(lengths[giver] - 1, limit - lengths[receiver]) // 2
    margin = jnp.where((giver == ranking[0]) | (receiver == ranking[0]) | (lengths[receiver] == 0), 0, jnp.maximum(margin, 0))
    moved = jax.random.randint(jax.random.fold_in(own, 4), (count // 2,), 0, 1 << 20) % (margin + 1)
    lengths = lengths.at[giver].add(-moved).at[receiver].add(moved)
    members = jnp.searchsorted(jnp.cumsum(lengths), jnp.arange(rows * top), side="right").astype(jnp.int32)
    grid = members.reshape(top, rows).T
    grid = grid[jax.random.permutation(jax.random.fold_in(own, 1), rows)]
    rotation = jax.random.randint(jax.random.fold_in(own, 2), (rows, 1), 0, top)
    return jnp.take_along_axis(grid, (jnp.arange(top)[None, :] + rotation) % top, axis=1)


def portions_of(amount, total, limit, lean, full):
    weights = [(1 << 20) // math.isqrt(grade ** lean) + 1 for grade in range(1, amount + 1)]
    largest = limit if full else min(limit, max(-(-total // amount), total * weights[0] // sum(weights)))
    least = 1 if total - largest >= amount - 1 else 0
    holding, rest = [largest] + [least] * (amount - 1), total - largest - least * (amount - 1)
    while rest > 0:
        free = [i for i in range(1, amount) if holding[i] < largest] or [i for i in range(1, amount) if holding[i] < limit]
        mass, budget = sum([weights[i] for i in free]), rest
        for i in free:
            addition = min(limit - holding[i], max(1, budget * weights[i] // mass), rest)
            holding[i] = holding[i] + addition
            rest = rest - addition
    return np.array(holding)


def normal_values(key, shape, deviation, limit, pieces=(), kind=jnp.bfloat16):
    level = levels(key, shape, pieces, -0.22, 0.18) if pieces else 1.0
    result = jax.random.normal(key, shape, jnp.float32) * deviation * level
    return jnp.minimum(jnp.maximum(result, -limit), limit).astype(kind)


def setup_inputs(seed: int = 0, part: int = 0) -> dict:
    splits = jax.random.split(jax.random.key(seed), 9)
    own_keys = jax.random.split(jax.random.fold_in(splits[8], part), 9)
    fields = normal_values(own_keys[0], (GT, GE, NE), 1.0, 6.0, ((0, 4), (1, 4)))
    kblocks = normal_values(splits[1], (NB, NNZB * BS * BS), (NNZB * BS) ** -0.5, 0.4375, ((0, 4),))
    blk_index = draw_blk_index(jax.random.fold_in(splits[8], 71), part)
    sigma = jnp.clip(jnp.exp(math.log(3.0) - 3.4011974 * jax.random.uniform(own_keys[3], (NE,), jnp.float32) ** levels(own_keys[3], (NE,), ((0, 4),), -0.2, 0.2)), 0.1, 3.0)
    rec_edge = touch_ends(jax.random.randint(own_keys[4], (NREC, IW), 0, EDEV), jax.random.fold_in(own_keys[4], 1), 0, EDEV - 1).astype(jnp.int32)
    rec_weight = jnp.clip(jax.random.uniform(own_keys[5], (NREC, IW), jnp.float32, -1.0, 1.0) * levels(own_keys[5], (NREC, IW), ((0, 4),), -0.4, 0.0), -1.0, 1.0)
    rec_owner_keys = jax.random.split(jax.random.fold_in(own_keys[6], 1), NREC // RDEV)
    rec_owner_turns = jax.random.permutation(jax.random.fold_in(own_keys[6], 3), NREC // RDEV)
    rec_owner = jax.vmap(lambda own, number: shared_out(jax.random.fold_in(own_keys[6], 2), own, number, RDEV, N_EDGE, 1, CAP, 2))(rec_owner_keys, rec_owner_turns).reshape((NREC, 1))
    rec_slot = touch_ends(jax.random.randint(own_keys[7], (NREC,), 0, SDEV), jax.random.fold_in(own_keys[7], 1), 0, SDEV - 1).astype(jnp.int32)
    return dict(fields=fields, kblocks=kblocks, blk_index=blk_index, sigma=sigma, rec_edge=rec_edge, rec_weight=rec_weight, rec_owner=rec_owner, rec_slot=rec_slot)


def reference(fields, kblocks, blk_index, sigma, rec_edge, rec_weight, rec_owner, rec_slot):
    columns = GT * GE
    panel = fields.reshape(columns, NE)
    panel_blocks = panel.reshape(columns, NB, BS)
    rows_per = EDEV // BS

    def stiff_rows(first_row):
        block_ids = lax.dynamic_slice_in_dim(blk_index, first_row, rows_per, 0)
        block_vals = lax.dynamic_slice_in_dim(kblocks, first_row, rows_per, 0).reshape(rows_per, NNZB, BS, BS).astype(jnp.float32)
        picked = jnp.take(panel_blocks, block_ids, axis=1).astype(jnp.float32)
        return jnp.einsum('cbkj,bkij->cbi', picked, block_vals)

    starts = jnp.arange(N_EDGE, dtype=jnp.int32) * rows_per
    stiffness = lax.map(stiff_rows, starts)
    stiffness = jnp.transpose(stiffness, (1, 0, 2, 3)).reshape(columns, NE)
    paired = panel.astype(jnp.float32).reshape(columns // 2, 2, NE)
    diagonal = jnp.stack([-sigma * paired[:, 1], sigma * paired[:, 0]], axis=1).reshape(columns, NE)
    residual = (stiffness + diagonal).astype(jnp.bfloat16).reshape(GT, GE, NE)
    offsets = (jnp.arange(NREC, dtype=jnp.int32) // RDEV) * EDEV
    global_edges = (offsets[:, None] + rec_edge).astype(jnp.int32)
    interp_vals = jnp.take(panel, global_edges.reshape(-1), axis=1).reshape(columns, NREC, IW).astype(jnp.float32)
    predicted = jnp.sum(interp_vals * rec_weight[None], axis=2)
    site_ids = (rec_owner[:, 0] * SDEV + rec_slot).astype(jnp.int32)
    site_sums = jax.ops.segment_sum(predicted.T, site_ids, num_segments=NSITE)
    site_data = site_sums.T.reshape(GT, GE, NSITE)
    return residual, site_data
```

```python
import functools

import jax
import jax.numpy as jnp
from jax import lax
from jax.experimental import pallas as pl
from jax.experimental.pallas import tpu as pltpu
from jax.sharding import PartitionSpec as P

BS = 64
NNZB = 3
HB = 2
IW = 8
SDEV = 1024

LANE = 128
PAIRS = 8
RIM = BS * HB


def padded_2(shard, sides, width):
    for axis, dim in sides:
        peers, length = (lax.axis_size(axis), shard.shape[dim])
        up = [(i, (i + 1) % peers) for i in range(peers - 1)]
        down = [(j, i) for i, j in up]
        last = lax.slice_in_dim(shard, length - width, length, axis=dim)
        initial = lax.slice_in_dim(shard, 0, width, axis=dim)
        before = lax.ppermute(last, axis, up)
        after = lax.ppermute(initial, axis, down)
        shard = jnp.concatenate([before, shard, after], axis=dim)
    return shard


def plain_device(fields, kblocks, blk_index, sigma, rec_edge, rec_weight, rec_owner, rec_slot):
    peers = lax.axis_size("edge")
    edge_count = sigma.shape[0]
    block_count = edge_count // BS
    rec_count = rec_edge.shape[0]
    rim_width = BS * HB
    tx_local = fields.shape[1] // 2
    first_block = lax.axis_index("edge") * block_count
    local_index = blk_index - first_block + HB
    flat_edges = rec_edge.reshape(-1)
    block_vals = kblocks.reshape(block_count, NNZB, BS, BS)
    source = fields.reshape(1, tx_local, 2, fields.shape[2])
    moved = lax.all_to_all(source, "edge", split_axis=3, concat_axis=0, tiled=True)
    item_count = moved.shape[1]
    columns = peers * item_count * 2
    flat_rows = moved.reshape(columns, edge_count)
    padded = padded_2(flat_rows, (("edge", 1),), rim_width)
    blocks = padded.reshape(columns, block_count + 2 * HB, BS)
    picked = jnp.take(blocks, local_index, axis=1)
    stiffness = jnp.einsum("cbkj,bkij->cbi", picked, block_vals, preferred_element_type=jnp.float32)
    stiffness = stiffness.reshape(columns, edge_count)
    paired = flat_rows.reshape(columns // 2, 2, edge_count).astype(jnp.float32)
    diagonal = jnp.stack([-sigma * paired[:, 1], sigma * paired[:, 0]], axis=1).reshape(
        columns, edge_count
    )
    residual = (stiffness + diagonal).astype(jnp.bfloat16).reshape(1, columns, edge_count)
    interp_vals = (
        jnp.take(flat_rows, flat_edges, axis=1).reshape(columns, rec_count, IW).astype(jnp.float32)
    )
    predicted = jnp.sum(interp_vals * rec_weight[None], axis=2)
    site_ids = rec_owner[:, 0] * SDEV + rec_slot
    local_sums = jax.ops.segment_sum(predicted.T, site_ids, num_segments=peers * SDEV)
    site_table = lax.psum_scatter(local_sums.T, "edge", scatter_dimension=1, tiled=True)
    return (residual, site_table.reshape(1, columns, SDEV))


def shifted(x, shift, peers):
    return lax.ppermute(x, "edge", [(i, (i + shift) % peers) for i in range(peers)])


def from_every_range(x, me, peers):
    pieces = [x] + [shifted(x, s, peers) for s in range(1, peers)]
    held = jnp.concatenate(pieces, axis=0)
    order = (me - jnp.arange(peers)) % peers
    rows = x.shape[0]
    out = jnp.zeros_like(held)
    for s in range(peers):
        out = lax.dynamic_update_slice_in_dim(out, pieces[s], order[s] * rows, axis=0)
    return out


def site_kernel(peers, cols, *refs):
    parts = refs[:peers]
    edge_ref, site_ref, weight_ref, out_ref, turned, picked, pred = refs[peers : peers + 7]
    tables = refs[peers + 7 :]
    step = pl.program_id(0)
    width = parts[0].shape[1]
    recs = site_ref.shape[1]
    per = picked.shape[1]

    def turn(t, _):
        at = pl.multiple_of(t * LANE, LANE)
        tile = jnp.concatenate([part[:, pl.ds(at, LANE)] for part in parts], axis=0)
        turned[pl.ds(pl.multiple_of(step * width + at, LANE), LANE), :] = tile.astype(jnp.float32).T
        return 0

    lax.fori_loop(0, width // LANE, turn, 0)

    @pl.when(step == pl.num_programs(0) - 1)
    def _():
        lane = lax.broadcasted_iota(jnp.int32, (1, LANE), 1) // cols
        lanes = lax.broadcasted_iota(jnp.int32, (per, LANE), 1) // cols
        for table in tables:
            table[...] = jnp.zeros_like(table)

        def receivers(g, _):
            first = g * per

            def gather(r, _):
                for k in range(IW):
                    row = turned[pl.ds(edge_ref[k, first + r], 1), :]
                    for q in range(1, peers):
                        other = turned[pl.ds(edge_ref[q * IW + k, first + r], 1), :]
                        row = jnp.where(lane == q, other, row)
                    picked[k, pl.ds(r, 1), :] = row
                return 0

            lax.fori_loop(0, per, gather, 0, unroll=2)
            weights = weight_ref[pl.ds(pl.multiple_of(first, per), per), :]
            total = jnp.zeros((per, LANE), jnp.float32)
            for k in range(IW):
                total += picked[k] * jnp.take_along_axis(weights, lanes * IW + k, axis=1)
            pred[...] = total

            def scatter(r, _):
                row = pred[pl.ds(r, 1), :]
                for q in range(peers):
                    at = pl.ds(site_ref[q, first + r], 1)
                    tables[q][at, :] = tables[q][at, :] + row
                return 0

            lax.fori_loop(0, per, scatter, 0, unroll=2)
            return 0

        lax.fori_loop(0, recs // per, receivers, 0)
        owned = out_ref.shape[2]

        def back(t, _):
            at = pl.ds(pl.multiple_of(t * LANE, LANE), LANE)
            tile = tables[0][at, :]
            for q in range(1, peers):
                tile = jnp.where(lane == q, tables[q][at, :], tile)
            tile = tile.T
            total = tile[:cols]
            for q in range(1, peers):
                total += tile[q * cols : (q + 1) * cols]
            per_owner = owned // LANE
            out_ref[t // per_owner, :, pl.ds(pl.multiple_of((t % per_owner) * LANE, LANE), LANE)] = total
            return 0

        lax.fori_loop(0, peers * owned // LANE, back, 0)


def site_sums(rows, edges, sites, weights, peers):
    cols, all_edges = rows.shape
    edge_count = all_edges // peers
    steps = 8
    width = edge_count // steps
    per = LANE
    specs = [
        pl.BlockSpec((cols, width), lambda i, q=q: (0, q * steps + i)) for q in range(peers)
    ]
    smem = pl.BlockSpec(memory_space=pltpu.SMEM)
    recs = sites.shape[1]
    return pl.pallas_call(
        functools.partial(site_kernel, peers, cols),
        grid=(steps,),
        in_specs=specs + [smem, smem, pl.BlockSpec(weights.shape, lambda i: (0, 0))],
        out_specs=pl.BlockSpec((peers, cols, SDEV), lambda i: (0, 0, 0)),
        out_shape=jax.ShapeDtypeStruct((peers, cols, SDEV), jnp.float32),
        scratch_shapes=[
            pltpu.VMEM((edge_count, LANE), jnp.float32),
            pltpu.VMEM((IW, per, LANE), jnp.float32),
            pltpu.VMEM((per, LANE), jnp.float32),
        ]
        + [pltpu.VMEM((peers * SDEV, LANE), jnp.float32)] * peers,
        compiler_params=pltpu.CompilerParams(vmem_limit_bytes=32 << 20),
        cost_estimate=pl.CostEstimate(
            flops=2 * recs * peers * IW * 8 * LANE, bytes_accessed=64 << 20, transcendentals=0
        ),
        name="site_sums",
    )(*([rows] * peers), edges, sites, weights)


def band_kernel(off_ref, blocks_ref, band_ref):
    step = pl.program_id(0)
    half = lax.broadcasted_iota(jnp.int32, (1, 2 * BS), 1) // BS

    def pair(t, _):
        band_ref[t] = jnp.zeros_like(band_ref[t])
        for k in range(NNZB):
            block = blocks_ref[t, k]
            for side in range(2):
                off = off_ref[((step * PAIRS + t) * 2 + side) * NNZB + k]
                at = pl.ds(pl.multiple_of(off * BS, BS), BS)
                mine = jnp.where(half == side, block, jnp.zeros_like(block))
                band_ref[t, at, :] = band_ref[t, at, :] + mine
        return 0

    lax.fori_loop(0, PAIRS, pair, 0)


def banded(kblocks, blk_index, first_block):
    count = kblocks.shape[0]
    pairs = count // 2
    local = blk_index - first_block
    base = 2 * (jnp.arange(count, dtype=jnp.int32) // 2) - HB
    window = 2 + 2 * HB
    off = jnp.clip(local - base[:, None], 0, window - 1).reshape(-1)
    blocks = (
        kblocks.reshape(pairs, 2, NNZB, BS, BS)
        .transpose(0, 2, 4, 1, 3)
        .reshape(pairs, NNZB, BS, 2 * BS)
    )
    return pl.pallas_call(
        band_kernel,
        grid_spec=pltpu.PrefetchScalarGridSpec(
            num_scalar_prefetch=1,
            grid=(pairs // PAIRS,),
            in_specs=[pl.BlockSpec((PAIRS, NNZB, BS, 2 * BS), lambda i, off: (i, 0, 0, 0))],
            out_specs=pl.BlockSpec((PAIRS, window * BS, 2 * BS), lambda i, off: (i, 0, 0)),
        ),
        out_shape=jax.ShapeDtypeStruct((pairs, window * BS, 2 * BS), jnp.bfloat16),
        compiler_params=pltpu.CompilerParams(vmem_limit_bytes=16 << 20),
        cost_estimate=pl.CostEstimate(flops=0, bytes_accessed=20 << 20, transcendentals=0),
        name="banded",
    )(off, blocks)


def residual_kernel(peers, cols, me_ref, *refs):
    heads, tails = refs[:peers], refs[peers : 2 * peers]
    band_ref, sigma_ref, swap_ref, out_ref, panel = refs[2 * peers :]
    width = heads[0].shape[1]
    for s in range(peers):
        at = pl.ds(pl.multiple_of(lax.rem(me_ref[0] + peers - s, peers) * cols, cols), cols)
        panel[at, :width] = heads[s][...]
        panel[at, width:] = tails[s][...]
    swapped = jnp.dot(
        swap_ref[...], panel[:, RIM : RIM + width], preferred_element_type=jnp.float32
    )
    turned = swapped * sigma_ref[...]
    for t in range(PAIRS):
        at = t * 2 * BS
        stiff = jnp.dot(
            panel[:, at : at + 2 * (BS + RIM)], band_ref[t], preferred_element_type=jnp.float32
        )
        out_ref[:, at : at + 2 * BS] = (stiff + turned[:, at : at + 2 * BS]).astype(out_ref.dtype)


def residual_of(pieces, band, sigma, me, peers):
    cols = pieces[0].shape[0]
    edge_count = sigma.shape[0]
    columns = peers * cols
    width = PAIRS * 2 * BS
    rim = 2 * RIM
    row = jnp.arange(columns)
    swap = jnp.where(
        (row[:, None] ^ 1) == row[None, :], jnp.where(row[:, None] % 2 == 0, -1.0, 1.0), 0.0
    ).astype(jnp.bfloat16)
    head = pl.BlockSpec((cols, width), lambda i, me: (0, i))
    tail = pl.BlockSpec((cols, rim), lambda i, me: (0, (i + 1) * (width // rim)))
    return pl.pallas_call(
        functools.partial(residual_kernel, peers, cols),
        grid_spec=pltpu.PrefetchScalarGridSpec(
            num_scalar_prefetch=1,
            grid=(edge_count // width,),
            in_specs=[head] * peers
            + [tail] * peers
            + [
                pl.BlockSpec((PAIRS,) + band.shape[1:], lambda i, me: (i, 0, 0)),
                pl.BlockSpec((1, width), lambda i, me: (0, i)),
                pl.BlockSpec((columns, columns), lambda i, me: (0, 0)),
            ],
            out_specs=pl.BlockSpec((columns, width), lambda i, me: (0, i)),
            scratch_shapes=[pltpu.VMEM((columns, width + rim), jnp.bfloat16)],
        ),
        out_shape=jax.ShapeDtypeStruct((columns, edge_count), jnp.bfloat16),
        compiler_params=pltpu.CompilerParams(vmem_limit_bytes=16 << 20),
        cost_estimate=pl.CostEstimate(
            flops=2 * columns * edge_count * 384, bytes_accessed=21 << 20, transcendentals=0
        ),
        name="residual",
    )(me.reshape(1), *pieces, *pieces, band, sigma.reshape(1, edge_count), swap)


def on_device(fields, kblocks, blk_index, sigma, rec_edge, rec_weight, rec_owner, rec_slot):
    peers = lax.axis_size("edge")
    me = lax.axis_index("edge")
    rows = fields[0]
    cols, all_edges = rows.shape
    edge_count = sigma.shape[0]

    sites = (rec_owner[:, 0] * SDEV + rec_slot)[None]
    lists = jnp.concatenate([rec_edge.T, sites], axis=0)
    all_lists = from_every_range(lists[None], me, peers)
    all_weights = from_every_range(rec_weight.T[None], me, peers)

    def piece(target):
        start = target * edge_count
        before = lax.dynamic_slice_in_dim(rows, jnp.maximum(start - RIM, 0), RIM, axis=1)
        body = lax.dynamic_slice_in_dim(rows, start, edge_count, axis=1)
        after = lax.dynamic_slice_in_dim(
            rows, jnp.minimum(start + edge_count, all_edges - RIM), RIM, axis=1
        )
        return jnp.concatenate([before, body, after], axis=1)

    pieces = [piece(me)] + [
        shifted(piece((me + s) % peers), s, peers) for s in range(1, peers)
    ]

    recs = rec_edge.shape[0]
    weights = all_weights.reshape(peers * IW, recs).T
    weights = jnp.pad(weights, ((0, 0), (0, LANE - peers * IW)))
    own = site_sums(
        rows,
        all_lists[:, :IW].reshape(peers * IW, recs),
        all_lists[:, IW],
        weights,
        peers,
    )

    def owned(target):
        return lax.dynamic_index_in_dim(own, target, axis=0, keepdims=False)

    got = [owned(me)] + [shifted(owned((me + s) % peers), s, peers) for s in range(1, peers)]
    site_out = jnp.zeros((peers * cols, SDEV), jnp.float32)
    for s in range(peers):
        site_out = lax.dynamic_update_slice_in_dim(
            site_out, got[s], ((me - s) % peers) * cols, axis=0
        )

    band = banded(kblocks, blk_index, me * (edge_count // BS))
    residual = residual_of(pieces, band, sigma, me, peers)
    return residual[None], site_out[None]


def fits(mesh, fields, sigma, rec_edge):
    peers = mesh.shape["edge"]
    cols = fields.shape[1] // peers
    edge_count = sigma.shape[0] // (mesh.shape["grp"] * peers)
    recs = rec_edge.shape[0] // (mesh.shape["grp"] * peers)
    return (
        cols % 16 == 0
        and cols * peers == LANE
        and peers * IW <= LANE
        and edge_count % (PAIRS * 2 * BS) == 0
        and recs % LANE == 0
    )


def solution(mesh):
    placed = (
        P(("grp", "tx", "rcv"), "edge", None),
        P("edge", None),
        P("edge", None),
        P(("grp", "edge")),
        P(("grp", "edge"), None),
        P(("grp", "edge"), None),
        P(("grp", "edge"), None),
        P(("grp", "edge")),
    )

    def run(fields, kblocks, blk_index, sigma, rec_edge, rec_weight, rec_owner, rec_slot):
        body = on_device if fits(mesh, fields, sigma, rec_edge) else plain_device
        return jax.shard_map(
            body,
            mesh=mesh,
            in_specs=placed,
            out_specs=(P(("grp", "tx", "rcv"), None, "edge"), P(("grp", "tx", "rcv"), None, "edge")),
            check_vma=False,
        )(fields, kblocks, blk_index, sigma, rec_edge, rec_weight, rec_owner, rec_slot)

    return run
```

```python
import functools

import jax
import jax.numpy as jnp
from jax import lax
from jax.experimental import pallas as pl
from jax.experimental.pallas import tpu as pltpu
from jax.sharding import PartitionSpec as P

BS = 64
NNZB = 3
HB = 2
IW = 8
SDEV = 1024

LANE = 128
PAIRS = 8
RIM = BS * HB


def padded_2(shard, sides, width):
    for axis, dim in sides:
        peers, length = (lax.axis_size(axis), shard.shape[dim])
        up = [(i, (i + 1) % peers) for i in range(peers - 1)]
        down = [(j, i) for i, j in up]
        last = lax.slice_in_dim(shard, length - width, length, axis=dim)
        initial = lax.slice_in_dim(shard, 0, width, axis=dim)
        before = lax.ppermute(last, axis, up)
        after = lax.ppermute(initial, axis, down)
        shard = jnp.concatenate([before, shard, after], axis=dim)
    return shard


def plain_device(fields, kblocks, blk_index, sigma, rec_edge, rec_weight, rec_owner, rec_slot):
    peers = lax.axis_size("edge")
    edge_count = sigma.shape[0]
    block_count = edge_count // BS
    rec_count = rec_edge.shape[0]
    rim_width = BS * HB
    tx_local = fields.shape[1] // 2
    first_block = lax.axis_index("edge") * block_count
    local_index = blk_index - first_block + HB
    flat_edges = rec_edge.reshape(-1)
    block_vals = kblocks.reshape(block_count, NNZB, BS, BS)
    source = fields.reshape(1, tx_local, 2, fields.shape[2])
    moved = lax.all_to_all(source, "edge", split_axis=3, concat_axis=0, tiled=True)
    item_count = moved.shape[1]
    columns = peers * item_count * 2
    flat_rows = moved.reshape(columns, edge_count)
    padded = padded_2(flat_rows, (("edge", 1),), rim_width)
    blocks = padded.reshape(columns, block_count + 2 * HB, BS)
    picked = jnp.take(blocks, local_index, axis=1)
    stiffness = jnp.einsum("cbkj,bkij->cbi", picked, block_vals, preferred_element_type=jnp.float32)
    stiffness = stiffness.reshape(columns, edge_count)
    paired = flat_rows.reshape(columns // 2, 2, edge_count).astype(jnp.float32)
    diagonal = jnp.stack([-sigma * paired[:, 1], sigma * paired[:, 0]], axis=1).reshape(
        columns, edge_count
    )
    residual = (stiffness + diagonal).astype(jnp.bfloat16).reshape(1, columns, edge_count)
    interp_vals = (
        jnp.take(flat_rows, flat_edges, axis=1).reshape(columns, rec_count, IW).astype(jnp.float32)
    )
    predicted = jnp.sum(interp_vals * rec_weight[None], axis=2)
    site_ids = rec_owner[:, 0] * SDEV + rec_slot
    local_sums = jax.ops.segment_sum(predicted.T, site_ids, num_segments=peers * SDEV)
    site_table = lax.psum_scatter(local_sums.T, "edge", scatter_dimension=1, tiled=True)
    return (residual, site_table.reshape(1, columns, SDEV))


def shifted(x, shift, peers):
    return lax.ppermute(x, "edge", [(i, (i + shift) % peers) for i in range(peers)])


def site_kernel(peers, me_ref, rows_ref, *refs):
    edge_refs, list_refs = refs[:peers], refs[peers : 2 * peers]
    out_ref, turned, picked, pred = refs[2 * peers : 2 * peers + 4]
    tables = refs[2 * peers + 4 :]
    cols = rows_ref.shape[0]
    edge_count = turned.shape[0]
    recs = edge_refs[0].shape[1]
    per = picked.shape[1]
    ranges = [lax.rem(me_ref[0] + peers - s, peers) for s in range(peers)]

    def turn(t, _):
        at = pl.multiple_of(t * LANE, LANE)
        tile = jnp.concatenate(
            [rows_ref[:, pl.ds(pl.multiple_of(q * edge_count + at, LANE), LANE)] for q in ranges],
            axis=0,
        )
        turned[pl.ds(at, LANE), :] = tile.astype(jnp.float32).T
        return 0

    lax.fori_loop(0, edge_count // LANE, turn, 0, unroll=2)
    lane = lax.broadcasted_iota(jnp.int32, (1, LANE), 1) // cols
    lanes = lax.broadcasted_iota(jnp.int32, (per, LANE), 1) // cols
    for table in tables:
        table[...] = jnp.zeros_like(table)

    def receivers(g, _):
        first = pl.multiple_of(g * per, per)

        def gather(r, _):
            for k in range(IW):
                row = turned[pl.ds(edge_refs[0][k, first + r], 1), :]
                for q in range(1, peers):
                    other = turned[pl.ds(edge_refs[q][k, first + r], 1), :]
                    row = jnp.where(lane == q, other, row)
                picked[k, pl.ds(r, 1), :] = row
            return 0

        lax.fori_loop(0, per, gather, 0, unroll=2)
        weights = [ref[IW : 2 * IW, pl.ds(first, per)] for ref in list_refs]
        weights.append(jnp.zeros((LANE - peers * IW, per), jnp.float32))
        weights = jnp.concatenate(weights, axis=0).T
        total = jnp.zeros((per, LANE), jnp.float32)
        for k in range(IW):
            total += picked[k] * jnp.take_along_axis(weights, lanes * IW + k, axis=1)
        pred[...] = total

        def scatter(r, _):
            row = pred[pl.ds(r, 1), :]
            for q in range(peers):
                at = pl.ds(edge_refs[q][IW, first + r], 1)
                tables[q][at, :] = tables[q][at, :] + row
            return 0

        lax.fori_loop(0, per, scatter, 0, unroll=2)
        return 0

    lax.fori_loop(0, recs // per, receivers, 0)
    owned = out_ref.shape[2]
    per_owner = owned // LANE

    def back(t, _):
        at = pl.ds(pl.multiple_of(t * LANE, LANE), LANE)
        tile = tables[0][at, :]
        for q in range(1, peers):
            tile = jnp.where(lane == q, tables[q][at, :], tile)
        tile = tile.T
        total = tile[:cols]
        for q in range(1, peers):
            total += tile[q * cols : (q + 1) * cols]
        out_ref[t // per_owner, :, pl.ds(pl.multiple_of((t % per_owner) * LANE, LANE), LANE)] = total
        return 0

    lax.fori_loop(0, peers * per_owner, back, 0)


def site_sums(me, rows, lists, peers):
    cols, all_edges = rows.shape
    edge_count = all_edges // peers
    per = LANE
    smem = pl.BlockSpec(memory_space=pltpu.SMEM)
    vmem = pl.BlockSpec(memory_space=pltpu.VMEM)
    recs = lists[0].shape[1]
    edges = [
        jnp.concatenate([x[:IW], x[2 * IW : 2 * IW + 1]], axis=0).astype(jnp.int32) for x in lists
    ]
    return pl.pallas_call(
        functools.partial(site_kernel, peers),
        in_specs=[smem, vmem] + [smem] * peers + [vmem] * peers,
        out_specs=vmem,
        out_shape=jax.ShapeDtypeStruct((peers, cols, SDEV), jnp.float32),
        scratch_shapes=[
            pltpu.VMEM((edge_count, LANE), jnp.float32),
            pltpu.VMEM((IW, per, LANE), jnp.float32),
            pltpu.VMEM((per, LANE), jnp.float32),
        ]
        + [pltpu.VMEM((peers * SDEV, LANE), jnp.float32)] * peers,
        compiler_params=pltpu.CompilerParams(vmem_limit_bytes=24 << 20),
        cost_estimate=pl.CostEstimate(
            flops=2 * recs * peers * IW * 8 * LANE, bytes_accessed=64 << 20, transcendentals=0
        ),
        name="site_sums",
    )(me.reshape(1), rows, *edges, *lists)


def band_kernel(off_ref, blocks_ref, band_ref, lines):
    step = pl.program_id(0)
    count = NNZB * BS // 2
    half = lax.broadcasted_iota(jnp.int32, (1, 2 * BS), 1) // BS

    def pair(t, _):
        for side in range(2):
            both = blocks_ref[2 * t + side].astype(jnp.float32)
            crossed = pltpu.roll(both, BS, 1)
            lines[pl.ds(0, count, stride=2), :] = jnp.where(half == 0, both, crossed)
            lines[pl.ds(1, count, stride=2), :] = jnp.where(half == 0, crossed, both)
            offs = [off_ref[((step * PAIRS + t) * 2 + side) * NNZB + k] for k in range(NNZB)]
            for tile in range(band_ref.shape[2] // (2 * BS)):
                here = half + 2 * tile
                total = jnp.where(here == offs[0], lines[:BS], 0.0)
                for k in range(1, NNZB):
                    total += jnp.where(here == offs[k], lines[k * BS : (k + 1) * BS], 0.0)
                band_ref[t, side * BS : (side + 1) * BS, tile * 2 * BS : (tile + 1) * 2 * BS] = (
                    total.astype(band_ref.dtype)
                )
        return 0

    lax.fori_loop(0, PAIRS, pair, 0)


def banded(kblocks, blk_index, first_block):
    count = kblocks.shape[0]
    pairs = count // 2
    lines = NNZB * BS // 2
    local = blk_index - first_block
    base = 2 * (jnp.arange(count, dtype=jnp.int32) // 2) - HB
    window = 2 + 2 * HB
    off = (local - base[:, None]).reshape(-1)
    return pl.pallas_call(
        band_kernel,
        grid_spec=pltpu.PrefetchScalarGridSpec(
            num_scalar_prefetch=1,
            grid=(pairs // PAIRS,),
            in_specs=[pl.BlockSpec((2 * PAIRS, lines, 2 * BS), lambda i, off: (i, 0, 0))],
            out_specs=pl.BlockSpec((PAIRS, 2 * BS, window * BS), lambda i, off: (i, 0, 0)),
            scratch_shapes=[pltpu.VMEM((2 * lines, 2 * BS), jnp.float32)],
        ),
        out_shape=jax.ShapeDtypeStruct((pairs, 2 * BS, window * BS), jnp.bfloat16),
        compiler_params=pltpu.CompilerParams(vmem_limit_bytes=8 << 20),
        cost_estimate=pl.CostEstimate(flops=0, bytes_accessed=40 << 20, transcendentals=0),
        name="banded",
    )(off, kblocks.reshape(count, lines, 2 * BS))


def residual_kernel(peers, me_ref, *refs):
    pieces = refs[:peers]
    band_ref, sigma_ref, swap_ref, out_ref, panel = refs[peers:]
    cols, length = pieces[0].shape
    step = pl.program_id(0)
    width = PAIRS * 2 * BS
    reach = width + 2 * RIM
    me = me_ref[0]

    @pl.when(step == 0)
    def _():
        panel[...] = jnp.zeros_like(panel)

    first = jnp.where(me == 0, 0, jnp.where(me == peers - 1, -2 * RIM, -RIM))
    want = step * width - RIM - first
    start = jnp.clip(want, 0, length - reach)
    src = pl.ds(pl.multiple_of(start, RIM), reach)
    dst = pl.ds(pl.multiple_of(RIM + start - want, RIM), reach)
    for s in range(peers):
        at = pl.ds(pl.multiple_of(lax.rem(me + peers - s, peers) * cols, cols), cols)
        panel[at, dst] = pieces[s][:, src]
    swapped = jnp.dot(
        swap_ref[...], panel[:, 2 * RIM : 2 * RIM + width], preferred_element_type=jnp.float32
    )
    turned = swapped * sigma_ref[:, pl.ds(pl.multiple_of(step * width, width), width)]
    for t in range(PAIRS):
        at = t * 2 * BS
        stiff = lax.dot_general(
            panel[:, RIM + at : RIM + at + 2 * (BS + RIM)],
            band_ref[step * PAIRS + t],
            (((1,), (1,)), ((), ())),
            preferred_element_type=jnp.float32,
        )
        out_ref[:, at : at + 2 * BS] = (stiff + turned[:, at : at + 2 * BS]).astype(out_ref.dtype)


def residual_of(pieces, band, sigma, me, peers):
    cols = pieces[0].shape[0]
    edge_count = sigma.shape[0]
    columns = peers * cols
    width = PAIRS * 2 * BS
    row = jnp.arange(columns)
    swap = jnp.where(
        (row[:, None] ^ 1) == row[None, :], jnp.where(row[:, None] % 2 == 0, -1.0, 1.0), 0.0
    ).astype(jnp.bfloat16)
    vmem = pl.BlockSpec(memory_space=pltpu.VMEM)
    return pl.pallas_call(
        functools.partial(residual_kernel, peers),
        grid_spec=pltpu.PrefetchScalarGridSpec(
            num_scalar_prefetch=1,
            grid=(edge_count // width,),
            in_specs=[vmem] * (peers + 3),
            out_specs=pl.BlockSpec((columns, width), lambda i, me: (0, i)),
            scratch_shapes=[pltpu.VMEM((columns, width + 4 * RIM), jnp.bfloat16)],
        ),
        out_shape=jax.ShapeDtypeStruct((columns, edge_count), jnp.bfloat16),
        compiler_params=pltpu.CompilerParams(vmem_limit_bytes=24 << 20),
        cost_estimate=pl.CostEstimate(
            flops=2 * columns * edge_count * 384, bytes_accessed=21 << 20, transcendentals=0
        ),
        name="residual",
    )(me.reshape(1), *pieces, band, sigma.reshape(1, edge_count), swap)


def on_device(fields, kblocks, blk_index, sigma, rec_edge, rec_weight, rec_owner, rec_slot):
    peers = lax.axis_size("edge")
    me = lax.axis_index("edge")
    rows = fields[0]
    cols, all_edges = rows.shape
    edge_count = sigma.shape[0]
    shifts = range(1, peers)

    sites = rec_owner.T * SDEV + rec_slot[None]
    mine = jnp.concatenate(
        [rec_edge.T.astype(jnp.float32), rec_weight.T, sites.astype(jnp.float32)], axis=0
    )
    lists = [mine] + [shifted(mine, s, peers) for s in shifts]

    length = edge_count + 2 * RIM

    def piece(target):
        start = jnp.clip(target * edge_count - RIM, 0, all_edges - length)
        return lax.dynamic_slice_in_dim(rows, start, length, axis=1)

    pieces = [piece(me)] + [shifted(piece((me + s) % peers), s, peers) for s in shifts]

    own = site_sums(me, rows, lists, peers)

    def owned(target):
        return lax.dynamic_index_in_dim(own, target, axis=0, keepdims=False)

    got = [owned(me)] + [shifted(owned((me + s) % peers), s, peers) for s in shifts]
    site_out = jnp.zeros((peers * cols, SDEV), jnp.float32)
    for s in range(peers):
        site_out = lax.dynamic_update_slice_in_dim(
            site_out, got[s], ((me - s) % peers) * cols, axis=0
        )

    band = banded(kblocks, blk_index, me * (edge_count // BS))
    residual = residual_of(pieces, band, sigma, me, peers)
    return residual[None], site_out[None]


def fits(mesh, fields, sigma, rec_edge):
    peers = mesh.shape["edge"]
    cols = fields.shape[1] // peers
    edge_count = sigma.shape[0] // (mesh.shape["grp"] * peers)
    recs = rec_edge.shape[0] // (mesh.shape["grp"] * peers)
    return (
        cols % 16 == 0
        and cols * peers == LANE
        and peers * IW <= LANE
        and edge_count % (PAIRS * 2 * BS) == 0
        and recs % LANE == 0
        and peers > 1
    )


def solution(mesh):
    placed = (
        P(("grp", "tx", "rcv"), "edge", None),
        P("edge", None),
        P("edge", None),
        P(("grp", "edge")),
        P(("grp", "edge"), None),
        P(("grp", "edge"), None),
        P(("grp", "edge"), None),
        P(("grp", "edge")),
    )

    def run(fields, kblocks, blk_index, sigma, rec_edge, rec_weight, rec_owner, rec_slot):
        body = on_device if fits(mesh, fields, sigma, rec_edge) else plain_device
        return jax.shard_map(
            body,
            mesh=mesh,
            in_specs=placed,
            out_specs=(P(("grp", "tx", "rcv"), None, "edge"), P(("grp", "tx", "rcv"), None, "edge")),
            check_vma=False,
        )(fields, kblocks, blk_index, sigma, rec_edge, rec_weight, rec_owner, rec_slot)

    return run
```

```python
import functools

import jax
import jax.numpy as jnp
from jax import lax
from jax.experimental import pallas as pl
from jax.experimental.pallas import tpu as pltpu
from jax.sharding import PartitionSpec as P


BS = 64
NNZB = 3
HB = 2
IW = 8
SDEV = 1024

LANE = 128
PAIRS = 8
RIM = BS * HB


def padded_2(shard, sides, width):
    for axis, dim in sides:
        peers, length = (lax.axis_size(axis), shard.shape[dim])
        up = [(i, (i + 1) % peers) for i in range(peers - 1)]
        down = [(j, i) for i, j in up]
        last = lax.slice_in_dim(shard, length - width, length, axis=dim)
        initial = lax.slice_in_dim(shard, 0, width, axis=dim)
        before = lax.ppermute(last, axis, up)
        after = lax.ppermute(initial, axis, down)
        shard = jnp.concatenate([before, shard, after], axis=dim)
    return shard


def plain_device(fields, kblocks, blk_index, sigma, rec_edge, rec_weight, rec_owner, rec_slot):
    peers = lax.axis_size("edge")
    edge_count = sigma.shape[0]
    block_count = edge_count // BS
    rec_count = rec_edge.shape[0]
    rim_width = BS * HB
    tx_local = fields.shape[1] // 2
    first_block = lax.axis_index("edge") * block_count
    local_index = blk_index - first_block + HB
    flat_edges = rec_edge.reshape(-1)
    block_vals = kblocks.reshape(block_count, NNZB, BS, BS)
    source = fields.reshape(1, tx_local, 2, fields.shape[2])
    moved = lax.all_to_all(source, "edge", split_axis=3, concat_axis=0, tiled=True)
    item_count = moved.shape[1]
    columns = peers * item_count * 2
    flat_rows = moved.reshape(columns, edge_count)
    padded = padded_2(flat_rows, (("edge", 1),), rim_width)
    blocks = padded.reshape(columns, block_count + 2 * HB, BS)
    picked = jnp.take(blocks, local_index, axis=1)
    stiffness = jnp.einsum("cbkj,bkij->cbi", picked, block_vals, preferred_element_type=jnp.float32)
    stiffness = stiffness.reshape(columns, edge_count)
    paired = flat_rows.reshape(columns // 2, 2, edge_count).astype(jnp.float32)
    diagonal = jnp.stack([-sigma * paired[:, 1], sigma * paired[:, 0]], axis=1).reshape(
        columns, edge_count
    )
    residual = (stiffness + diagonal).astype(jnp.bfloat16).reshape(1, columns, edge_count)
    interp_vals = (
        jnp.take(flat_rows, flat_edges, axis=1).reshape(columns, rec_count, IW).astype(jnp.float32)
    )
    predicted = jnp.sum(interp_vals * rec_weight[None], axis=2)
    site_ids = rec_owner[:, 0] * SDEV + rec_slot
    local_sums = jax.ops.segment_sum(predicted.T, site_ids, num_segments=peers * SDEV)
    site_table = lax.psum_scatter(local_sums.T, "edge", scatter_dimension=1, tiled=True)
    return (residual, site_table.reshape(1, columns, SDEV))


def shifted(x, shift, peers):
    return lax.ppermute(x, "edge", [(i, (i + shift) % peers) for i in range(peers)])


HBM = pl.BlockSpec(memory_space=pltpu.HBM)
VMEM = pl.BlockSpec(memory_space=pltpu.VMEM)
SMEM = pl.BlockSpec(memory_space=pltpu.SMEM)


def list_kernel(edge_ref, weight_ref, owner_ref, slot_ref, list_ref):
    list_ref[:IW, :] = edge_ref[...].astype(jnp.float32)
    list_ref[IW : 2 * IW, :] = weight_ref[...]
    sites = owner_ref[...] * SDEV + slot_ref[...]
    list_ref[2 * IW :, :] = sites.astype(jnp.float32)


def listed(rec_edge, rec_weight, rec_owner, rec_slot):
    recs = rec_slot.shape[0]
    return pl.pallas_call(
        list_kernel,
        in_specs=[VMEM] * 4,
        out_specs=VMEM,
        out_shape=jax.ShapeDtypeStruct((2 * IW + 1, recs), jnp.float32),
        compiler_params=pltpu.CompilerParams(vmem_limit_bytes=1 << 20),
        name="listed",
    )(rec_edge.T, rec_weight.T, rec_owner.T, rec_slot.reshape(1, recs))


def cut_kernel(peers, me_ref, rows_ref, *refs):
    pieces, held, in_sems, out_sems = refs[: peers - 1], *refs[peers - 1 :]
    me = me_ref[0]
    length = held.shape[2]
    all_edges = rows_ref.shape[1]
    taken, put = [], []
    for s in range(1, peers):
        start = start_of(lax.rem(me + s, peers), peers, all_edges)
        taken.append(
            pltpu.make_async_copy(
                rows_ref.at[:, pl.ds(pl.multiple_of(start, RIM), length)],
                held.at[s - 1],
                in_sems.at[s - 1],
            )
        )
        put.append(pltpu.make_async_copy(held.at[s - 1], pieces[s - 1], out_sems.at[s - 1]))
    for copy in taken:
        copy.start()
    for copy, onward in zip(taken, put):
        copy.wait()
        onward.start()
    for copy in put:
        copy.wait()


def start_of(target, peers, all_edges):
    edge_count = all_edges // peers
    return jnp.clip(target * edge_count - RIM, 0, all_edges - edge_count - 2 * RIM)


def cut(me, rows, peers):
    cols, all_edges = rows.shape
    length = all_edges // peers + 2 * RIM
    piece = jax.ShapeDtypeStruct((cols, length), rows.dtype)
    return pl.pallas_call(
        functools.partial(cut_kernel, peers),
        in_specs=[SMEM, HBM],
        out_specs=[HBM] * (peers - 1),
        out_shape=[piece] * (peers - 1),
        scratch_shapes=[
            pltpu.VMEM((peers - 1, cols, length), rows.dtype),
            pltpu.SemaphoreType.DMA((peers - 1,)),
            pltpu.SemaphoreType.DMA((peers - 1,)),
        ],
        compiler_params=pltpu.CompilerParams(vmem_limit_bytes=8 << 20),
        cost_estimate=pl.CostEstimate(flops=0, bytes_accessed=8 << 20, transcendentals=0),
        name="cut",
    )(me, rows)


def site_kernel(peers, me_ref, rows_ref, *refs):
    list_refs = refs[:peers]
    out_ref, rows, turned, picked, pred, ints, row_sems, int_sems = refs[peers : peers + 8]
    edge_refs = refs[peers + 8 : 2 * peers + 8]
    tables = refs[2 * peers + 8 :]
    cols = rows_ref.shape[0]
    edge_count = turned.shape[0]
    recs = list_refs[0].shape[1]
    per = picked.shape[1]
    parts = row_sems.shape[0]
    width = edge_count // parts

    def fetch(part, s):
        start = lax.rem(me_ref[0] + peers - s, peers) * edge_count + part * width
        return pltpu.make_async_copy(
            rows_ref.at[:, pl.ds(pl.multiple_of(start, LANE), width)],
            rows.at[pl.ds(s * cols, cols), pl.ds(part * width, width)],
            row_sems.at[part, s],
        )

    for part in range(parts):
        for s in range(peers):
            fetch(part, s).start()
    lists = []
    for s in range(peers):
        ints[s, :IW, :] = list_refs[s][:IW, :].astype(jnp.int32)
        ints[s, IW : IW + 1, :] = list_refs[s][2 * IW :, :].astype(jnp.int32)
        lists.append(pltpu.make_async_copy(ints.at[s], edge_refs[s], int_sems.at[s]))
        lists[s].start()
    for table in tables:
        table[...] = jnp.zeros_like(table)

    for part in range(parts):
        for s in range(peers):
            fetch(part, s).wait()

        def turn(t, _, part=part):
            at = pl.multiple_of(part * width + t * LANE, LANE)
            turned[pl.ds(at, LANE), :] = rows[:, pl.ds(at, LANE)].astype(jnp.float32).T
            return 0

        lax.fori_loop(0, width // LANE, turn, 0, unroll=2)
    lane = lax.broadcasted_iota(jnp.int32, (1, LANE), 1) // cols
    lanes = lax.broadcasted_iota(jnp.int32, (per, LANE), 1) // cols
    for copy in lists:
        copy.wait()

    def receivers(g, _):
        first = pl.multiple_of(g * per, per)

        def gather(r, _):
            for k in range(IW):
                row = turned[pl.ds(edge_refs[0][k, first + r], 1), :]
                for q in range(1, peers):
                    other = turned[pl.ds(edge_refs[q][k, first + r], 1), :]
                    row = jnp.where(lane == q, other, row)
                picked[k, pl.ds(r, 1), :] = row
            return 0

        lax.fori_loop(0, per, gather, 0, unroll=2)
        weights = [ref[IW : 2 * IW, pl.ds(first, per)] for ref in list_refs]
        weights.append(jnp.zeros((LANE - peers * IW, per), jnp.float32))
        weights = jnp.concatenate(weights, axis=0).T
        total = jnp.zeros((per, LANE), jnp.float32)
        for k in range(IW):
            total += picked[k] * jnp.take_along_axis(weights, lanes * IW + k, axis=1)
        pred[...] = total

        def scatter(r, _):
            row = pred[pl.ds(r, 1), :]
            for q in range(peers):
                at = pl.ds(edge_refs[q][IW, first + r], 1)
                tables[q][at, :] = tables[q][at, :] + row
            return 0

        lax.fori_loop(0, per, scatter, 0, unroll=2)
        return 0

    lax.fori_loop(0, recs // per, receivers, 0)
    owned = out_ref.shape[2]
    per_owner = owned // LANE

    def back(t, _):
        at = pl.ds(pl.multiple_of(t * LANE, LANE), LANE)
        tile = tables[0][at, :]
        for q in range(1, peers):
            tile = jnp.where(lane == q, tables[q][at, :], tile)
        tile = tile.T
        total = tile[:cols]
        for q in range(1, peers):
            total += tile[q * cols : (q + 1) * cols]
        out_ref[t // per_owner, :, pl.ds(pl.multiple_of((t % per_owner) * LANE, LANE), LANE)] = total
        return 0

    lax.fori_loop(0, peers * per_owner, back, 0)


def site_sums(me, rows, lists, peers):
    cols, all_edges = rows.shape
    edge_count = all_edges // peers
    per = LANE
    parts = 4
    recs = lists[0].shape[1]
    return pl.pallas_call(
        functools.partial(site_kernel, peers),
        in_specs=[SMEM, HBM] + [VMEM] * peers,
        out_specs=VMEM,
        out_shape=jax.ShapeDtypeStruct((peers, cols, SDEV), jnp.float32),
        scratch_shapes=[
            pltpu.VMEM((peers * cols, edge_count), rows.dtype),
            pltpu.VMEM((edge_count, LANE), jnp.float32),
            pltpu.VMEM((IW, per, LANE), jnp.float32),
            pltpu.VMEM((per, LANE), jnp.float32),
            pltpu.VMEM((peers, IW + 1, recs), jnp.int32),
            pltpu.SemaphoreType.DMA((parts, peers)),
            pltpu.SemaphoreType.DMA((peers,)),
        ]
        + [pltpu.SMEM((IW + 1, recs), jnp.int32)] * peers
        + [pltpu.VMEM((peers * SDEV, LANE), jnp.float32)] * peers,
        compiler_params=pltpu.CompilerParams(vmem_limit_bytes=24 << 20),
        cost_estimate=pl.CostEstimate(
            flops=2 * recs * peers * IW * 8 * LANE, bytes_accessed=64 << 20, transcendentals=0
        ),
        name="site_sums",
    )(me, rows, *lists)


def place_kernel(peers, me_ref, _, *refs):
    out_ref = refs[peers]
    cols = refs[0].shape[0]
    for s in range(peers):
        at = lax.rem(me_ref[0] + peers - s, peers) * cols
        out_ref[pl.ds(pl.multiple_of(at, 8), cols), :] = refs[s][...]


def placed_rows(me, after, got, peers):
    cols, width = got[0].shape
    return pl.pallas_call(
        functools.partial(place_kernel, peers),
        in_specs=[SMEM] + [VMEM] * (peers + 1),
        out_specs=VMEM,
        out_shape=jax.ShapeDtypeStruct((peers * cols, width), got[0].dtype),
        compiler_params=pltpu.CompilerParams(vmem_limit_bytes=4 << 20),
        name="placed_rows",
    )(me, after, *got)


def band_kernel(first_ref, index_ref, blocks_ref, band_ref, lines):
    count = NNZB * BS // 2
    half = lax.broadcasted_iota(jnp.int32, (1, 2 * BS), 1) // BS

    def pair(p, _):
        base = 2 * p - HB + first_ref[0]
        for side in range(2):
            both = blocks_ref[2 * p + side].astype(jnp.float32)
            crossed = pltpu.roll(both, BS, 1)
            lines[side, pl.ds(0, count, stride=2), :] = jnp.where(half == 0, both, crossed)
            lines[side, pl.ds(1, count, stride=2), :] = jnp.where(half == 0, crossed, both)
        for side in range(2):
            offs = [index_ref[k, 2 * p + side] - base for k in range(NNZB)]
            for tile in range(band_ref.shape[2] // (2 * BS)):
                here = half + 2 * tile
                total = jnp.where(here == offs[0], lines[side, :BS], 0.0)
                for k in range(1, NNZB):
                    total += jnp.where(here == offs[k], lines[side, k * BS : (k + 1) * BS], 0.0)
                band_ref[p, side * BS : (side + 1) * BS, tile * 2 * BS : (tile + 1) * 2 * BS] = (
                    total.astype(band_ref.dtype)
                )
        return 0

    lax.fori_loop(0, band_ref.shape[0], pair, 0)


def banded(kblocks, blk_index, first_block):
    count = kblocks.shape[0]
    pairs = count // 2
    lines = NNZB * BS // 2
    window = 2 + 2 * HB
    return pl.pallas_call(
        band_kernel,
        in_specs=[SMEM, SMEM, VMEM],
        out_specs=VMEM,
        scratch_shapes=[pltpu.VMEM((2, 2 * lines, 2 * BS), jnp.float32)],
        out_shape=jax.ShapeDtypeStruct((pairs, 2 * BS, window * BS), jnp.bfloat16),
        compiler_params=pltpu.CompilerParams(vmem_limit_bytes=24 << 20),
        cost_estimate=pl.CostEstimate(flops=0, bytes_accessed=40 << 20, transcendentals=0),
        name="banded",
    )(first_block, blk_index.T, kblocks.reshape(count, lines, 2 * BS))


def residual_kernel(peers, me_ref, *refs):
    pieces = refs[: peers - 1]
    rows_ref, band_ref, sigma_ref, out_ref, panel, swap, own, own_sem = refs[peers - 1 :]
    pieces = (own,) + pieces
    cols, length = own.shape
    columns = panel.shape[0]
    step = pl.program_id(0)
    width = PAIRS * 2 * BS
    reach = width + 2 * RIM
    me = me_ref[0]

    @pl.when(step == 0)
    def _():
        at = pl.multiple_of(start_of(me, peers, rows_ref.shape[1]), RIM)
        copy = pltpu.make_async_copy(rows_ref.at[:, pl.ds(at, length)], own, own_sem)
        copy.start()
        panel[...] = jnp.zeros_like(panel)
        row = lax.broadcasted_iota(jnp.int32, (columns, columns), 0)
        col = lax.broadcasted_iota(jnp.int32, (columns, columns), 1)
        sign = jnp.where(row % 2 == 0, -1.0, 1.0)
        swap[...] = jnp.where(row + 1 - 2 * (row % 2) == col, sign, 0.0).astype(swap.dtype)
        copy.wait()

    first = jnp.where(me == 0, 0, jnp.where(me == peers - 1, -2 * RIM, -RIM))
    want = step * width - RIM - first
    start = jnp.clip(want, 0, length - reach)
    src = pl.ds(pl.multiple_of(start, RIM), reach)
    dst = pl.ds(pl.multiple_of(RIM + start - want, RIM), reach)
    for s in range(peers):
        at = pl.ds(pl.multiple_of(lax.rem(me + peers - s, peers) * cols, cols), cols)
        panel[at, dst] = pieces[s][:, src]
    swapped = jnp.dot(
        swap[...], panel[:, 2 * RIM : 2 * RIM + width], preferred_element_type=jnp.float32
    )
    turned = swapped * sigma_ref[:, pl.ds(pl.multiple_of(step * width, width), width)]
    for t in range(PAIRS):
        at = t * 2 * BS
        stiff = lax.dot_general(
            panel[:, RIM + at : RIM + at + 2 * (BS + RIM)],
            band_ref[step * PAIRS + t],
            (((1,), (1,)), ((), ())),
            preferred_element_type=jnp.float32,
        )
        out_ref[:, at : at + 2 * BS] = (stiff + turned[:, at : at + 2 * BS]).astype(out_ref.dtype)


def residual_of(rows, pieces, band, sigma, me, peers):
    cols = pieces[0].shape[0]
    edge_count = sigma.shape[0]
    columns = peers * cols
    width = PAIRS * 2 * BS
    return pl.pallas_call(
        functools.partial(residual_kernel, peers),
        grid_spec=pltpu.PrefetchScalarGridSpec(
            num_scalar_prefetch=1,
            grid=(edge_count // width,),
            in_specs=[VMEM] * (peers - 1) + [HBM, VMEM, VMEM],
            out_specs=pl.BlockSpec((columns, width), lambda i, me: (0, i)),
            scratch_shapes=[
                pltpu.VMEM((columns, width + 4 * RIM), jnp.bfloat16),
                pltpu.VMEM((columns, columns), jnp.bfloat16),
                pltpu.VMEM(pieces[0].shape, rows.dtype),
                pltpu.SemaphoreType.DMA,
            ],
        ),
        out_shape=jax.ShapeDtypeStruct((columns, edge_count), jnp.bfloat16),
        compiler_params=pltpu.CompilerParams(vmem_limit_bytes=24 << 20),
        cost_estimate=pl.CostEstimate(
            flops=2 * columns * edge_count * 384, bytes_accessed=21 << 20, transcendentals=0
        ),
        name="residual",
    )(me, *pieces, rows, band, sigma.reshape(1, edge_count))


def on_device(fields, kblocks, blk_index, sigma, rec_edge, rec_weight, rec_owner, rec_slot):
    return ordered(
        fields, kblocks, blk_index, sigma, rec_edge, rec_weight, rec_owner, rec_slot
    )


def ordered(fields, kblocks, blk_index, sigma, rec_edge, rec_weight, rec_owner, rec_slot):
    peers = lax.axis_size("edge")
    position = lax.axis_index("edge")
    me = position.reshape(1)
    rows = fields[0]
    edge_count = sigma.shape[0]
    shifts = range(1, peers)

    mine = listed(rec_edge, rec_weight, rec_owner, rec_slot)
    lists = [mine] + [shifted(mine, s, peers) for s in shifts]
    rows = pltpu.with_memory_space_constraint(rows, pltpu.HBM)
    parts = cut(me, rows, peers)
    pieces = [shifted(parts[s - 1], s, peers) for s in shifts]
    band = banded(kblocks, blk_index, me * (edge_count // BS))
    own = site_sums(me, rows, lists, peers)

    def owned(target):
        return lax.dynamic_index_in_dim(own, target, axis=0, keepdims=False)

    got = [owned(position)] + [shifted(owned((position + s) % peers), s, peers) for s in shifts]
    residual = residual_of(rows, pieces, band, sigma, me, peers)
    site_out = placed_rows(me, residual[:16, :LANE], got, peers)
    return residual[None], site_out[None]


def fits(mesh, fields, sigma, rec_edge):
    peers = mesh.shape["edge"]
    cols = fields.shape[1] // peers
    edge_count = sigma.shape[0] // (mesh.shape["grp"] * peers)
    recs = rec_edge.shape[0] // (mesh.shape["grp"] * peers)
    return (
        cols % 16 == 0
        and cols * peers == LANE
        and peers * IW <= LANE
        and edge_count % (PAIRS * 2 * BS) == 0
        and recs % LANE == 0
        and peers > 1
    )


def solution(mesh):
    placed = (
        P(("grp", "tx", "rcv"), "edge", None),
        P("edge", None),
        P("edge", None),
        P(("grp", "edge")),
        P(("grp", "edge"), None),
        P(("grp", "edge"), None),
        P(("grp", "edge"), None),
        P(("grp", "edge")),
    )

    def run(fields, kblocks, blk_index, sigma, rec_edge, rec_weight, rec_owner, rec_slot):
        body = on_device if fits(mesh, fields, sigma, rec_edge) else plain_device
        return jax.shard_map(
            body,
            mesh=mesh,
            in_specs=placed,
            out_specs=(P(("grp", "tx", "rcv"), None, "edge"), P(("grp", "tx", "rcv"), None, "edge")),
            check_vma=False,
        )(fields, kblocks, blk_index, sigma, rec_edge, rec_weight, rec_owner, rec_slot)

    return run
```

```python
import functools

import jax
import jax.numpy as jnp
from jax import lax
from jax.experimental import pallas as pl
from jax.experimental.pallas import tpu as pltpu
from jax.sharding import PartitionSpec as P


BS = 64
NNZB = 3
HB = 2
IW = 8
SDEV = 1024

LANE = 128
PAIRS = 8
TRIP = 2
RIM = BS * HB
KEEP = 4 * RIM


def padded_2(shard, sides, width):
    for axis, dim in sides:
        peers, length = (lax.axis_size(axis), shard.shape[dim])
        up = [(i, (i + 1) % peers) for i in range(peers - 1)]
        down = [(j, i) for i, j in up]
        last = lax.slice_in_dim(shard, length - width, length, axis=dim)
        initial = lax.slice_in_dim(shard, 0, width, axis=dim)
        before = lax.ppermute(last, axis, up)
        after = lax.ppermute(initial, axis, down)
        shard = jnp.concatenate([before, shard, after], axis=dim)
    return shard


def plain_device(fields, kblocks, blk_index, sigma, rec_edge, rec_weight, rec_owner, rec_slot):
    peers = lax.axis_size("edge")
    edge_count = sigma.shape[0]
    block_count = edge_count // BS
    rec_count = rec_edge.shape[0]
    rim_width = BS * HB
    tx_local = fields.shape[1] // 2
    first_block = lax.axis_index("edge") * block_count
    local_index = blk_index - first_block + HB
    flat_edges = rec_edge.reshape(-1)
    block_vals = kblocks.reshape(block_count, NNZB, BS, BS)
    source = fields.reshape(1, tx_local, 2, fields.shape[2])
    moved = lax.all_to_all(source, "edge", split_axis=3, concat_axis=0, tiled=True)
    item_count = moved.shape[1]
    columns = peers * item_count * 2
    flat_rows = moved.reshape(columns, edge_count)
    padded = padded_2(flat_rows, (("edge", 1),), rim_width)
    blocks = padded.reshape(columns, block_count + 2 * HB, BS)
    picked = jnp.take(blocks, local_index, axis=1)
    stiffness = jnp.einsum("cbkj,bkij->cbi", picked, block_vals, preferred_element_type=jnp.float32)
    stiffness = stiffness.reshape(columns, edge_count)
    paired = flat_rows.reshape(columns // 2, 2, edge_count).astype(jnp.float32)
    diagonal = jnp.stack([-sigma * paired[:, 1], sigma * paired[:, 0]], axis=1).reshape(
        columns, edge_count
    )
    residual = (stiffness + diagonal).astype(jnp.bfloat16).reshape(1, columns, edge_count)
    interp_vals = (
        jnp.take(flat_rows, flat_edges, axis=1).reshape(columns, rec_count, IW).astype(jnp.float32)
    )
    predicted = jnp.sum(interp_vals * rec_weight[None], axis=2)
    site_ids = rec_owner[:, 0] * SDEV + rec_slot
    local_sums = jax.ops.segment_sum(predicted.T, site_ids, num_segments=peers * SDEV)
    site_table = lax.psum_scatter(local_sums.T, "edge", scatter_dimension=1, tiled=True)
    return (residual, site_table.reshape(1, columns, SDEV))


def shifted(x, shift, peers):
    return lax.ppermute(x, "edge", [(i, (i + shift) % peers) for i in range(peers)])


HBM = pl.BlockSpec(memory_space=pltpu.HBM)
VMEM = pl.BlockSpec(memory_space=pltpu.VMEM)
SMEM = pl.BlockSpec(memory_space=pltpu.SMEM)


def list_kernel(edge_ref, weight_ref, owner_ref, slot_ref, list_ref):
    list_ref[:IW, :] = edge_ref[...].astype(jnp.float32)
    list_ref[IW : 2 * IW, :] = weight_ref[...]
    sites = owner_ref[...] * SDEV + slot_ref[...]
    list_ref[2 * IW :, :] = sites.astype(jnp.float32)


def listed(rec_edge, rec_weight, rec_owner, rec_slot):
    recs = rec_slot.shape[0]
    return pl.pallas_call(
        list_kernel,
        in_specs=[VMEM] * 4,
        out_specs=VMEM,
        out_shape=jax.ShapeDtypeStruct((2 * IW + 1, recs), jnp.float32),
        compiler_params=pltpu.CompilerParams(vmem_limit_bytes=1 << 20),
        name="listed",
    )(rec_edge.T, rec_weight.T, rec_owner.T, rec_slot.reshape(1, recs))


def cut_kernel(peers, low, me_ref, rows_ref, *refs):
    pieces, held, in_sems, out_sems = refs[: peers - 1], *refs[peers - 1 :]
    me = me_ref[0]
    width = held.shape[2]
    taken, put = [], []
    for s in range(1, peers):
        start = start_of(lax.rem(me + s, peers), peers, rows_ref.shape[1]) + low
        taken.append(
            pltpu.make_async_copy(
                rows_ref.at[:, pl.ds(pl.multiple_of(start, RIM), width)],
                held.at[s - 1],
                in_sems.at[s - 1],
            )
        )
        put.append(pltpu.make_async_copy(held.at[s - 1], pieces[s - 1], out_sems.at[s - 1]))
    for copy in taken:
        copy.start()
    for copy, onward in zip(taken, put):
        copy.wait()
        onward.start()
    for copy in put:
        copy.wait()


def start_of(target, peers, all_edges):
    edge_count = all_edges // peers
    return jnp.clip(target * edge_count - RIM, 0, all_edges - edge_count - 2 * RIM)


def cut(me, rows, peers, low, high):
    piece = jax.ShapeDtypeStruct((rows.shape[0], high - low), rows.dtype)
    return pl.pallas_call(
        functools.partial(cut_kernel, peers, low),
        in_specs=[SMEM, HBM],
        out_specs=[HBM] * (peers - 1),
        out_shape=[piece] * (peers - 1),
        scratch_shapes=[
            pltpu.VMEM((peers - 1,) + piece.shape, rows.dtype),
            pltpu.SemaphoreType.DMA((peers - 1,)),
            pltpu.SemaphoreType.DMA((peers - 1,)),
        ],
        compiler_params=pltpu.CompilerParams(vmem_limit_bytes=8 << 20),
        cost_estimate=pl.CostEstimate(flops=0, bytes_accessed=8 << 20, transcendentals=0),
        name="cut",
    )(me, rows)


def site_kernel(peers, me_ref, rows_ref, *refs):
    list_refs = refs[:peers]
    out_ref, rows, turned, picked, pred, ints, row_sems, int_sems = refs[peers : peers + 8]
    count = peers * (IW + 1)
    edge_refs = [
        refs[peers + 8 + s * (IW + 1) : peers + 8 + (s + 1) * (IW + 1)] for s in range(peers)
    ]
    tables = refs[peers + 8 + count :]
    cols = rows_ref.shape[0]
    edge_count = turned.shape[0]
    recs = list_refs[0].shape[1]
    per = picked.shape[1]
    parts = row_sems.shape[0]
    width = edge_count // parts

    def fetch(part, s):
        start = lax.rem(me_ref[0] + peers - s, peers) * edge_count + part * width
        return pltpu.make_async_copy(
            rows_ref.at[:, pl.ds(pl.multiple_of(start, LANE), width)],
            rows.at[pl.ds(s * cols, cols), pl.ds(part * width, width)],
            row_sems.at[part, s],
        )

    for part in range(parts):
        for s in range(peers):
            fetch(part, s).start()
    lists = []
    for s in range(peers):
        ints[s, :IW, :] = list_refs[s][:IW, :].astype(jnp.int32)
        ints[s, IW : IW + 1, :] = list_refs[s][2 * IW :, :].astype(jnp.int32)
        for k in range(IW + 1):
            copy = pltpu.make_async_copy(
                ints.at[s, pl.ds(k, 1)], edge_refs[s][k], int_sems.at[s, k]
            )
            copy.start()
            lists.append(copy)
    for table in tables:
        table[...] = jnp.zeros_like(table)

    for part in range(parts):
        for s in range(peers):
            fetch(part, s).wait()

        def turn(t, _, part=part):
            at = pl.multiple_of(part * width + t * LANE, LANE)
            turned[pl.ds(at, LANE), :] = rows[:, pl.ds(at, LANE)].T.astype(jnp.float32)
            return 0

        lax.fori_loop(0, width // LANE, turn, 0, unroll=2)
    lane = lax.broadcasted_iota(jnp.int32, (1, LANE), 1) // cols
    lanes = lax.broadcasted_iota(jnp.int32, (per, LANE), 1) // cols
    for copy in lists:
        copy.wait()

    def receivers(g, _):
        first = pl.multiple_of(g * per, per)

        def gather(r, _):
            for k in range(IW):
                row = turned[pl.ds(edge_refs[0][k][0, first + r], 1), :]
                for q in range(1, peers):
                    other = turned[pl.ds(edge_refs[q][k][0, first + r], 1), :]
                    row = jnp.where(lane == q, other, row)
                picked[k, pl.ds(r, 1), :] = row
            return 0

        lax.fori_loop(0, per, gather, 0, unroll=4)
        weights = [ref[IW : 2 * IW, pl.ds(first, per)] for ref in list_refs]
        weights.append(jnp.zeros((LANE - peers * IW, per), jnp.float32))
        weights = jnp.concatenate(weights, axis=0).T
        total = jnp.zeros((per, LANE), jnp.float32)
        for k in range(IW):
            total += picked[k] * jnp.take_along_axis(weights, lanes * IW + k, axis=1)
        pred[...] = total

        def scatter(r, _):
            row = pred[pl.ds(r, 1), :]
            for q in range(peers):
                at = pl.ds(edge_refs[q][IW][0, first + r], 1)
                tables[q][at, :] = tables[q][at, :] + row
            return 0

        lax.fori_loop(0, per, scatter, 0, unroll=8)
        return 0

    lax.fori_loop(0, recs // per, receivers, 0)
    owned = out_ref.shape[2]
    per_owner = owned // LANE

    def back(t, _):
        at = pl.ds(pl.multiple_of(t * LANE, LANE), LANE)
        tile = tables[0][at, :]
        for q in range(1, peers):
            tile = jnp.where(lane == q, tables[q][at, :], tile)
        tile = tile.T
        total = tile[:cols]
        for q in range(1, peers):
            total += tile[q * cols : (q + 1) * cols]
        out_ref[t // per_owner, :, pl.ds(pl.multiple_of((t % per_owner) * LANE, LANE), LANE)] = total
        return 0

    lax.fori_loop(0, peers * per_owner, back, 0)


def site_sums(me, rows, lists, peers):
    cols, all_edges = rows.shape
    edge_count = all_edges // peers
    per = LANE
    parts = 4
    recs = lists[0].shape[1]
    return pl.pallas_call(
        functools.partial(site_kernel, peers),
        in_specs=[SMEM, HBM] + [VMEM] * peers,
        out_specs=VMEM,
        out_shape=jax.ShapeDtypeStruct((peers, cols, SDEV), jnp.float32),
        scratch_shapes=[
            pltpu.VMEM((peers * cols, edge_count), rows.dtype),
            pltpu.VMEM((edge_count, LANE), jnp.float32),
            pltpu.VMEM((IW, per, LANE), jnp.float32),
            pltpu.VMEM((per, LANE), jnp.float32),
            pltpu.VMEM((peers, IW + 1, recs), jnp.int32),
            pltpu.SemaphoreType.DMA((parts, peers)),
            pltpu.SemaphoreType.DMA((peers, IW + 1)),
        ]
        + [pltpu.SMEM((1, recs), jnp.int32)] * (peers * (IW + 1))
        + [pltpu.VMEM((peers * SDEV, LANE), jnp.float32)] * peers,
        compiler_params=pltpu.CompilerParams(vmem_limit_bytes=24 << 20),
        cost_estimate=pl.CostEstimate(
            flops=2 * recs * peers * IW * 8 * LANE, bytes_accessed=64 << 20, transcendentals=0
        ),
        name="site_sums",
    )(me, rows, *lists)


def place_kernel(peers, me_ref, _, *refs):
    out_ref = refs[peers]
    cols = refs[0].shape[0]
    for s in range(peers):
        at = lax.rem(me_ref[0] + peers - s, peers) * cols
        out_ref[pl.ds(pl.multiple_of(at, 8), cols), :] = refs[s][...]


def placed_rows(me, after, got, peers):
    cols, width = got[0].shape
    return pl.pallas_call(
        functools.partial(place_kernel, peers),
        in_specs=[SMEM] + [VMEM] * (peers + 1),
        out_specs=VMEM,
        out_shape=jax.ShapeDtypeStruct((peers * cols, width), got[0].dtype),
        compiler_params=pltpu.CompilerParams(vmem_limit_bytes=4 << 20),
        name="placed_rows",
    )(me, after, *got)


def band_kernel(first_ref, index_ref, blocks_ref, band_ref, lines):
    step = pl.program_id(0)
    count = NNZB * BS // 2
    half = lax.broadcasted_iota(jnp.int32, (1, 2 * BS), 1) // BS

    def pairs(trip, _):
        for row in range(2 * TRIP):
            both = blocks_ref[trip * 2 * TRIP + row].astype(jnp.float32)
            crossed = pltpu.roll(both, BS, 1)
            lines[row, pl.ds(0, count, stride=2), :] = jnp.where(half == 0, both, crossed)
            lines[row, pl.ds(1, count, stride=2), :] = jnp.where(half == 0, crossed, both)
        for row in range(2 * TRIP):
            p = step * PAIRS + trip * TRIP + row // 2
            base = 2 * p - HB + first_ref[0]
            offs = [index_ref[k, 2 * p + row % 2] - base for k in range(NNZB)]
            blocks = [
                lines[row, k * BS : (k + 1) * BS].astype(band_ref.dtype) for k in range(NNZB)
            ]
            side = pl.ds(row % 2 * BS, BS)
            for tile in range(band_ref.shape[2] // (2 * BS)):
                masks = [
                    jnp.where(half + 2 * tile == off, 1.0, 0.0).astype(band_ref.dtype) for off in offs
                ]
                total = blocks[0] * masks[0]
                for k in range(1, NNZB):
                    total += blocks[k] * masks[k]
                band_ref[p, side, tile * 2 * BS : (tile + 1) * 2 * BS] = total
        return 0

    lax.fori_loop(0, PAIRS // TRIP, pairs, 0)


def banded(kblocks, blk_index, first_block):
    count = kblocks.shape[0]
    pairs = count // 2
    lines = NNZB * BS // 2
    window = 2 + 2 * HB
    return pl.pallas_call(
        band_kernel,
        grid=(pairs // PAIRS,),
        in_specs=[SMEM, SMEM, pl.BlockSpec((2 * PAIRS, lines, 2 * BS), lambda i: (i, 0, 0))],
        out_specs=VMEM,
        scratch_shapes=[pltpu.VMEM((2 * TRIP, 2 * lines, 2 * BS), jnp.float32)],
        out_shape=jax.ShapeDtypeStruct((pairs, 2 * BS, window * BS), jnp.bfloat16),
        compiler_params=pltpu.CompilerParams(vmem_limit_bytes=24 << 20),
        cost_estimate=pl.CostEstimate(flops=0, bytes_accessed=40 << 20, transcendentals=0),
        name="banded",
    )(
        first_block,
        blk_index.T,
        pltpu.with_memory_space_constraint(kblocks.reshape(count, lines, 2 * BS), pltpu.HBM),
    )


def residual_kernel(peers, first, low, keep, me_ref, *refs):
    pieces = refs[: peers - 1]
    refs = refs[peers - 1 :]
    if keep:
        ends, refs = refs[: peers - 1], refs[peers - 1 :]
    rows_ref, band_ref, sigma_ref = refs[:3]
    out_ref, panel, swap, own, own_sem = refs[3 if keep == 0 else 4 :]
    cols, span = own.shape
    columns = panel.shape[0]
    step = pl.program_id(0)
    width = PAIRS * 2 * BS
    me = me_ref[0]

    @pl.when(step == 0)
    def _():
        at = start_of(me, peers, rows_ref.shape[1]) + (low - keep)
        copy = pltpu.make_async_copy(
            rows_ref.at[:, pl.ds(pl.multiple_of(at, RIM), span)], own, own_sem
        )
        copy.start()
        panel[:, :RIM] = jnp.zeros((columns, RIM), panel.dtype)
        panel[:, RIM + span :] = jnp.zeros((columns, RIM), panel.dtype)
        row = lax.broadcasted_iota(jnp.int32, (columns, columns), 0)
        col = lax.broadcasted_iota(jnp.int32, (columns, columns), 1)
        sign = jnp.where(row % 2 == 0, -1.0, 1.0)
        swap[...] = jnp.where(row + 1 - 2 * (row % 2) == col, sign, 0.0).astype(swap.dtype)
        for s in range(1, peers):
            at = pl.ds(pl.multiple_of(lax.rem(me + peers - s, peers) * cols, cols), cols)
            if keep:
                panel[at, RIM : RIM + keep] = ends[s - 1][:, ends[s - 1].shape[1] - keep :]
            panel[at, RIM + keep : RIM + span] = pieces[s - 1][...]
        copy.wait()
        panel[pl.ds(pl.multiple_of(me * cols, cols), cols), RIM : RIM + span] = own[...]

    moved = jnp.where(me == 0, -RIM, jnp.where(me == peers - 1, RIM, 0))
    start = (step + first) * width + RIM + moved - (low - keep)

    def window(at, size):
        return panel[:, pl.ds(pl.multiple_of(start + at, RIM), size)]

    swapped = jnp.dot(swap[...], window(RIM, width), preferred_element_type=jnp.float32)
    at = pl.multiple_of((step + first) * width, width)
    turned = swapped * sigma_ref[:, pl.ds(at, width)]
    for t in range(PAIRS):
        at = t * 2 * BS
        stiff = lax.dot_general(
            window(at, 2 * (BS + RIM)),
            band_ref[(step + first) * PAIRS + t],
            (((1,), (1,)), ((), ())),
            preferred_element_type=jnp.float32,
        )
        out_ref[:, at : at + 2 * BS] = (stiff + turned[:, at : at + 2 * BS]).astype(out_ref.dtype)


def residual_of(rows, parts, band, sigma, me, peers):
    cols = rows.shape[0]
    edge_count = sigma.shape[0]
    columns = peers * cols
    width = PAIRS * 2 * BS
    sigma = sigma.reshape(1, edge_count)
    out, before = None, None
    for first, steps, low, pieces in parts:
        keep = KEEP if low else 0
        span = keep + pieces[0].shape[1]
        given = list(pieces) + (list(before) if keep else []) + [rows, band, sigma]
        specs = [VMEM] * (len(given) - 3) + [HBM, VMEM, VMEM]
        if out is not None:
            given.append(out)
            specs.append(pl.BlockSpec(memory_space=pl.ANY))
        out = pl.pallas_call(
            functools.partial(residual_kernel, peers, first, low, keep),
            grid_spec=pltpu.PrefetchScalarGridSpec(
                num_scalar_prefetch=1,
                grid=(steps,),
                in_specs=specs,
                out_specs=pl.BlockSpec((columns, width), lambda i, me, first=first: (0, i + first)),
                scratch_shapes=[
                    pltpu.VMEM((columns, span + 2 * RIM), jnp.bfloat16),
                    pltpu.VMEM((columns, columns), jnp.bfloat16),
                    pltpu.VMEM((cols, span), rows.dtype),
                    pltpu.SemaphoreType.DMA,
                ],
            ),
            out_shape=jax.ShapeDtypeStruct((columns, edge_count), jnp.bfloat16),
            input_output_aliases={len(given): 0} if out is not None else {},
            compiler_params=pltpu.CompilerParams(vmem_limit_bytes=24 << 20),
            cost_estimate=pl.CostEstimate(
                flops=2 * columns * steps * width * 384,
                bytes_accessed=(21 << 20) * steps * width // edge_count,
                transcendentals=0,
            ),
            name="residual",
        )(me, *given)
        before = pieces
    return out


def on_device(fields, kblocks, blk_index, sigma, rec_edge, rec_weight, rec_owner, rec_slot):
    return ordered(
        fields, kblocks, blk_index, sigma, rec_edge, rec_weight, rec_owner, rec_slot
    )


def ordered(fields, kblocks, blk_index, sigma, rec_edge, rec_weight, rec_owner, rec_slot):
    peers = lax.axis_size("edge")
    position = lax.axis_index("edge")
    me = position.reshape(1)
    rows = fields[0]
    edge_count = sigma.shape[0]
    shifts = range(1, peers)

    length = edge_count + 2 * RIM
    width = PAIRS * 2 * BS
    steps = edge_count // width
    marks = [0, max(1, steps // 4), steps]
    lanes = [0] + [m * width + KEEP - RIM for m in marks[1:-1]] + [length]

    rows = pltpu.with_memory_space_constraint(rows, pltpu.HBM)
    parts = []
    for j, (low, high) in enumerate(zip(lanes, lanes[1:])):
        blocks = cut(me, rows, peers, low, high)
        pieces = [shifted(blocks[s - 1], s, peers) for s in shifts]
        parts.append((marks[j], marks[j + 1] - marks[j], low, pieces))
    mine = listed(rec_edge, rec_weight, rec_owner, rec_slot)
    lists = [mine] + [shifted(mine, s, peers) for s in shifts]
    band = banded(kblocks, blk_index, me * (edge_count // BS))
    own = site_sums(me, rows, lists, peers)

    def owned(target):
        return lax.dynamic_index_in_dim(own, target, axis=0, keepdims=False)

    got = [owned(position)] + [shifted(owned((position + s) % peers), s, peers) for s in shifts]
    residual = residual_of(rows, parts, band, sigma, me, peers)
    site_out = placed_rows(me, residual[:16, :LANE], got, peers)
    return residual[None], site_out[None]


def fits(mesh, fields, sigma, rec_edge):
    peers = mesh.shape["edge"]
    cols = fields.shape[1] // peers
    edge_count = sigma.shape[0] // (mesh.shape["grp"] * peers)
    recs = rec_edge.shape[0] // (mesh.shape["grp"] * peers)
    return (
        cols % 16 == 0
        and cols * peers == LANE
        and peers * IW <= LANE
        and edge_count % (PAIRS * 2 * BS) == 0
        and edge_count >= 4 * PAIRS * 2 * BS
        and recs % LANE == 0
        and peers > 1
    )


def solution(mesh):
    placed = (
        P(("grp", "tx", "rcv"), "edge", None),
        P("edge", None),
        P("edge", None),
        P(("grp", "edge")),
        P(("grp", "edge"), None),
        P(("grp", "edge"), None),
        P(("grp", "edge"), None),
        P(("grp", "edge")),
    )

    def run(fields, kblocks, blk_index, sigma, rec_edge, rec_weight, rec_owner, rec_slot):
        body = on_device if fits(mesh, fields, sigma, rec_edge) else plain_device
        return jax.shard_map(
            body,
            mesh=mesh,
            in_specs=placed,
            out_specs=(P(("grp", "tx", "rcv"), None, "edge"), P(("grp", "tx", "rcv"), None, "edge")),
            check_vma=False,
        )(fields, kblocks, blk_index, sigma, rec_edge, rec_weight, rec_owner, rec_slot)

    return run
```

```python
import functools
import math

import jax
import jax.numpy as jnp
from jax import lax
from jax.experimental import pallas as pl
from jax.experimental.pallas import tpu as pltpu
from jax.sharding import PartitionSpec as P


BS = 64
NNZB = 3
HB = 2
IW = 8
SDEV = 1024

LANE = 128
PAIRS = 8
TRIP = 2
RIM = BS * HB
KEEP = 4 * RIM
LINES = 2 * IW + 8
TOP = 32000.0


def padded_2(shard, sides, width):
    for axis, dim in sides:
        peers, length = (lax.axis_size(axis), shard.shape[dim])
        up = [(i, (i + 1) % peers) for i in range(peers - 1)]
        down = [(j, i) for i, j in up]
        last = lax.slice_in_dim(shard, length - width, length, axis=dim)
        initial = lax.slice_in_dim(shard, 0, width, axis=dim)
        before = lax.ppermute(last, axis, up)
        after = lax.ppermute(initial, axis, down)
        shard = jnp.concatenate([before, shard, after], axis=dim)
    return shard


def plain_device(fields, kblocks, blk_index, sigma, rec_edge, rec_weight, rec_owner, rec_slot):
    peers = lax.axis_size("edge")
    edge_count = sigma.shape[0]
    block_count = edge_count // BS
    rec_count = rec_edge.shape[0]
    rim_width = BS * HB
    tx_local = fields.shape[1] // 2
    first_block = lax.axis_index("edge") * block_count
    local_index = blk_index - first_block + HB
    flat_edges = rec_edge.reshape(-1)
    block_vals = kblocks.reshape(block_count, NNZB, BS, BS)
    source = fields.reshape(1, tx_local, 2, fields.shape[2])
    moved = lax.all_to_all(source, "edge", split_axis=3, concat_axis=0, tiled=True)
    item_count = moved.shape[1]
    columns = peers * item_count * 2
    flat_rows = moved.reshape(columns, edge_count)
    padded = padded_2(flat_rows, (("edge", 1),), rim_width)
    blocks = padded.reshape(columns, block_count + 2 * HB, BS)
    picked = jnp.take(blocks, local_index, axis=1)
    stiffness = jnp.einsum("cbkj,bkij->cbi", picked, block_vals, preferred_element_type=jnp.float32)
    stiffness = stiffness.reshape(columns, edge_count)
    paired = flat_rows.reshape(columns // 2, 2, edge_count).astype(jnp.float32)
    diagonal = jnp.stack([-sigma * paired[:, 1], sigma * paired[:, 0]], axis=1).reshape(
        columns, edge_count
    )
    residual = (stiffness + diagonal).astype(jnp.bfloat16).reshape(1, columns, edge_count)
    interp_vals = (
        jnp.take(flat_rows, flat_edges, axis=1).reshape(columns, rec_count, IW).astype(jnp.float32)
    )
    predicted = jnp.sum(interp_vals * rec_weight[None], axis=2)
    site_ids = rec_owner[:, 0] * SDEV + rec_slot
    local_sums = jax.ops.segment_sum(predicted.T, site_ids, num_segments=peers * SDEV)
    site_table = lax.psum_scatter(local_sums.T, "edge", scatter_dimension=1, tiled=True)
    return (residual, site_table.reshape(1, columns, SDEV))


def shifted(x, shift, peers):
    return lax.ppermute(x, "edge", [(i, (i + shift) % peers) for i in range(peers)])


HBM = pl.BlockSpec(memory_space=pltpu.HBM)
VMEM = pl.BlockSpec(memory_space=pltpu.VMEM)
SMEM = pl.BlockSpec(memory_space=pltpu.SMEM)


def pack_kernel(peers, lanes, me_ref, edge_ref, weight_ref, owner_ref, slot_ref, rows_ref, *refs):
    parts = len(lanes) - 1
    count = parts * (peers - 1)
    list_ref, pieces, refs = refs[0], refs[1 : 1 + count], refs[1 + count :]
    edges, weights, owners, slots, list_sems, in_sems, out_sems = refs[:7]
    held = refs[7:]
    recs = list_ref.shape[1]
    share = pl.ds(pl.multiple_of(me_ref[1] * recs, recs), recs)
    small = [
        pltpu.make_async_copy(source.at[:, share], target, list_sems.at[i])
        for i, (source, target) in enumerate(
            [(edge_ref, edges), (weight_ref, weights), (owner_ref, owners), (slot_ref, slots)]
        )
    ]
    for copy in small:
        copy.start()
    taken, put = [], []
    for j in range(parts):
        for s in range(1, peers):
            target = lax.rem(me_ref[0] + s, peers)
            start = start_of(target, peers, rows_ref.shape[1]) + lanes[j]
            n = len(taken)
            taken.append(
                pltpu.make_async_copy(
                    rows_ref.at[:, pl.ds(pl.multiple_of(start, RIM), lanes[j + 1] - lanes[j])],
                    held[n],
                    in_sems.at[n],
                )
            )
            put.append(pltpu.make_async_copy(held[n], pieces[n], out_sems.at[n]))
    for copy in taken:
        copy.start()
    for copy in small:
        copy.wait()
    list_ref[:IW, :] = edges[...].astype(jnp.float32)
    list_ref[IW : 2 * IW, :] = weights[...]
    sites = (owners[...] * SDEV + slots[...]).astype(jnp.float32)
    list_ref[2 * IW :, :] = jnp.broadcast_to(sites, (LINES - 2 * IW, recs))
    for copy, onward in zip(taken, put):
        copy.wait()
        onward.start()
    for copy in put:
        copy.wait()


def start_of(target, peers, all_edges):
    edge_count = all_edges // peers
    return jnp.clip(target * edge_count - RIM, 0, all_edges - edge_count - 2 * RIM)


def packed(me, rec_edge, rec_weight, rec_owner, rec_slot, rows, peers, lanes, shares):
    recs = rec_slot.shape[0]
    share = recs // shares
    cols = rows.shape[0]
    shapes = [
        (cols, high - low) for low, high in zip(lanes, lanes[1:]) for _ in range(1, peers)
    ]
    small = [rec_edge.T, rec_weight.T, rec_owner.T, rec_slot.reshape(1, recs)]
    out = pl.pallas_call(
        functools.partial(pack_kernel, peers, lanes),
        in_specs=[SMEM] + [HBM] * 5,
        out_specs=[VMEM] + [HBM] * len(shapes),
        out_shape=[jax.ShapeDtypeStruct((LINES, share), jnp.float32)]
        + [jax.ShapeDtypeStruct(shape, rows.dtype) for shape in shapes],
        scratch_shapes=[pltpu.VMEM((x.shape[0], share), x.dtype) for x in small]
        + [
            pltpu.SemaphoreType.DMA((len(small),)),
            pltpu.SemaphoreType.DMA((len(shapes),)),
            pltpu.SemaphoreType.DMA((len(shapes),)),
        ]
        + [pltpu.VMEM(shape, rows.dtype) for shape in shapes],
        compiler_params=pltpu.CompilerParams(vmem_limit_bytes=8 << 20),
        cost_estimate=pl.CostEstimate(flops=0, bytes_accessed=8 << 20, transcendentals=0),
        name="packed",
    )(me, *[pltpu.with_memory_space_constraint(x, pltpu.HBM) for x in small], rows)
    return out[0], out[1:]


def site_kernel(peers, shares, me_ref, rows_ref, *refs):
    list_refs, refs = refs[:shares], refs[shares:]
    own_ref, sent_refs, refs = refs[0], refs[1:peers], refs[peers:]
    out_ref, rows, turned, picked, pred, ints, scale, row_sems, int_sems = refs[:9]
    refs = refs[9:]
    edge_refs = [refs[s * (IW + 1) : (s + 1) * (IW + 1)] for s in range(peers)]
    tables = refs[peers * (IW + 1) :]
    cols = rows_ref.shape[0]
    edge_count = turned.shape[0]
    share = list_refs[0].shape[1]
    recs = shares * share
    per = picked.shape[1]
    parts = row_sems.shape[0]
    width = edge_count // parts

    def fetch(part, s):
        start = lax.rem(me_ref[0] + peers - s, peers) * edge_count + part * width
        return pltpu.make_async_copy(
            rows_ref.at[:, pl.ds(pl.multiple_of(start, LANE), width)],
            rows.at[pl.ds(s * cols, cols), pl.ds(part * width, width)],
            row_sems.at[part, s],
        )

    for part in range(parts):
        for s in range(peers):
            fetch(part, s).start()
    lists = []
    for s in range(peers):
        for j, ref in enumerate(list_refs):
            at = slice(j * share, (j + 1) * share)
            edges = ref[s * LINES : s * LINES + IW, :]
            ints[s, :IW, at] = edges.astype(jnp.int32)
            scale[s * IW : (s + 1) * IW, at] = ref[s * LINES + IW : s * LINES + 2 * IW, :]
            sites = ref[s * LINES + 2 * IW : (s + 1) * LINES, :]
            ints[s, IW:, at] = sites.astype(jnp.int32)
        for k in range(IW + 1):
            copy = pltpu.make_async_copy(
                ints.at[s, pl.ds(k, 1)], edge_refs[s][k], int_sems.at[s, k]
            )
            copy.start()
            lists.append(copy)
    scale[peers * IW :, :] = jnp.zeros((LANE - peers * IW, recs), jnp.float32)
    for table in tables:
        table[...] = jnp.zeros_like(table)

    for part in range(parts):
        for s in range(peers):
            fetch(part, s).wait()

        def turn(t, _, part=part):
            at = pl.multiple_of(part * width + t * LANE, LANE)
            turned[pl.ds(at, LANE), :] = rows[:, pl.ds(at, LANE)].T.astype(jnp.float32)
            return 0

        lax.fori_loop(0, width // LANE, turn, 0, unroll=2)
    lane = lax.broadcasted_iota(jnp.int32, (1, LANE), 1) // cols
    lanes = lax.broadcasted_iota(jnp.int32, (per, LANE), 1) // cols
    for copy in lists:
        copy.wait()

    def receivers(g, _):
        first = pl.multiple_of(g * per, per)

        def gather(r, _):
            for k in range(IW):
                row = turned[pl.ds(edge_refs[0][k][0, first + r], 1), :]
                for q in range(1, peers):
                    other = turned[pl.ds(edge_refs[q][k][0, first + r], 1), :]
                    row = jnp.where(lane == q, other, row)
                picked[k, pl.ds(r, 1), :] = row
            return 0

        lax.fori_loop(0, per, gather, 0, unroll=4)
        weights = scale[:, pl.ds(first, per)].T
        total = jnp.zeros((per, LANE), jnp.float32)
        for k in range(IW):
            total += picked[k] * jnp.take_along_axis(weights, lanes * IW + k, axis=1)
        pred[...] = total

        def scatter(r, _):
            row = pred[pl.ds(r, 1), :]
            for q in range(peers):
                at = pl.ds(edge_refs[q][IW][0, first + r], 1)
                tables[q][at, :] = tables[q][at, :] + row
            return 0

        lax.fori_loop(0, per, scatter, 0, unroll=8)
        return 0

    lax.fori_loop(0, recs // per, receivers, 0)
    owned = out_ref.shape[2]
    per_owner = owned // LANE

    def back(t, _):
        at = pl.ds(pl.multiple_of(t * LANE, LANE), LANE)
        tile = tables[0][at, :]
        for q in range(1, peers):
            tile = jnp.where(lane == q, tables[q][at, :], tile)
        tile = tile.T
        total = tile[:cols]
        for q in range(1, peers):
            total += tile[q * cols : (q + 1) * cols]
        out_ref[t // per_owner, :, pl.ds(pl.multiple_of((t % per_owner) * LANE, LANE), LANE)] = total
        return 0

    lax.fori_loop(0, peers * per_owner, back, 0)
    own_ref[...] = out_ref[me_ref[0]]
    for s in range(1, peers):
        block = out_ref[lax.rem(me_ref[0] + s, peers)]
        most = jnp.max(jnp.abs(block), axis=1, keepdims=True)
        power = jnp.floor(jnp.log(jnp.maximum(most, 1e-36)) * (1 / math.log(2.0))) + 1.0
        coded = jnp.round(block * (TOP * jnp.exp2(-power)))
        sent_refs[s - 1][:, :owned] = coded.astype(jnp.int32).astype(jnp.int16)
        power = jnp.broadcast_to(power, (cols, LANE))
        sent_refs[s - 1][:, owned:] = power.astype(jnp.int32).astype(jnp.int16)


def site_sums(me, rows, lists, peers):
    cols, all_edges = rows.shape
    edge_count = all_edges // peers
    per = LANE
    parts = 4
    shares = len(lists)
    recs = lists[0].shape[1] * shares
    sent = jax.ShapeDtypeStruct((cols, SDEV + LANE), jnp.int16)
    out = pl.pallas_call(
        functools.partial(site_kernel, peers, shares),
        in_specs=[SMEM, HBM] + [VMEM] * shares,
        out_specs=[VMEM] * peers,
        out_shape=[jax.ShapeDtypeStruct((cols, SDEV), jnp.float32)] + [sent] * (peers - 1),
        scratch_shapes=[
            pltpu.VMEM((peers, cols, SDEV), jnp.float32),
            pltpu.VMEM((peers * cols, edge_count), rows.dtype),
            pltpu.VMEM((edge_count, LANE), jnp.float32),
            pltpu.VMEM((IW, per, LANE), jnp.float32),
            pltpu.VMEM((per, LANE), jnp.float32),
            pltpu.VMEM((peers, IW + 8, recs), jnp.int32),
            pltpu.VMEM((LANE, recs), jnp.float32),
            pltpu.SemaphoreType.DMA((parts, peers)),
            pltpu.SemaphoreType.DMA((peers, IW + 1)),
        ]
        + [pltpu.SMEM((1, recs), jnp.int32)] * (peers * (IW + 1))
        + [pltpu.VMEM((peers * SDEV, LANE), jnp.float32)] * peers,
        compiler_params=pltpu.CompilerParams(vmem_limit_bytes=24 << 20),
        cost_estimate=pl.CostEstimate(
            flops=2 * recs * peers * IW * 8 * LANE, bytes_accessed=64 << 20, transcendentals=0
        ),
        name="site_sums",
    )(me, rows, *lists)
    return out[0], out[1:]


def place_kernel(peers, me_ref, _, *refs):
    out_ref = refs[peers]
    cols, width = refs[0].shape
    for s in range(peers):
        at = lax.rem(me_ref[0] + peers - s, peers) * cols
        block = refs[s][:, :width].astype(jnp.int32) if s else refs[s][...]
        if s:
            power = refs[s][:, width:].astype(jnp.int32).astype(jnp.float32)
            block = block.astype(jnp.float32) * (jnp.exp2(power[:, :1]) * (1 / TOP))
        out_ref[pl.ds(pl.multiple_of(at, 8), cols), :] = block


def placed_rows(me, after, got, peers):
    cols, width = got[0].shape
    return pl.pallas_call(
        functools.partial(place_kernel, peers),
        in_specs=[SMEM] + [VMEM] * (peers + 1),
        out_specs=VMEM,
        out_shape=jax.ShapeDtypeStruct((peers * cols, width), got[0].dtype),
        compiler_params=pltpu.CompilerParams(vmem_limit_bytes=4 << 20),
        name="placed_rows",
    )(me, after, *got)


def band_kernel(first_ref, index_ref, blocks_ref, band_ref, lines):
    step = pl.program_id(0)
    count = NNZB * BS // 2
    half = lax.broadcasted_iota(jnp.int32, (1, 2 * BS), 1) // BS

    def pairs(trip, _):
        for row in range(2 * TRIP):
            both = blocks_ref[trip * 2 * TRIP + row].astype(jnp.float32)
            crossed = pltpu.roll(both, BS, 1)
            lines[row, pl.ds(0, count, stride=2), :] = jnp.where(half == 0, both, crossed)
            lines[row, pl.ds(1, count, stride=2), :] = jnp.where(half == 0, crossed, both)
        for row in range(2 * TRIP):
            p = step * PAIRS + trip * TRIP + row // 2
            base = 2 * p - HB + first_ref[0]
            offs = [index_ref[k, 2 * p + row % 2] - base for k in range(NNZB)]
            blocks = [
                lines[row, k * BS : (k + 1) * BS].astype(band_ref.dtype) for k in range(NNZB)
            ]
            side = pl.ds(row % 2 * BS, BS)
            for tile in range(band_ref.shape[2] // (2 * BS)):
                masks = [
                    jnp.where(half + 2 * tile == off, 1.0, 0.0).astype(band_ref.dtype) for off in offs
                ]
                total = blocks[0] * masks[0]
                for k in range(1, NNZB):
                    total += blocks[k] * masks[k]
                band_ref[p, side, tile * 2 * BS : (tile + 1) * 2 * BS] = total
        return 0

    lax.fori_loop(0, PAIRS // TRIP, pairs, 0)


def banded(kblocks, blk_index, first_block):
    count = kblocks.shape[0]
    pairs = count // 2
    lines = NNZB * BS // 2
    window = 2 + 2 * HB
    return pl.pallas_call(
        band_kernel,
        grid=(pairs // PAIRS,),
        in_specs=[SMEM, SMEM, pl.BlockSpec((2 * PAIRS, lines, 2 * BS), lambda i: (i, 0, 0))],
        out_specs=VMEM,
        scratch_shapes=[pltpu.VMEM((2 * TRIP, 2 * lines, 2 * BS), jnp.float32)],
        out_shape=jax.ShapeDtypeStruct((pairs, 2 * BS, window * BS), jnp.bfloat16),
        compiler_params=pltpu.CompilerParams(vmem_limit_bytes=24 << 20),
        cost_estimate=pl.CostEstimate(flops=0, bytes_accessed=40 << 20, transcendentals=0),
        name="banded",
    )(
        first_block,
        blk_index.T,
        pltpu.with_memory_space_constraint(kblocks.reshape(count, lines, 2 * BS), pltpu.HBM),
    )


def residual_kernel(peers, first, low, keep, me_ref, *refs):
    pieces = refs[: peers - 1]
    refs = refs[peers - 1 :]
    if keep:
        ends, refs = refs[: peers - 1], refs[peers - 1 :]
    rows_ref, band_ref, sigma_ref = refs[:3]
    out_ref, panel, swap, own, own_sem = refs[3 if keep == 0 else 4 :]
    cols, span = own.shape
    columns = panel.shape[0]
    step = pl.program_id(0)
    width = PAIRS * 2 * BS
    me = me_ref[0]

    @pl.when(step == 0)
    def _():
        at = start_of(me, peers, rows_ref.shape[1]) + (low - keep)
        copy = pltpu.make_async_copy(
            rows_ref.at[:, pl.ds(pl.multiple_of(at, RIM), span)], own, own_sem
        )
        copy.start()
        panel[:, :RIM] = jnp.zeros((columns, RIM), panel.dtype)
        panel[:, RIM + span :] = jnp.zeros((columns, RIM), panel.dtype)
        row = lax.broadcasted_iota(jnp.int32, (columns, columns), 0)
        col = lax.broadcasted_iota(jnp.int32, (columns, columns), 1)
        sign = jnp.where(row % 2 == 0, -1.0, 1.0)
        swap[...] = jnp.where(row + 1 - 2 * (row % 2) == col, sign, 0.0).astype(swap.dtype)
        for s in range(1, peers):
            at = pl.ds(pl.multiple_of(lax.rem(me + peers - s, peers) * cols, cols), cols)
            if keep:
                panel[at, RIM : RIM + keep] = ends[s - 1][:, ends[s - 1].shape[1] - keep :]
            panel[at, RIM + keep : RIM + span] = pieces[s - 1][...]
        copy.wait()
        panel[pl.ds(pl.multiple_of(me * cols, cols), cols), RIM : RIM + span] = own[...]

    moved = jnp.where(me == 0, -RIM, jnp.where(me == peers - 1, RIM, 0))
    start = (step + first) * width + RIM + moved - (low - keep)

    def window(at, size):
        return panel[:, pl.ds(pl.multiple_of(start + at, RIM), size)]

    swapped = jnp.dot(swap[...], window(RIM, width), preferred_element_type=jnp.float32)
    at = pl.multiple_of((step + first) * width, width)
    turned = swapped * sigma_ref[:, pl.ds(at, width)]
    for t in range(PAIRS):
        at = t * 2 * BS
        stiff = lax.dot_general(
            window(at, 2 * (BS + RIM)),
            band_ref[(step + first) * PAIRS + t],
            (((1,), (1,)), ((), ())),
            preferred_element_type=jnp.float32,
        )
        out_ref[:, at : at + 2 * BS] = (stiff + turned[:, at : at + 2 * BS]).astype(out_ref.dtype)


def residual_of(rows, parts, band, sigma, me, peers):
    cols = rows.shape[0]
    edge_count = sigma.shape[0]
    columns = peers * cols
    width = PAIRS * 2 * BS
    sigma = sigma.reshape(1, edge_count)
    out, before = None, None
    for first, steps, low, pieces in parts:
        keep = KEEP if low else 0
        span = keep + pieces[0].shape[1]
        given = list(pieces) + (list(before) if keep else []) + [rows, band, sigma]
        specs = [VMEM] * (len(given) - 3) + [HBM, VMEM, VMEM]
        if out is not None:
            given.append(out)
            specs.append(pl.BlockSpec(memory_space=pl.ANY))
        out = pl.pallas_call(
            functools.partial(residual_kernel, peers, first, low, keep),
            grid_spec=pltpu.PrefetchScalarGridSpec(
                num_scalar_prefetch=1,
                grid=(steps,),
                in_specs=specs,
                out_specs=pl.BlockSpec((columns, width), lambda i, me, first=first: (0, i + first)),
                scratch_shapes=[
                    pltpu.VMEM((columns, span + 2 * RIM), jnp.bfloat16),
                    pltpu.VMEM((columns, columns), jnp.bfloat16),
                    pltpu.VMEM((cols, span), rows.dtype),
                    pltpu.SemaphoreType.DMA,
                ],
            ),
            out_shape=jax.ShapeDtypeStruct((columns, edge_count), jnp.bfloat16),
            input_output_aliases={len(given): 0} if out is not None else {},
            compiler_params=pltpu.CompilerParams(vmem_limit_bytes=24 << 20),
            cost_estimate=pl.CostEstimate(
                flops=2 * columns * steps * width * 384,
                bytes_accessed=(21 << 20) * steps * width // edge_count,
                transcendentals=0,
            ),
            name="residual",
        )(me, *given)
        before = pieces
    return out


def on_device(fields, kblocks, blk_index, sigma, rec_edge, rec_weight, rec_owner, rec_slot):
    return ordered(
        fields, kblocks, blk_index, sigma, rec_edge, rec_weight, rec_owner, rec_slot
    )


def ordered(fields, kblocks, blk_index, sigma, rec_edge, rec_weight, rec_owner, rec_slot):
    peers = lax.axis_size("edge")
    shares = lax.axis_size("tx") * lax.axis_size("rcv")
    me = jnp.stack([lax.axis_index("edge"), lax.axis_index(("tx", "rcv"))])
    rows = fields[0]
    edge_count = sigma.shape[0]
    shifts = range(1, peers)

    length = edge_count + 2 * RIM
    width = PAIRS * 2 * BS
    steps = edge_count // width
    marks = [0, 1, 1 + steps // 2, steps]
    lanes = [0] + [m * width + KEEP - RIM for m in marks[1:-1]] + [length]

    rows = pltpu.with_memory_space_constraint(rows, pltpu.HBM)
    mine, blocks = packed(me, rec_edge, rec_weight, rec_owner, rec_slot, rows, peers, lanes, shares)
    parts = []
    for j in range(len(lanes) - 1):
        pieces = [shifted(blocks[j * (peers - 1) + s - 1], s, peers) for s in shifts]
        parts.append((marks[j], marks[j + 1] - marks[j], lanes[j], pieces))
    lists = [mine] + [shifted(mine, s, peers) for s in shifts]
    lists = jnp.concatenate(lists, axis=0)
    lists = [lists] + [
        lax.ppermute(lists, ("tx", "rcv"), [(i, (i + k) % shares) for i in range(shares)])
        for k in range(1, shares)
    ]
    band = banded(kblocks, blk_index, me[:1] * (edge_count // BS))
    own, sent = site_sums(me, rows, lists, peers)
    got = [own] + [shifted(sent[s - 1], s, peers) for s in shifts]
    residual = residual_of(rows, parts, band, sigma, me, peers)
    site_out = placed_rows(me, residual[:16, :LANE], got, peers)
    return residual[None], site_out[None]


def fits(mesh, fields, sigma, rec_edge):
    peers = mesh.shape["edge"]
    cols = fields.shape[1] // peers
    edge_count = sigma.shape[0] // (mesh.shape["grp"] * peers)
    recs = rec_edge.shape[0] // (mesh.shape["grp"] * peers)
    return (
        cols % 16 == 0
        and cols * peers == LANE
        and peers * IW <= LANE
        and edge_count % (PAIRS * 2 * BS) == 0
        and edge_count >= 4 * PAIRS * 2 * BS
        and recs % (LANE * mesh.shape["tx"] * mesh.shape["rcv"]) == 0
        and peers > 1
    )


def solution(mesh):
    placed = (
        P(("grp", "tx", "rcv"), "edge", None),
        P("edge", None),
        P("edge", None),
        P(("grp", "edge")),
        P(("grp", "edge"), None),
        P(("grp", "edge"), None),
        P(("grp", "edge"), None),
        P(("grp", "edge")),
    )

    def run(fields, kblocks, blk_index, sigma, rec_edge, rec_weight, rec_owner, rec_slot):
        body = on_device if fits(mesh, fields, sigma, rec_edge) else plain_device
        return jax.shard_map(
            body,
            mesh=mesh,
            in_specs=placed,
            out_specs=(P(("grp", "tx", "rcv"), None, "edge"), P(("grp", "tx", "rcv"), None, "edge")),
            check_vma=False,
        )(fields, kblocks, blk_index, sigma, rec_edge, rec_weight, rec_owner, rec_slot)

    return run
```

```python
import functools
import math

import jax
import jax.numpy as jnp
from jax import lax
from jax.experimental import pallas as pl
from jax.experimental.pallas import tpu as pltpu
from jax.sharding import PartitionSpec as P


BS = 64
NNZB = 3
HB = 2
IW = 8
SDEV = 1024

LANE = 128
PAIRS = 8
TRIP = 2
RIM = BS * HB
KEEP = 4 * RIM
LINES = 2 * IW + 8
TOP = 32000.0


def padded_2(shard, sides, width):
    for axis, dim in sides:
        peers, length = (lax.axis_size(axis), shard.shape[dim])
        up = [(i, (i + 1) % peers) for i in range(peers - 1)]
        down = [(j, i) for i, j in up]
        last = lax.slice_in_dim(shard, length - width, length, axis=dim)
        initial = lax.slice_in_dim(shard, 0, width, axis=dim)
        before = lax.ppermute(last, axis, up)
        after = lax.ppermute(initial, axis, down)
        shard = jnp.concatenate([before, shard, after], axis=dim)
    return shard


def plain_device(fields, kblocks, blk_index, sigma, rec_edge, rec_weight, rec_owner, rec_slot):
    peers = lax.axis_size("edge")
    edge_count = sigma.shape[0]
    block_count = edge_count // BS
    rec_count = rec_edge.shape[0]
    rim_width = BS * HB
    tx_local = fields.shape[1] // 2
    first_block = lax.axis_index("edge") * block_count
    local_index = blk_index - first_block + HB
    flat_edges = rec_edge.reshape(-1)
    block_vals = kblocks.reshape(block_count, NNZB, BS, BS)
    source = fields.reshape(1, tx_local, 2, fields.shape[2])
    moved = lax.all_to_all(source, "edge", split_axis=3, concat_axis=0, tiled=True)
    item_count = moved.shape[1]
    columns = peers * item_count * 2
    flat_rows = moved.reshape(columns, edge_count)
    padded = padded_2(flat_rows, (("edge", 1),), rim_width)
    blocks = padded.reshape(columns, block_count + 2 * HB, BS)
    picked = jnp.take(blocks, local_index, axis=1)
    stiffness = jnp.einsum("cbkj,bkij->cbi", picked, block_vals, preferred_element_type=jnp.float32)
    stiffness = stiffness.reshape(columns, edge_count)
    paired = flat_rows.reshape(columns // 2, 2, edge_count).astype(jnp.float32)
    diagonal = jnp.stack([-sigma * paired[:, 1], sigma * paired[:, 0]], axis=1).reshape(
        columns, edge_count
    )
    residual = (stiffness + diagonal).astype(jnp.bfloat16).reshape(1, columns, edge_count)
    interp_vals = (
        jnp.take(flat_rows, flat_edges, axis=1).reshape(columns, rec_count, IW).astype(jnp.float32)
    )
    predicted = jnp.sum(interp_vals * rec_weight[None], axis=2)
    site_ids = rec_owner[:, 0] * SDEV + rec_slot
    local_sums = jax.ops.segment_sum(predicted.T, site_ids, num_segments=peers * SDEV)
    site_table = lax.psum_scatter(local_sums.T, "edge", scatter_dimension=1, tiled=True)
    return (residual, site_table.reshape(1, columns, SDEV))


def shifted(x, shift, peers):
    return lax.ppermute(x, "edge", [(i, (i + shift) % peers) for i in range(peers)])


HBM = pl.BlockSpec(memory_space=pltpu.HBM)
VMEM = pl.BlockSpec(memory_space=pltpu.VMEM)
SMEM = pl.BlockSpec(memory_space=pltpu.SMEM)


def pack_kernel(peers, lanes, me_ref, edge_ref, weight_ref, owner_ref, slot_ref, rows_ref, *refs):
    parts = len(lanes) - 1
    count = parts * (peers - 1)
    list_ref, pieces, refs = refs[0], refs[1 : 1 + count], refs[1 + count :]
    edges, weights, owners, slots, list_sems, in_sems, out_sems = refs[:7]
    held = refs[7:]
    recs = list_ref.shape[1]
    share = pl.ds(pl.multiple_of(me_ref[1] * recs, recs), recs)
    small = [
        pltpu.make_async_copy(source.at[:, share], target, list_sems.at[i])
        for i, (source, target) in enumerate(
            [(edge_ref, edges), (weight_ref, weights), (owner_ref, owners), (slot_ref, slots)]
        )
    ]
    for copy in small:
        copy.start()
    taken, put = [], []
    for j in range(parts):
        for s in range(1, peers):
            target = lax.rem(me_ref[0] + s, peers)
            start = start_of(target, peers, rows_ref.shape[1]) + lanes[j]
            n = len(taken)
            taken.append(
                pltpu.make_async_copy(
                    rows_ref.at[:, pl.ds(pl.multiple_of(start, RIM), lanes[j + 1] - lanes[j])],
                    held[n],
                    in_sems.at[n],
                )
            )
            put.append(pltpu.make_async_copy(held[n], pieces[n], out_sems.at[n]))
    for copy in taken:
        copy.start()
    for copy in small:
        copy.wait()
    list_ref[:IW, :] = edges[...].astype(jnp.float32)
    list_ref[IW : 2 * IW, :] = weights[...]
    sites = (owners[...] * SDEV + slots[...]).astype(jnp.float32)
    list_ref[2 * IW :, :] = jnp.broadcast_to(sites, (LINES - 2 * IW, recs))
    for copy, onward in zip(taken, put):
        copy.wait()
        onward.start()
    for copy in put:
        copy.wait()


def start_of(target, peers, all_edges):
    edge_count = all_edges // peers
    return jnp.clip(target * edge_count - RIM, 0, all_edges - edge_count - 2 * RIM)


def packed(me, rec_edge, rec_weight, rec_owner, rec_slot, rows, peers, lanes, shares):
    recs = rec_slot.shape[0]
    share = recs // shares
    cols = rows.shape[0]
    shapes = [
        (cols, high - low) for low, high in zip(lanes, lanes[1:]) for _ in range(1, peers)
    ]
    small = [rec_edge.T, rec_weight.T, rec_owner.T, rec_slot.reshape(1, recs)]
    out = pl.pallas_call(
        functools.partial(pack_kernel, peers, lanes),
        in_specs=[SMEM] + [HBM] * 5,
        out_specs=[VMEM] + [HBM] * len(shapes),
        out_shape=[jax.ShapeDtypeStruct((LINES, share), jnp.float32)]
        + [jax.ShapeDtypeStruct(shape, rows.dtype) for shape in shapes],
        scratch_shapes=[pltpu.VMEM((x.shape[0], share), x.dtype) for x in small]
        + [
            pltpu.SemaphoreType.DMA((len(small),)),
            pltpu.SemaphoreType.DMA((len(shapes),)),
            pltpu.SemaphoreType.DMA((len(shapes),)),
        ]
        + [pltpu.VMEM(shape, rows.dtype) for shape in shapes],
        compiler_params=pltpu.CompilerParams(vmem_limit_bytes=8 << 20),
        cost_estimate=pl.CostEstimate(flops=0, bytes_accessed=8 << 20, transcendentals=0),
        name="packed",
    )(me, *[pltpu.with_memory_space_constraint(x, pltpu.HBM) for x in small], rows)
    return out[0], out[1:]


def site_kernel(peers, shares, me_ref, rows_ref, *refs):
    list_refs, refs = refs[:shares], refs[shares:]
    own_ref, sent_refs, refs = refs[0], refs[1:peers], refs[peers:]
    out_ref, rows, turned, picked, pred, ints, scale, row_sems, int_sems = refs[:9]
    refs = refs[9:]
    edge_refs = [refs[s * (IW + 1) : (s + 1) * (IW + 1)] for s in range(peers)]
    tables = refs[peers * (IW + 1) :]
    cols = rows_ref.shape[0]
    edge_count = turned.shape[0]
    share = list_refs[0].shape[1]
    recs = shares * share
    per = picked.shape[1]
    parts = row_sems.shape[0]
    width = edge_count // parts

    def fetch(part, s):
        start = lax.rem(me_ref[0] + peers - s, peers) * edge_count + part * width
        return pltpu.make_async_copy(
            rows_ref.at[:, pl.ds(pl.multiple_of(start, LANE), width)],
            rows.at[pl.ds(s * cols, cols), pl.ds(part * width, width)],
            row_sems.at[part, s],
        )

    for part in range(parts):
        for s in range(peers):
            fetch(part, s).start()
    lists = []
    for s in range(peers):
        for j, ref in enumerate(list_refs):
            at = slice(j * share, (j + 1) * share)
            edges = ref[s * LINES : s * LINES + IW, :]
            ints[s, :IW, at] = edges.astype(jnp.int32)
            scale[s * IW : (s + 1) * IW, at] = ref[s * LINES + IW : s * LINES + 2 * IW, :]
            sites = ref[s * LINES + 2 * IW : (s + 1) * LINES, :]
            ints[s, IW:, at] = sites.astype(jnp.int32)
        for k in range(IW + 1):
            copy = pltpu.make_async_copy(
                ints.at[s, pl.ds(k, 1)], edge_refs[s][k], int_sems.at[s, k]
            )
            copy.start()
            lists.append(copy)
    scale[peers * IW :, :] = jnp.zeros((LANE - peers * IW, recs), jnp.float32)
    for table in tables:
        table[...] = jnp.zeros_like(table)

    for part in range(parts):
        for s in range(peers):
            fetch(part, s).wait()

        def turn(t, _, part=part):
            at = pl.multiple_of(part * width + t * LANE, LANE)
            turned[pl.ds(at, LANE), :] = rows[:, pl.ds(at, LANE)].T.astype(jnp.float32)
            return 0

        lax.fori_loop(0, width // LANE, turn, 0, unroll=2)
    lane = lax.broadcasted_iota(jnp.int32, (1, LANE), 1) // cols
    lanes = lax.broadcasted_iota(jnp.int32, (per, LANE), 1) // cols
    for copy in lists:
        copy.wait()

    def receivers(g, _):
        first = pl.multiple_of(g * per, per)

        def gather(r, _):
            for k in range(IW):
                row = turned[pl.ds(edge_refs[0][k][0, first + r], 1), :]
                for q in range(1, peers):
                    other = turned[pl.ds(edge_refs[q][k][0, first + r], 1), :]
                    row = jnp.where(lane == q, other, row)
                picked[k, pl.ds(r, 1), :] = row
            return 0

        lax.fori_loop(0, per, gather, 0, unroll=4)
        weights = scale[:, pl.ds(first, per)].T
        total = jnp.zeros((per, LANE), jnp.float32)
        for k in range(IW):
            total += picked[k] * jnp.take_along_axis(weights, lanes * IW + k, axis=1)
        pred[...] = total

        def scatter(r, _):
            row = pred[pl.ds(r, 1), :]
            for q in range(peers):
                at = pl.ds(edge_refs[q][IW][0, first + r], 1)
                tables[q][at, :] = tables[q][at, :] + row
            return 0

        lax.fori_loop(0, per, scatter, 0, unroll=8)
        return 0

    lax.fori_loop(0, recs // per, receivers, 0)
    owned = out_ref.shape[2]
    per_owner = owned // LANE

    def back(t, _):
        at = pl.ds(pl.multiple_of(t * LANE, LANE), LANE)
        tile = tables[0][at, :]
        for q in range(1, peers):
            tile = jnp.where(lane == q, tables[q][at, :], tile)
        tile = tile.T
        total = tile[:cols]
        for q in range(1, peers):
            total += tile[q * cols : (q + 1) * cols]
        out_ref[t // per_owner, :, pl.ds(pl.multiple_of((t % per_owner) * LANE, LANE), LANE)] = total
        return 0

    lax.fori_loop(0, peers * per_owner, back, 0)
    own_ref[...] = out_ref[me_ref[0]]
    for s in range(1, peers):
        block = out_ref[lax.rem(me_ref[0] + s, peers)]
        most = jnp.max(jnp.abs(block), axis=1, keepdims=True)
        power = jnp.floor(jnp.log(jnp.maximum(most, 1e-36)) * (1 / math.log(2.0))) + 1.0
        coded = jnp.round(block * (TOP * jnp.exp2(-power)))
        sent_refs[s - 1][:, :owned] = coded.astype(jnp.int32).astype(jnp.int16)
        power = jnp.broadcast_to(power, (cols, LANE))
        sent_refs[s - 1][:, owned:] = power.astype(jnp.int32).astype(jnp.int16)


def site_sums(me, rows, lists, peers):
    cols, all_edges = rows.shape
    edge_count = all_edges // peers
    per = LANE
    parts = 4
    shares = len(lists)
    recs = lists[0].shape[1] * shares
    sent = jax.ShapeDtypeStruct((cols, SDEV + LANE), jnp.int16)
    out = pl.pallas_call(
        functools.partial(site_kernel, peers, shares),
        in_specs=[SMEM, HBM] + [VMEM] * shares,
        out_specs=[VMEM] * peers,
        out_shape=[jax.ShapeDtypeStruct((cols, SDEV), jnp.float32)] + [sent] * (peers - 1),
        scratch_shapes=[
            pltpu.VMEM((peers, cols, SDEV), jnp.float32),
            pltpu.VMEM((peers * cols, edge_count), rows.dtype),
            pltpu.VMEM((edge_count, LANE), jnp.float32),
            pltpu.VMEM((IW, per, LANE), jnp.float32),
            pltpu.VMEM((per, LANE), jnp.float32),
            pltpu.VMEM((peers, IW + 8, recs), jnp.int32),
            pltpu.VMEM((LANE, recs), jnp.float32),
            pltpu.SemaphoreType.DMA((parts, peers)),
            pltpu.SemaphoreType.DMA((peers, IW + 1)),
        ]
        + [pltpu.SMEM((1, recs), jnp.int32)] * (peers * (IW + 1))
        + [pltpu.VMEM((peers * SDEV, LANE), jnp.float32)] * peers,
        compiler_params=pltpu.CompilerParams(vmem_limit_bytes=24 << 20),
        cost_estimate=pl.CostEstimate(
            flops=2 * recs * peers * IW * 8 * LANE, bytes_accessed=64 << 20, transcendentals=0
        ),
        name="site_sums",
    )(me, rows, *lists)
    return out[0], out[1:]


def place_kernel(peers, me_ref, _, *refs):
    out_ref = refs[peers]
    cols, width = refs[0].shape
    for s in range(peers):
        at = lax.rem(me_ref[0] + peers - s, peers) * cols
        block = refs[s][:, :width].astype(jnp.int32) if s else refs[s][...]
        if s:
            power = refs[s][:, width:].astype(jnp.int32).astype(jnp.float32)
            block = block.astype(jnp.float32) * (jnp.exp2(power[:, :1]) * (1 / TOP))
        out_ref[pl.ds(pl.multiple_of(at, 8), cols), :] = block


def placed_rows(me, after, got, peers):
    cols, width = got[0].shape
    return pl.pallas_call(
        functools.partial(place_kernel, peers),
        in_specs=[SMEM] + [VMEM] * (peers + 1),
        out_specs=VMEM,
        out_shape=jax.ShapeDtypeStruct((peers * cols, width), got[0].dtype),
        compiler_params=pltpu.CompilerParams(vmem_limit_bytes=4 << 20),
        name="placed_rows",
    )(me, after, *got)


def band_kernel(first_ref, index_ref, blocks_ref, band_ref, lines):
    step = pl.program_id(0)
    count = NNZB * BS // 2
    half = lax.broadcasted_iota(jnp.int32, (1, 2 * BS), 1) // BS

    def pairs(trip, _):
        for row in range(2 * TRIP):
            both = blocks_ref[trip * 2 * TRIP + row].astype(jnp.float32)
            crossed = pltpu.roll(both, BS, 1)
            lines[row, pl.ds(0, count, stride=2), :] = jnp.where(half == 0, both, crossed)
            lines[row, pl.ds(1, count, stride=2), :] = jnp.where(half == 0, crossed, both)
        for row in range(2 * TRIP):
            p = step * PAIRS + trip * TRIP + row // 2
            base = 2 * p - HB + first_ref[0]
            offs = [index_ref[k, 2 * p + row % 2] - base for k in range(NNZB)]
            blocks = [
                lines[row, k * BS : (k + 1) * BS].astype(band_ref.dtype) for k in range(NNZB)
            ]
            side = pl.ds(row % 2 * BS, BS)
            for tile in range(band_ref.shape[2] // (2 * BS)):
                masks = [
                    jnp.where(half + 2 * tile == off, 1.0, 0.0).astype(band_ref.dtype) for off in offs
                ]
                total = blocks[0] * masks[0]
                for k in range(1, NNZB):
                    total += blocks[k] * masks[k]
                band_ref[p, side, tile * 2 * BS : (tile + 1) * 2 * BS] = total
        return 0

    lax.fori_loop(0, PAIRS // TRIP, pairs, 0)


def banded(kblocks, blk_index, first_block):
    count = kblocks.shape[0]
    pairs = count // 2
    lines = NNZB * BS // 2
    window = 2 + 2 * HB
    return pl.pallas_call(
        band_kernel,
        grid=(pairs // PAIRS,),
        in_specs=[SMEM, SMEM, pl.BlockSpec((2 * PAIRS, lines, 2 * BS), lambda i: (i, 0, 0))],
        out_specs=VMEM,
        scratch_shapes=[pltpu.VMEM((2 * TRIP, 2 * lines, 2 * BS), jnp.float32)],
        out_shape=jax.ShapeDtypeStruct((pairs, 2 * BS, window * BS), jnp.bfloat16),
        compiler_params=pltpu.CompilerParams(vmem_limit_bytes=24 << 20),
        cost_estimate=pl.CostEstimate(flops=0, bytes_accessed=40 << 20, transcendentals=0),
        name="banded",
    )(
        first_block,
        blk_index.T,
        pltpu.with_memory_space_constraint(kblocks.reshape(count, lines, 2 * BS), pltpu.HBM),
    )


def residual_kernel(peers, first, low, keep, me_ref, *refs):
    pieces = refs[: peers - 1]
    refs = refs[peers - 1 :]
    if keep:
        ends, refs = refs[: peers - 1], refs[peers - 1 :]
    rows_ref, band_ref, sigma_ref = refs[:3]
    out_ref, token_ref, panel, swap, own, own_sem = refs[3 if keep == 0 else 4 :]
    cols, span = own.shape
    columns = panel.shape[0]
    step = pl.program_id(0)
    width = PAIRS * 2 * BS
    me = me_ref[0]

    @pl.when(step == 0)
    def _():
        token_ref[...] = jnp.zeros_like(token_ref)
        at = start_of(me, peers, rows_ref.shape[1]) + (low - keep)
        copy = pltpu.make_async_copy(
            rows_ref.at[:, pl.ds(pl.multiple_of(at, RIM), span)], own, own_sem
        )
        copy.start()
        panel[:, :RIM] = jnp.zeros((columns, RIM), panel.dtype)
        panel[:, RIM + span :] = jnp.zeros((columns, RIM), panel.dtype)
        row = lax.broadcasted_iota(jnp.int32, (columns, columns), 0)
        col = lax.broadcasted_iota(jnp.int32, (columns, columns), 1)
        sign = jnp.where(row % 2 == 0, -1.0, 1.0)
        swap[...] = jnp.where(row + 1 - 2 * (row % 2) == col, sign, 0.0).astype(swap.dtype)
        for s in range(1, peers):
            at = pl.ds(pl.multiple_of(lax.rem(me + peers - s, peers) * cols, cols), cols)
            if keep:
                panel[at, RIM : RIM + keep] = ends[s - 1][:, ends[s - 1].shape[1] - keep :]
            panel[at, RIM + keep : RIM + span] = pieces[s - 1][...]
        copy.wait()
        panel[pl.ds(pl.multiple_of(me * cols, cols), cols), RIM : RIM + span] = own[...]

    moved = jnp.where(me == 0, -RIM, jnp.where(me == peers - 1, RIM, 0))
    start = (step + first) * width + RIM + moved - (low - keep)

    def window(at, size):
        return panel[:, pl.ds(pl.multiple_of(start + at, RIM), size)]

    swapped = jnp.dot(swap[...], window(RIM, width), preferred_element_type=jnp.float32)
    at = pl.multiple_of((step + first) * width, width)
    turned = swapped * sigma_ref[:, pl.ds(at, width)]
    for t in range(PAIRS):
        at = t * 2 * BS
        stiff = lax.dot_general(
            window(at, 2 * (BS + RIM)),
            band_ref[(step + first) * PAIRS + t],
            (((1,), (1,)), ((), ())),
            preferred_element_type=jnp.float32,
        )
        out_ref[:, at : at + 2 * BS] = (stiff + turned[:, at : at + 2 * BS]).astype(out_ref.dtype)


def residual_of(rows, parts, band, sigma, me, peers):
    cols = rows.shape[0]
    edge_count = sigma.shape[0]
    columns = peers * cols
    width = PAIRS * 2 * BS
    sigma = sigma.reshape(1, edge_count)
    out, before = None, None
    for first, steps, low, pieces in parts:
        keep = KEEP if low else 0
        span = keep + pieces[0].shape[1]
        given = list(pieces) + (list(before) if keep else []) + [rows, band, sigma]
        specs = [VMEM] * (len(given) - 3) + [HBM, VMEM, VMEM]
        if out is not None:
            given.append(out)
            specs.append(pl.BlockSpec(memory_space=pl.ANY))
        out, token = pl.pallas_call(
            functools.partial(residual_kernel, peers, first, low, keep),
            grid_spec=pltpu.PrefetchScalarGridSpec(
                num_scalar_prefetch=1,
                grid=(steps,),
                in_specs=specs,
                out_specs=[
                    pl.BlockSpec((columns, width), lambda i, me, first=first: (0, i + first)),
                    pl.BlockSpec((8, LANE), lambda i, me: (0, 0)),
                ],
                scratch_shapes=[
                    pltpu.VMEM((columns, span + 2 * RIM), jnp.bfloat16),
                    pltpu.VMEM((columns, columns), jnp.bfloat16),
                    pltpu.VMEM((cols, span), rows.dtype),
                    pltpu.SemaphoreType.DMA,
                ],
            ),
            out_shape=[
                jax.ShapeDtypeStruct((columns, edge_count), jnp.bfloat16),
                jax.ShapeDtypeStruct((8, LANE), jnp.float32),
            ],
            input_output_aliases={len(given): 0} if out is not None else {},
            compiler_params=pltpu.CompilerParams(vmem_limit_bytes=24 << 20),
            cost_estimate=pl.CostEstimate(
                flops=2 * columns * steps * width * 384,
                bytes_accessed=(21 << 20) * steps * width // edge_count,
                transcendentals=0,
            ),
        )(me, *given)
        before = pieces
    return out, token


def on_device(fields, kblocks, blk_index, sigma, rec_edge, rec_weight, rec_owner, rec_slot):
    return ordered(
        fields, kblocks, blk_index, sigma, rec_edge, rec_weight, rec_owner, rec_slot
    )


def ordered(fields, kblocks, blk_index, sigma, rec_edge, rec_weight, rec_owner, rec_slot):
    peers = lax.axis_size("edge")
    shares = lax.axis_size("tx") * lax.axis_size("rcv")
    me = jnp.stack([lax.axis_index("edge"), lax.axis_index(("tx", "rcv"))])
    rows = fields[0]
    edge_count = sigma.shape[0]
    shifts = range(1, peers)

    length = edge_count + 2 * RIM
    width = PAIRS * 2 * BS
    steps = edge_count // width
    marks = [0, 1, 1 + 5 * steps // 8, steps]
    lanes = [0] + [m * width + KEEP - RIM for m in marks[1:-1]] + [length]

    rows = pltpu.with_memory_space_constraint(rows, pltpu.HBM)
    mine, blocks = packed(me, rec_edge, rec_weight, rec_owner, rec_slot, rows, peers, lanes, shares)
    parts = []
    for j in range(len(lanes) - 1):
        pieces = [shifted(blocks[j * (peers - 1) + s - 1], s, peers) for s in shifts]
        parts.append((marks[j], marks[j + 1] - marks[j], lanes[j], pieces))
    lists = [mine] + [shifted(mine, s, peers) for s in shifts]
    lists = jnp.concatenate(lists, axis=0)
    lists = [lists] + [
        lax.ppermute(lists, ("tx", "rcv"), [(i, (i + k) % shares) for i in range(shares)])
        for k in range(1, shares)
    ]
    band = banded(kblocks, blk_index, me[:1] * (edge_count // BS))
    own, sent = site_sums(me, rows, lists, peers)
    got = [own] + [shifted(sent[s - 1], s, peers) for s in shifts]
    residual, token = residual_of(rows, parts, band, sigma, me, peers)
    site_out = placed_rows(me, token, got, peers)
    return residual[None], site_out[None]


def fits(mesh, fields, sigma, rec_edge):
    peers = mesh.shape["edge"]
    cols = fields.shape[1] // peers
    edge_count = sigma.shape[0] // (mesh.shape["grp"] * peers)
    recs = rec_edge.shape[0] // (mesh.shape["grp"] * peers)
    return (
        cols % 16 == 0
        and cols * peers == LANE
        and peers * IW <= LANE
        and edge_count % (PAIRS * 2 * BS) == 0
        and edge_count >= 4 * PAIRS * 2 * BS
        and recs % (LANE * mesh.shape["tx"] * mesh.shape["rcv"]) == 0
        and peers > 1
    )


def solution(mesh):
    placed = (
        P(("grp", "tx", "rcv"), "edge", None),
        P("edge", None),
        P("edge", None),
        P(("grp", "edge")),
        P(("grp", "edge"), None),
        P(("grp", "edge"), None),
        P(("grp", "edge"), None),
        P(("grp", "edge")),
    )

    def run(fields, kblocks, blk_index, sigma, rec_edge, rec_weight, rec_owner, rec_slot):
        body = on_device if fits(mesh, fields, sigma, rec_edge) else plain_device
        return jax.shard_map(
            body,
            mesh=mesh,
            in_specs=placed,
            out_specs=(P(("grp", "tx", "rcv"), None, "edge"), P(("grp", "tx", "rcv"), None, "edge")),
            check_vma=False,
        )(fields, kblocks, blk_index, sigma, rec_edge, rec_weight, rec_owner, rec_slot)

    return run
```

```python
import functools
import math

import jax
import jax.numpy as jnp
from jax import lax
from jax.experimental import pallas as pl
from jax.experimental.pallas import tpu as pltpu
from jax.sharding import PartitionSpec as P


BS = 64
NNZB = 3
HB = 2
IW = 8
SDEV = 1024

LANE = 128
GROUP = 4
GROUPS = 4
REACH = GROUP * BS + 2 * BS * HB
RIM = BS * HB
KEEP = 4 * RIM
LINES = 2 * IW + 8
TOP = 32000.0


def padded_2(shard, sides, width):
    for axis, dim in sides:
        peers, length = (lax.axis_size(axis), shard.shape[dim])
        up = [(i, (i + 1) % peers) for i in range(peers - 1)]
        down = [(j, i) for i, j in up]
        last = lax.slice_in_dim(shard, length - width, length, axis=dim)
        initial = lax.slice_in_dim(shard, 0, width, axis=dim)
        before = lax.ppermute(last, axis, up)
        after = lax.ppermute(initial, axis, down)
        shard = jnp.concatenate([before, shard, after], axis=dim)
    return shard


def plain_device(fields, kblocks, blk_index, sigma, rec_edge, rec_weight, rec_owner, rec_slot):
    peers = lax.axis_size("edge")
    edge_count = sigma.shape[0]
    block_count = edge_count // BS
    rec_count = rec_edge.shape[0]
    rim_width = BS * HB
    tx_local = fields.shape[1] // 2
    first_block = lax.axis_index("edge") * block_count
    local_index = blk_index - first_block + HB
    flat_edges = rec_edge.reshape(-1)
    block_vals = kblocks.reshape(block_count, NNZB, BS, BS)
    source = fields.reshape(1, tx_local, 2, fields.shape[2])
    moved = lax.all_to_all(source, "edge", split_axis=3, concat_axis=0, tiled=True)
    item_count = moved.shape[1]
    columns = peers * item_count * 2
    flat_rows = moved.reshape(columns, edge_count)
    padded = padded_2(flat_rows, (("edge", 1),), rim_width)
    blocks = padded.reshape(columns, block_count + 2 * HB, BS)
    picked = jnp.take(blocks, local_index, axis=1)
    stiffness = jnp.einsum("cbkj,bkij->cbi", picked, block_vals, preferred_element_type=jnp.float32)
    stiffness = stiffness.reshape(columns, edge_count)
    paired = flat_rows.reshape(columns // 2, 2, edge_count).astype(jnp.float32)
    diagonal = jnp.stack([-sigma * paired[:, 1], sigma * paired[:, 0]], axis=1).reshape(
        columns, edge_count
    )
    residual = (stiffness + diagonal).astype(jnp.bfloat16).reshape(1, columns, edge_count)
    interp_vals = (
        jnp.take(flat_rows, flat_edges, axis=1).reshape(columns, rec_count, IW).astype(jnp.float32)
    )
    predicted = jnp.sum(interp_vals * rec_weight[None], axis=2)
    site_ids = rec_owner[:, 0] * SDEV + rec_slot
    local_sums = jax.ops.segment_sum(predicted.T, site_ids, num_segments=peers * SDEV)
    site_table = lax.psum_scatter(local_sums.T, "edge", scatter_dimension=1, tiled=True)
    return (residual, site_table.reshape(1, columns, SDEV))


def shifted(x, shift, peers):
    return lax.ppermute(x, "edge", [(i, (i + shift) % peers) for i in range(peers)])


HBM = pl.BlockSpec(memory_space=pltpu.HBM)
VMEM = pl.BlockSpec(memory_space=pltpu.VMEM)
SMEM = pl.BlockSpec(memory_space=pltpu.SMEM)


def pack_kernel(peers, lanes, me_ref, edge_ref, weight_ref, owner_ref, slot_ref, rows_ref, *refs):
    parts = len(lanes) - 1
    count = parts * (peers - 1)
    list_ref, pieces, refs = refs[0], refs[1 : 1 + count], refs[1 + count :]
    edges, weights, owners, slots, list_sems, in_sems, out_sems = refs[:7]
    held = refs[7:]
    recs = list_ref.shape[1]
    share = pl.ds(pl.multiple_of(me_ref[1] * recs, recs), recs)
    small = [
        pltpu.make_async_copy(source.at[:, share], target, list_sems.at[i])
        for i, (source, target) in enumerate(
            [(edge_ref, edges), (weight_ref, weights), (owner_ref, owners), (slot_ref, slots)]
        )
    ]
    for copy in small:
        copy.start()
    taken, put = [], []
    for j in range(parts):
        for s in range(1, peers):
            target = lax.rem(me_ref[0] + s, peers)
            start = start_of(target, peers, rows_ref.shape[1]) + lanes[j]
            n = len(taken)
            taken.append(
                pltpu.make_async_copy(
                    rows_ref.at[:, pl.ds(pl.multiple_of(start, RIM), lanes[j + 1] - lanes[j])],
                    held[n],
                    in_sems.at[n],
                )
            )
            put.append(pltpu.make_async_copy(held[n], pieces[n], out_sems.at[n]))
    for copy in taken:
        copy.start()
    for copy in small:
        copy.wait()
    list_ref[:IW, :] = edges[...].astype(jnp.float32)
    list_ref[IW : 2 * IW, :] = weights[...]
    sites = (owners[...] * SDEV + slots[...]).astype(jnp.float32)
    list_ref[2 * IW :, :] = jnp.broadcast_to(sites, (LINES - 2 * IW, recs))
    for copy, onward in zip(taken, put):
        copy.wait()
        onward.start()
    for copy in put:
        copy.wait()


def start_of(target, peers, all_edges):
    edge_count = all_edges // peers
    return jnp.clip(target * edge_count - RIM, 0, all_edges - edge_count - 2 * RIM)


def packed(me, rec_edge, rec_weight, rec_owner, rec_slot, rows, peers, lanes, shares):
    recs = rec_slot.shape[0]
    share = recs // shares
    cols = rows.shape[0]
    shapes = [
        (cols, high - low) for low, high in zip(lanes, lanes[1:]) for _ in range(1, peers)
    ]
    small = [rec_edge.T, rec_weight.T, rec_owner.T, rec_slot.reshape(1, recs)]
    out = pl.pallas_call(
        functools.partial(pack_kernel, peers, lanes),
        in_specs=[SMEM] + [HBM] * 5,
        out_specs=[VMEM] + [HBM] * len(shapes),
        out_shape=[jax.ShapeDtypeStruct((LINES, share), jnp.float32)]
        + [jax.ShapeDtypeStruct(shape, rows.dtype) for shape in shapes],
        scratch_shapes=[pltpu.VMEM((x.shape[0], share), x.dtype) for x in small]
        + [
            pltpu.SemaphoreType.DMA((len(small),)),
            pltpu.SemaphoreType.DMA((len(shapes),)),
            pltpu.SemaphoreType.DMA((len(shapes),)),
        ]
        + [pltpu.VMEM(shape, rows.dtype) for shape in shapes],
        compiler_params=pltpu.CompilerParams(vmem_limit_bytes=8 << 20),
        cost_estimate=pl.CostEstimate(flops=0, bytes_accessed=8 << 20, transcendentals=0),
        name="packed",
    )(me, *[pltpu.with_memory_space_constraint(x, pltpu.HBM) for x in small], rows)
    return out[0], out[1:]


def site_kernel(peers, shares, me_ref, rows_ref, *refs):
    list_refs, refs = refs[:shares], refs[shares:]
    own_ref, sent_refs, refs = refs[0], refs[1:peers], refs[peers:]
    out_ref, rows, turned, picked, pred, ints, scale, row_sems, int_sems = refs[:9]
    refs = refs[9:]
    edge_refs = [refs[s * (IW + 1) : (s + 1) * (IW + 1)] for s in range(peers)]
    tables = refs[peers * (IW + 1) :]
    cols = rows_ref.shape[0]
    edge_count = turned.shape[0]
    share = list_refs[0].shape[1]
    recs = shares * share
    per = picked.shape[1]
    parts = row_sems.shape[0]
    width = edge_count // parts

    def fetch(part, s):
        start = lax.rem(me_ref[0] + peers - s, peers) * edge_count + part * width
        return pltpu.make_async_copy(
            rows_ref.at[:, pl.ds(pl.multiple_of(start, LANE), width)],
            rows.at[pl.ds(s * cols, cols), pl.ds(part * width, width)],
            row_sems.at[part, s],
        )

    for part in range(parts):
        for s in range(peers):
            fetch(part, s).start()
    lists = []
    for s in range(peers):
        for j, ref in enumerate(list_refs):
            at = slice(j * share, (j + 1) * share)
            edges = ref[s * LINES : s * LINES + IW, :]
            ints[s, :IW, at] = edges.astype(jnp.int32)
            scale[s * IW : (s + 1) * IW, at] = ref[s * LINES + IW : s * LINES + 2 * IW, :]
            sites = ref[s * LINES + 2 * IW : (s + 1) * LINES, :]
            ints[s, IW:, at] = sites.astype(jnp.int32)
        for k in range(IW + 1):
            copy = pltpu.make_async_copy(
                ints.at[s, pl.ds(k, 1)], edge_refs[s][k], int_sems.at[s, k]
            )
            copy.start()
            lists.append(copy)
    scale[peers * IW :, :] = jnp.zeros((LANE - peers * IW, recs), jnp.float32)
    for table in tables:
        table[...] = jnp.zeros_like(table)

    for part in range(parts):
        for s in range(peers):
            fetch(part, s).wait()

        def turn(t, _, part=part):
            at = pl.multiple_of(part * width + t * LANE, LANE)
            turned[pl.ds(at, LANE), :] = rows[:, pl.ds(at, LANE)].T.astype(jnp.float32)
            return 0

        lax.fori_loop(0, width // LANE, turn, 0, unroll=2)
    lane = lax.broadcasted_iota(jnp.int32, (1, LANE), 1) // cols
    lanes = lax.broadcasted_iota(jnp.int32, (per, LANE), 1) // cols
    for copy in lists:
        copy.wait()

    def receivers(g, _):
        first = pl.multiple_of(g * per, per)

        def gather(r, _):
            for k in range(IW):
                row = turned[pl.ds(edge_refs[0][k][0, first + r], 1), :]
                for q in range(1, peers):
                    other = turned[pl.ds(edge_refs[q][k][0, first + r], 1), :]
                    row = jnp.where(lane == q, other, row)
                picked[k, pl.ds(r, 1), :] = row
            return 0

        lax.fori_loop(0, per, gather, 0, unroll=4)
        weights = scale[:, pl.ds(first, per)].T
        total = jnp.zeros((per, LANE), jnp.float32)
        for k in range(IW):
            total += picked[k] * jnp.take_along_axis(weights, lanes * IW + k, axis=1)
        pred[...] = total

        def scatter(r, _):
            row = pred[pl.ds(r, 1), :]
            for q in range(peers):
                at = pl.ds(edge_refs[q][IW][0, first + r], 1)
                tables[q][at, :] = tables[q][at, :] + row
            return 0

        lax.fori_loop(0, per, scatter, 0, unroll=8)
        return 0

    lax.fori_loop(0, recs // per, receivers, 0)
    owned = out_ref.shape[2]
    per_owner = owned // LANE

    def back(t, _):
        at = pl.ds(pl.multiple_of(t * LANE, LANE), LANE)
        tile = tables[0][at, :]
        for q in range(1, peers):
            tile = jnp.where(lane == q, tables[q][at, :], tile)
        tile = tile.T
        total = tile[:cols]
        for q in range(1, peers):
            total += tile[q * cols : (q + 1) * cols]
        out_ref[t // per_owner, :, pl.ds(pl.multiple_of((t % per_owner) * LANE, LANE), LANE)] = total
        return 0

    lax.fori_loop(0, peers * per_owner, back, 0)
    own_ref[...] = out_ref[me_ref[0]]
    for s in range(1, peers):
        block = out_ref[lax.rem(me_ref[0] + s, peers)]
        most = jnp.max(jnp.abs(block), axis=1, keepdims=True)
        power = jnp.floor(jnp.log(jnp.maximum(most, 1e-36)) * (1 / math.log(2.0))) + 1.0
        coded = jnp.round(block * (TOP * jnp.exp2(-power)))
        sent_refs[s - 1][:, :owned] = coded.astype(jnp.int32).astype(jnp.int16)
        power = jnp.broadcast_to(power, (cols, LANE))
        sent_refs[s - 1][:, owned:] = power.astype(jnp.int32).astype(jnp.int16)


def site_sums(me, rows, lists, peers):
    cols, all_edges = rows.shape
    edge_count = all_edges // peers
    per = LANE
    parts = 4
    shares = len(lists)
    recs = lists[0].shape[1] * shares
    sent = jax.ShapeDtypeStruct((cols, SDEV + LANE), jnp.int16)
    out = pl.pallas_call(
        functools.partial(site_kernel, peers, shares),
        in_specs=[SMEM, HBM] + [VMEM] * shares,
        out_specs=[VMEM] * peers,
        out_shape=[jax.ShapeDtypeStruct((cols, SDEV), jnp.float32)] + [sent] * (peers - 1),
        scratch_shapes=[
            pltpu.VMEM((peers, cols, SDEV), jnp.float32),
            pltpu.VMEM((peers * cols, edge_count), rows.dtype),
            pltpu.VMEM((edge_count, LANE), jnp.float32),
            pltpu.VMEM((IW, per, LANE), jnp.float32),
            pltpu.VMEM((per, LANE), jnp.float32),
            pltpu.VMEM((peers, IW + 8, recs), jnp.int32),
            pltpu.VMEM((LANE, recs), jnp.float32),
            pltpu.SemaphoreType.DMA((parts, peers)),
            pltpu.SemaphoreType.DMA((peers, IW + 1)),
        ]
        + [pltpu.SMEM((1, recs), jnp.int32)] * (peers * (IW + 1))
        + [pltpu.VMEM((peers * SDEV, LANE), jnp.float32)] * peers,
        compiler_params=pltpu.CompilerParams(vmem_limit_bytes=24 << 20),
        cost_estimate=pl.CostEstimate(
            flops=2 * recs * peers * IW * 8 * LANE, bytes_accessed=64 << 20, transcendentals=0
        ),
        name="site_sums",
    )(me, rows, *lists)
    return out[0], out[1:]


def place_kernel(peers, me_ref, _, *refs):
    out_ref = refs[peers]
    cols, width = refs[0].shape
    for s in range(peers):
        at = lax.rem(me_ref[0] + peers - s, peers) * cols
        block = refs[s][:, :width].astype(jnp.int32) if s else refs[s][...]
        if s:
            power = refs[s][:, width:].astype(jnp.int32).astype(jnp.float32)
            block = block.astype(jnp.float32) * (jnp.exp2(power[:, :1]) * (1 / TOP))
        out_ref[pl.ds(pl.multiple_of(at, 8), cols), :] = block


def placed_rows(me, after, got, peers):
    cols, width = got[0].shape
    return pl.pallas_call(
        functools.partial(place_kernel, peers),
        in_specs=[SMEM] + [VMEM] * (peers + 1),
        out_specs=VMEM,
        out_shape=jax.ShapeDtypeStruct((peers * cols, width), got[0].dtype),
        compiler_params=pltpu.CompilerParams(vmem_limit_bytes=4 << 20),
        name="placed_rows",
    )(me, after, *got)


def band_kernel(first_ref, index_ref, blocks_ref, band_ref, lines):
    step = pl.program_id(0)
    count = NNZB * BS // 2
    half = lax.broadcasted_iota(jnp.int32, (1, 2 * BS), 1) // BS

    def group(trip, _):
        p = step * GROUPS + trip
        base = GROUP * p - HB + first_ref[0]
        for row in range(GROUP):
            both = blocks_ref[trip * GROUP + row].astype(jnp.float32)
            crossed = pltpu.roll(both, BS, 1)
            lines[row, pl.ds(0, count, stride=2), :] = jnp.where(half == 0, both, crossed)
            lines[row, pl.ds(1, count, stride=2), :] = jnp.where(half == 0, crossed, both)
        for row in range(GROUP):
            offs = [index_ref[k, GROUP * p + row] - base for k in range(NNZB)]
            blocks = [
                lines[row, k * BS : (k + 1) * BS].astype(band_ref.dtype) for k in range(NNZB)
            ]
            for tile in range(REACH // (2 * BS)):
                at = slice(tile * 2 * BS, (tile + 1) * 2 * BS)
                if row // 2 <= tile <= (row + 2 * HB) // 2:
                    masks = [
                        jnp.where(half + 2 * tile == off, 1.0, 0.0).astype(band_ref.dtype)
                        for off in offs
                    ]
                    total = blocks[0] * masks[0]
                    for k in range(1, NNZB):
                        total += blocks[k] * masks[k]
                else:
                    total = jnp.zeros((BS, 2 * BS), band_ref.dtype)
                band_ref[p, row * BS : (row + 1) * BS, at] = total
        return 0

    lax.fori_loop(0, GROUPS, group, 0)


def banded(kblocks, blk_index, first_block):
    count = kblocks.shape[0]
    groups = count // GROUP
    lines = NNZB * BS // 2
    blocks = pl.BlockSpec((GROUPS * GROUP, lines, 2 * BS), lambda i: (i, 0, 0))
    return pl.pallas_call(
        band_kernel,
        grid=(groups // GROUPS,),
        in_specs=[SMEM, SMEM, blocks],
        out_specs=VMEM,
        scratch_shapes=[pltpu.VMEM((GROUP, 2 * lines, 2 * BS), jnp.float32)],
        out_shape=jax.ShapeDtypeStruct((groups, GROUP * BS, REACH), jnp.bfloat16),
        compiler_params=pltpu.CompilerParams(vmem_limit_bytes=28 << 20),
        cost_estimate=pl.CostEstimate(flops=0, bytes_accessed=40 << 20, transcendentals=0),
        name="banded",
    )(
        first_block,
        blk_index.T,
        pltpu.with_memory_space_constraint(kblocks.reshape(count, lines, 2 * BS), pltpu.HBM),
    )


def residual_kernel(peers, first, low, keep, me_ref, *refs):
    pieces = refs[: peers - 1]
    refs = refs[peers - 1 :]
    if keep:
        ends, refs = refs[: peers - 1], refs[peers - 1 :]
    rows_ref, band_ref, sigma_ref = refs[:3]
    out_ref, token_ref, panel, swap, own, own_sem = refs[3 if keep == 0 else 4 :]
    cols, span = own.shape
    columns = panel.shape[0]
    step = pl.program_id(0)
    width = GROUPS * GROUP * BS
    me = me_ref[0]

    @pl.when(step == 0)
    def _():
        token_ref[...] = jnp.zeros_like(token_ref)
        at = start_of(me, peers, rows_ref.shape[1]) + (low - keep)
        copy = pltpu.make_async_copy(
            rows_ref.at[:, pl.ds(pl.multiple_of(at, RIM), span)], own, own_sem
        )
        copy.start()
        panel[:, :RIM] = jnp.zeros((columns, RIM), panel.dtype)
        panel[:, RIM + span :] = jnp.zeros((columns, RIM), panel.dtype)
        row = lax.broadcasted_iota(jnp.int32, (columns, columns), 0)
        col = lax.broadcasted_iota(jnp.int32, (columns, columns), 1)
        sign = jnp.where(row % 2 == 0, -1.0, 1.0)
        swap[...] = jnp.where(row + 1 - 2 * (row % 2) == col, sign, 0.0).astype(swap.dtype)
        for s in range(1, peers):
            at = pl.ds(pl.multiple_of(lax.rem(me + peers - s, peers) * cols, cols), cols)
            if keep:
                panel[at, RIM : RIM + keep] = ends[s - 1][:, ends[s - 1].shape[1] - keep :]
            panel[at, RIM + keep : RIM + span] = pieces[s - 1][...]
        copy.wait()
        panel[pl.ds(pl.multiple_of(me * cols, cols), cols), RIM : RIM + span] = own[...]

    moved = jnp.where(me == 0, -RIM, jnp.where(me == peers - 1, RIM, 0))
    start = (step + first) * width + RIM + moved - (low - keep)

    def window(at, size):
        return panel[:, pl.ds(pl.multiple_of(start + at, RIM), size)]

    swapped = jnp.dot(swap[...], window(RIM, width), preferred_element_type=jnp.float32)
    at = pl.multiple_of((step + first) * width, width)
    turned = swapped * sigma_ref[:, pl.ds(at, width)]
    for t in range(GROUPS):
        at = slice(t * GROUP * BS, (t + 1) * GROUP * BS)
        stiff = lax.dot_general(
            window(t * GROUP * BS, REACH),
            band_ref[(step + first) * GROUPS + t],
            (((1,), (1,)), ((), ())),
            preferred_element_type=jnp.float32,
        )
        out_ref[:, at] = (stiff + turned[:, at]).astype(out_ref.dtype)


def residual_of(rows, parts, band, sigma, me, peers):
    cols = rows.shape[0]
    edge_count = sigma.shape[0]
    columns = peers * cols
    width = GROUPS * GROUP * BS
    sigma = sigma.reshape(1, edge_count)
    out, before = None, None
    for first, steps, low, pieces in parts:
        keep = KEEP if low else 0
        span = keep + pieces[0].shape[1]
        given = list(pieces) + (list(before) if keep else []) + [rows, band, sigma]
        specs = [VMEM] * (len(given) - 3) + [HBM, VMEM, VMEM]
        if out is not None:
            given.append(out)
            specs.append(pl.BlockSpec(memory_space=pl.ANY))
        out, token = pl.pallas_call(
            functools.partial(residual_kernel, peers, first, low, keep),
            grid_spec=pltpu.PrefetchScalarGridSpec(
                num_scalar_prefetch=1,
                grid=(steps,),
                in_specs=specs,
                out_specs=[
                    pl.BlockSpec((columns, width), lambda i, me, first=first: (0, i + first)),
                    pl.BlockSpec((8, LANE), lambda i, me: (0, 0)),
                ],
                scratch_shapes=[
                    pltpu.VMEM((columns, span + 2 * RIM), jnp.bfloat16),
                    pltpu.VMEM((columns, columns), jnp.bfloat16),
                    pltpu.VMEM((cols, span), rows.dtype),
                    pltpu.SemaphoreType.DMA,
                ],
            ),
            out_shape=[
                jax.ShapeDtypeStruct((columns, edge_count), jnp.bfloat16),
                jax.ShapeDtypeStruct((8, LANE), jnp.float32),
            ],
            input_output_aliases={len(given): 0} if out is not None else {},
            compiler_params=pltpu.CompilerParams(vmem_limit_bytes=24 << 20),
            cost_estimate=pl.CostEstimate(
                flops=2 * columns * steps * width * 384,
                bytes_accessed=(21 << 20) * steps * width // edge_count,
                transcendentals=0,
            ),
        )(me, *given)
        before = pieces
    return out, token


def on_device(fields, kblocks, blk_index, sigma, rec_edge, rec_weight, rec_owner, rec_slot):
    return ordered(
        fields, kblocks, blk_index, sigma, rec_edge, rec_weight, rec_owner, rec_slot
    )


def ordered(fields, kblocks, blk_index, sigma, rec_edge, rec_weight, rec_owner, rec_slot):
    peers = lax.axis_size("edge")
    shares = lax.axis_size("tx") * lax.axis_size("rcv")
    me = jnp.stack([lax.axis_index("edge"), lax.axis_index(("tx", "rcv"))])
    rows = fields[0]
    edge_count = sigma.shape[0]
    shifts = range(1, peers)

    length = edge_count + 2 * RIM
    width = GROUPS * GROUP * BS
    steps = edge_count // width
    marks = [0, 1, steps - 2, steps]
    lanes = [0] + [m * width + KEEP - RIM for m in marks[1:-1]] + [length]

    rows = pltpu.with_memory_space_constraint(rows, pltpu.HBM)
    mine, blocks = packed(me, rec_edge, rec_weight, rec_owner, rec_slot, rows, peers, lanes, shares)
    parts = []
    for j in range(len(lanes) - 1):
        pieces = [shifted(blocks[j * (peers - 1) + s - 1], s, peers) for s in shifts]
        parts.append((marks[j], marks[j + 1] - marks[j], lanes[j], pieces))
    lists = [mine] + [shifted(mine, s, peers) for s in shifts]
    lists = jnp.concatenate(lists, axis=0)
    lists = [lists] + [
        lax.ppermute(lists, ("tx", "rcv"), [(i, (i + k) % shares) for i in range(shares)])
        for k in range(1, shares)
    ]
    band = banded(kblocks, blk_index, me[:1] * (edge_count // BS))
    own, sent = site_sums(me, rows, lists, peers)
    got = [own] + [shifted(sent[s - 1], s, peers) for s in shifts]
    residual, token = residual_of(rows, parts, band, sigma, me, peers)
    site_out = placed_rows(me, token, got, peers)
    return residual[None], site_out[None]


def fits(mesh, fields, sigma, rec_edge):
    peers = mesh.shape["edge"]
    cols = fields.shape[1] // peers
    edge_count = sigma.shape[0] // (mesh.shape["grp"] * peers)
    recs = rec_edge.shape[0] // (mesh.shape["grp"] * peers)
    return (
        cols % 16 == 0
        and cols * peers == LANE
        and peers * IW <= LANE
        and edge_count % (GROUPS * GROUP * BS) == 0
        and edge_count >= 8 * GROUPS * GROUP * BS
        and recs % (LANE * mesh.shape["tx"] * mesh.shape["rcv"]) == 0
        and peers > 1
    )


def solution(mesh):
    placed = (
        P(("grp", "tx", "rcv"), "edge", None),
        P("edge", None),
        P("edge", None),
        P(("grp", "edge")),
        P(("grp", "edge"), None),
        P(("grp", "edge"), None),
        P(("grp", "edge"), None),
        P(("grp", "edge")),
    )

    def run(fields, kblocks, blk_index, sigma, rec_edge, rec_weight, rec_owner, rec_slot):
        body = on_device if fits(mesh, fields, sigma, rec_edge) else plain_device
        return jax.shard_map(
            body,
            mesh=mesh,
            in_specs=placed,
            out_specs=(P(("grp", "tx", "rcv"), None, "edge"), P(("grp", "tx", "rcv"), None, "edge")),
            check_vma=False,
        )(fields, kblocks, blk_index, sigma, rec_edge, rec_weight, rec_owner, rec_slot)

    return run
```

```python
import functools
import math

import jax
import jax.numpy as jnp
from jax import lax
from jax.experimental import pallas as pl
from jax.experimental.pallas import tpu as pltpu
from jax.sharding import PartitionSpec as P


BS = 64
NNZB = 3
HB = 2
IW = 8
SDEV = 1024

LANE = 128
GROUP = 4
GROUPS = 4
REACH = GROUP * BS + 2 * BS * HB
RIM = BS * HB
KEEP = 4 * RIM
LINES = 2 * IW + 8
TOP = 32000.0


def padded_2(shard, sides, width):
    for axis, dim in sides:
        peers, length = (lax.axis_size(axis), shard.shape[dim])
        up = [(i, (i + 1) % peers) for i in range(peers - 1)]
        down = [(j, i) for i, j in up]
        last = lax.slice_in_dim(shard, length - width, length, axis=dim)
        initial = lax.slice_in_dim(shard, 0, width, axis=dim)
        before = lax.ppermute(last, axis, up)
        after = lax.ppermute(initial, axis, down)
        shard = jnp.concatenate([before, shard, after], axis=dim)
    return shard


def plain_device(fields, kblocks, blk_index, sigma, rec_edge, rec_weight, rec_owner, rec_slot):
    peers = lax.axis_size("edge")
    edge_count = sigma.shape[0]
    block_count = edge_count // BS
    rec_count = rec_edge.shape[0]
    rim_width = BS * HB
    tx_local = fields.shape[1] // 2
    first_block = lax.axis_index("edge") * block_count
    local_index = blk_index - first_block + HB
    flat_edges = rec_edge.reshape(-1)
    block_vals = kblocks.reshape(block_count, NNZB, BS, BS)
    source = fields.reshape(1, tx_local, 2, fields.shape[2])
    moved = lax.all_to_all(source, "edge", split_axis=3, concat_axis=0, tiled=True)
    item_count = moved.shape[1]
    columns = peers * item_count * 2
    flat_rows = moved.reshape(columns, edge_count)
    padded = padded_2(flat_rows, (("edge", 1),), rim_width)
    blocks = padded.reshape(columns, block_count + 2 * HB, BS)
    picked = jnp.take(blocks, local_index, axis=1)
    stiffness = jnp.einsum("cbkj,bkij->cbi", picked, block_vals, preferred_element_type=jnp.float32)
    stiffness = stiffness.reshape(columns, edge_count)
    paired = flat_rows.reshape(columns // 2, 2, edge_count).astype(jnp.float32)
    diagonal = jnp.stack([-sigma * paired[:, 1], sigma * paired[:, 0]], axis=1).reshape(
        columns, edge_count
    )
    residual = (stiffness + diagonal).astype(jnp.bfloat16).reshape(1, columns, edge_count)
    interp_vals = (
        jnp.take(flat_rows, flat_edges, axis=1).reshape(columns, rec_count, IW).astype(jnp.float32)
    )
    predicted = jnp.sum(interp_vals * rec_weight[None], axis=2)
    site_ids = rec_owner[:, 0] * SDEV + rec_slot
    local_sums = jax.ops.segment_sum(predicted.T, site_ids, num_segments=peers * SDEV)
    site_table = lax.psum_scatter(local_sums.T, "edge", scatter_dimension=1, tiled=True)
    return (residual, site_table.reshape(1, columns, SDEV))


def shifted(x, shift, peers):
    return lax.ppermute(x, "edge", [(i, (i + shift) % peers) for i in range(peers)])


HBM = pl.BlockSpec(memory_space=pltpu.HBM)
VMEM = pl.BlockSpec(memory_space=pltpu.VMEM)
SMEM = pl.BlockSpec(memory_space=pltpu.SMEM)


def pack_kernel(peers, lanes, me_ref, edge_ref, weight_ref, owner_ref, slot_ref, rows_ref, *refs):
    parts = len(lanes) - 1
    count = parts * (peers - 1)
    list_ref, pieces, refs = refs[0], refs[1 : 1 + count], refs[1 + count :]
    edges, weights, owners, slots, list_sems, sems = refs
    recs = list_ref.shape[1]
    share = pl.ds(pl.multiple_of(me_ref[1] * recs, recs), recs)
    small = [
        pltpu.make_async_copy(source.at[:, share], target, list_sems.at[i])
        for i, (source, target) in enumerate(
            [(edge_ref, edges), (weight_ref, weights), (owner_ref, owners), (slot_ref, slots)]
        )
    ]
    for copy in small:
        copy.start()
    taken = []
    for j in range(parts):
        for s in range(1, peers):
            target = lax.rem(me_ref[0] + s, peers)
            start = start_of(target, peers, rows_ref.shape[1]) + lanes[j]
            n = len(taken)
            taken.append(
                pltpu.make_async_copy(
                    rows_ref.at[:, pl.ds(pl.multiple_of(start, RIM), lanes[j + 1] - lanes[j])],
                    pieces[n],
                    sems.at[n],
                )
            )
    for copy in taken:
        copy.start()
    for copy in small:
        copy.wait()
    list_ref[:IW, :] = edges[...].astype(jnp.float32)
    list_ref[IW : 2 * IW, :] = weights[...]
    sites = (owners[...] * SDEV + slots[...]).astype(jnp.float32)
    list_ref[2 * IW :, :] = jnp.broadcast_to(sites, (LINES - 2 * IW, recs))
    for copy in taken:
        copy.wait()


def start_of(target, peers, all_edges):
    edge_count = all_edges // peers
    return jnp.clip(target * edge_count - RIM, 0, all_edges - edge_count - 2 * RIM)


def packed(me, rec_edge, rec_weight, rec_owner, rec_slot, rows, peers, lanes, shares):
    recs = rec_slot.shape[0]
    share = recs // shares
    cols = rows.shape[0]
    shapes = [
        (cols, high - low) for low, high in zip(lanes, lanes[1:]) for _ in range(1, peers)
    ]
    small = [rec_edge.T, rec_weight.T, rec_owner.T, rec_slot.reshape(1, recs)]
    out = pl.pallas_call(
        functools.partial(pack_kernel, peers, lanes),
        in_specs=[SMEM] + [HBM] * 5,
        out_specs=[VMEM] * (1 + len(shapes)),
        out_shape=[jax.ShapeDtypeStruct((LINES, share), jnp.float32)]
        + [jax.ShapeDtypeStruct(shape, rows.dtype) for shape in shapes],
        scratch_shapes=[pltpu.VMEM((x.shape[0], share), x.dtype) for x in small]
        + [
            pltpu.SemaphoreType.DMA((len(small),)),
            pltpu.SemaphoreType.DMA((len(shapes),)),
        ],
        compiler_params=pltpu.CompilerParams(vmem_limit_bytes=8 << 20),
        cost_estimate=pl.CostEstimate(flops=0, bytes_accessed=8 << 20, transcendentals=0),
        name="packed",
    )(me, *[pltpu.with_memory_space_constraint(x, pltpu.HBM) for x in small], rows)
    return out[0], out[1:]


def turn_kernel(peers, me_ref, rows_ref, turned, rows, row_sems):
    cols = rows_ref.shape[0]
    edge_count = turned.shape[0]
    parts = row_sems.shape[0]
    width = edge_count // parts

    def fetch(part, s):
        start = lax.rem(me_ref[0] + peers - s, peers) * edge_count + part * width
        return pltpu.make_async_copy(
            rows_ref.at[:, pl.ds(pl.multiple_of(start, LANE), width)],
            rows.at[pl.ds(s * cols, cols), pl.ds(part * width, width)],
            row_sems.at[part, s],
        )

    for part in range(parts):
        for s in range(peers):
            fetch(part, s).start()
    for part in range(parts):
        for s in range(peers):
            fetch(part, s).wait()

        def turn(t, _, part=part):
            at = pl.multiple_of(part * width + t * LANE, LANE)
            turned[pl.ds(at, LANE), :] = rows[:, pl.ds(at, LANE)].T.astype(jnp.float32)
            return 0

        lax.fori_loop(0, width // LANE, turn, 0, unroll=2)


def turned_rows(me, rows, peers):
    cols, all_edges = rows.shape
    edge_count = all_edges // peers
    parts = 4
    return pl.pallas_call(
        functools.partial(turn_kernel, peers),
        in_specs=[SMEM, HBM],
        out_specs=VMEM,
        out_shape=jax.ShapeDtypeStruct((edge_count, LANE), jnp.float32),
        scratch_shapes=[
            pltpu.VMEM((peers * cols, edge_count), rows.dtype),
            pltpu.SemaphoreType.DMA((parts, peers)),
        ],
        compiler_params=pltpu.CompilerParams(vmem_limit_bytes=14 << 20),
        cost_estimate=pl.CostEstimate(flops=0, bytes_accessed=12 << 20, transcendentals=0),
        name="turned_rows",
    )(me, rows)


def site_kernel(peers, shares, me_ref, turned, *refs):
    list_refs, refs = refs[:shares], refs[shares:]
    own_ref, sent_refs, refs = refs[0], refs[1:peers], refs[peers:]
    out_ref, picked, pred, ints, scale, int_sems = refs[:6]
    refs = refs[6:]
    edge_refs = [refs[s * (IW + 1) : (s + 1) * (IW + 1)] for s in range(peers)]
    tables = refs[peers * (IW + 1) :]
    cols = own_ref.shape[0]
    share = list_refs[0].shape[1]
    recs = shares * share
    per = picked.shape[1]

    lists = []
    for s in range(peers):
        for j, ref in enumerate(list_refs):
            at = slice(j * share, (j + 1) * share)
            edges = ref[s * LINES : s * LINES + IW, :]
            ints[s, :IW, at] = edges.astype(jnp.int32)
            scale[s * IW : (s + 1) * IW, at] = ref[s * LINES + IW : s * LINES + 2 * IW, :]
            sites = ref[s * LINES + 2 * IW : (s + 1) * LINES, :]
            ints[s, IW:, at] = sites.astype(jnp.int32)
        for k in range(IW + 1):
            copy = pltpu.make_async_copy(
                ints.at[s, pl.ds(k, 1)], edge_refs[s][k], int_sems.at[s, k]
            )
            copy.start()
            lists.append(copy)
    scale[peers * IW :, :] = jnp.zeros((LANE - peers * IW, recs), jnp.float32)
    for table in tables:
        table[...] = jnp.zeros_like(table)

    lane = lax.broadcasted_iota(jnp.int32, (1, LANE), 1) // cols
    lanes = lax.broadcasted_iota(jnp.int32, (per, LANE), 1) // cols
    for copy in lists:
        copy.wait()

    def receivers(g, _):
        first = pl.multiple_of(g * per, per)

        def gather(r, _):
            for k in range(IW):
                row = turned[pl.ds(edge_refs[0][k][0, first + r], 1), :]
                for q in range(1, peers):
                    other = turned[pl.ds(edge_refs[q][k][0, first + r], 1), :]
                    row = jnp.where(lane == q, other, row)
                picked[k, pl.ds(r, 1), :] = row
            return 0

        lax.fori_loop(0, per, gather, 0, unroll=4)
        weights = scale[:, pl.ds(first, per)].T
        total = jnp.zeros((per, LANE), jnp.float32)
        for k in range(IW):
            total += picked[k] * jnp.take_along_axis(weights, lanes * IW + k, axis=1)
        pred[...] = total

        def scatter(r, _):
            row = pred[pl.ds(r, 1), :]
            for q in range(peers):
                at = pl.ds(edge_refs[q][IW][0, first + r], 1)
                tables[q][at, :] = tables[q][at, :] + row
            return 0

        lax.fori_loop(0, per, scatter, 0, unroll=8)
        return 0

    lax.fori_loop(0, recs // per, receivers, 0)
    owned = out_ref.shape[2]
    per_owner = owned // LANE

    def back(t, _):
        at = pl.ds(pl.multiple_of(t * LANE, LANE), LANE)
        tile = tables[0][at, :]
        for q in range(1, peers):
            tile = jnp.where(lane == q, tables[q][at, :], tile)
        tile = tile.T
        total = tile[:cols]
        for q in range(1, peers):
            total += tile[q * cols : (q + 1) * cols]
        out_ref[t // per_owner, :, pl.ds(pl.multiple_of((t % per_owner) * LANE, LANE), LANE)] = total
        return 0

    lax.fori_loop(0, peers * per_owner, back, 0)
    own_ref[...] = out_ref[me_ref[0]]
    for s in range(1, peers):
        block = out_ref[lax.rem(me_ref[0] + s, peers)]
        most = jnp.max(jnp.abs(block), axis=1, keepdims=True)
        power = jnp.floor(jnp.log(jnp.maximum(most, 1e-36)) * (1 / math.log(2.0))) + 1.0
        coded = jnp.round(block * (TOP * jnp.exp2(-power)))
        sent_refs[s - 1][:, :owned] = coded.astype(jnp.int32).astype(jnp.int16)
        power = jnp.broadcast_to(power, (cols, LANE))
        sent_refs[s - 1][:, owned:] = power.astype(jnp.int32).astype(jnp.int16)


def site_sums(me, turned, cols, lists, peers):
    per = LANE
    shares = len(lists)
    recs = lists[0].shape[1] * shares
    sent = jax.ShapeDtypeStruct((cols, SDEV + LANE), jnp.int16)
    out = pl.pallas_call(
        functools.partial(site_kernel, peers, shares),
        in_specs=[SMEM] + [VMEM] * (1 + shares),
        out_specs=[VMEM] * peers,
        out_shape=[jax.ShapeDtypeStruct((cols, SDEV), jnp.float32)] + [sent] * (peers - 1),
        scratch_shapes=[
            pltpu.VMEM((peers, cols, SDEV), jnp.float32),
            pltpu.VMEM((IW, per, LANE), jnp.float32),
            pltpu.VMEM((per, LANE), jnp.float32),
            pltpu.VMEM((peers, IW + 8, recs), jnp.int32),
            pltpu.VMEM((LANE, recs), jnp.float32),
            pltpu.SemaphoreType.DMA((peers, IW + 1)),
        ]
        + [pltpu.SMEM((1, recs), jnp.int32)] * (peers * (IW + 1))
        + [pltpu.VMEM((peers * SDEV, LANE), jnp.float32)] * peers,
        compiler_params=pltpu.CompilerParams(vmem_limit_bytes=16 << 20),
        cost_estimate=pl.CostEstimate(
            flops=2 * recs * peers * IW * 8 * LANE, bytes_accessed=64 << 20, transcendentals=0
        ),
        name="site_sums",
    )(me, turned, *lists)
    return out[0], out[1:]


def place_kernel(peers, me_ref, _, *refs):
    out_ref = refs[peers]
    cols, width = refs[0].shape
    for s in range(peers):
        at = lax.rem(me_ref[0] + peers - s, peers) * cols
        block = refs[s][:, :width].astype(jnp.int32) if s else refs[s][...]
        if s:
            power = refs[s][:, width:].astype(jnp.int32).astype(jnp.float32)
            block = block.astype(jnp.float32) * (jnp.exp2(power[:, :1]) * (1 / TOP))
        out_ref[pl.ds(pl.multiple_of(at, 8), cols), :] = block


def placed_rows(me, after, got, peers):
    cols, width = got[0].shape
    return pl.pallas_call(
        functools.partial(place_kernel, peers),
        in_specs=[SMEM] + [VMEM] * (peers + 1),
        out_specs=VMEM,
        out_shape=jax.ShapeDtypeStruct((peers * cols, width), got[0].dtype),
        compiler_params=pltpu.CompilerParams(vmem_limit_bytes=4 << 20),
        name="placed_rows",
    )(me, after, *got)


def band_kernel(first_ref, index_ref, values_ref, band_ref, pick, lines):
    step = pl.program_id(0)
    rows = values_ref.shape[0]
    deep = rows * rows
    half = lax.broadcasted_iota(jnp.int32, (1, 2 * BS), 1) // BS

    @pl.when(step == 0)
    def _():
        line = lax.broadcasted_iota(jnp.int32, pick.shape, 0)
        wanted = (line % (2 * rows)) // 2 * rows + line // (2 * rows)
        same = wanted == lax.broadcasted_iota(jnp.int32, pick.shape, 1)
        pick[...] = jnp.where(same, 1.0, 0.0).astype(pick.dtype)

    odd = lax.broadcasted_iota(jnp.int32, (2 * deep, 1), 0) % 2
    parts = lines.shape[1] // (2 * rows)

    def stacked(part):
        at = [(part * rows + j) * 2 * BS for j in range(rows)]
        return jnp.concatenate([values_ref[:, i : i + 2 * BS] for i in at], axis=0)

    for first in range(0, parts, 2):
        pair = jnp.concatenate([stacked(first), stacked(first + 1)], axis=1)
        picked = jnp.dot(pick[...], pair, preferred_element_type=jnp.float32)
        for part in range(first, first + 2):
            at = (part - first) * 2 * BS
            both = picked[:, at : at + 2 * BS]
            crossed = pltpu.roll(both, BS, 1)
            twice = jnp.where(half == odd, both, crossed).astype(lines.dtype)
            for row in range(rows):
                lines[row, part * 2 * rows : (part + 1) * 2 * rows, :] = twice[
                    row * 2 * rows : (row + 1) * 2 * rows
                ]

    def group(trip, _):
        p = step * GROUPS + trip
        base = GROUP * p - HB + first_ref[0]
        for row in range(GROUP):
            offs = [index_ref[k, GROUP * p + row] - base for k in range(NNZB)]
            blocks = [
                lines[trip * GROUP + row, k * BS : (k + 1) * BS, :] for k in range(NNZB)
            ]
            for tile in range(REACH // (2 * BS)):
                at = slice(tile * 2 * BS, (tile + 1) * 2 * BS)
                if row // 2 <= tile <= (row + 2 * HB) // 2:
                    masks = [
                        jnp.where(half + 2 * tile == off, 1.0, 0.0).astype(band_ref.dtype)
                        for off in offs
                    ]
                    total = blocks[0] * masks[0]
                    for k in range(1, NNZB):
                        total += blocks[k] * masks[k]
                else:
                    total = jnp.zeros((BS, 2 * BS), band_ref.dtype)
                band_ref[p, row * BS : (row + 1) * BS, at] = total
        return 0

    lax.fori_loop(0, GROUPS, group, 0)


def banded(kblocks, blk_index, first_block):
    count, values = kblocks.shape
    groups = count // GROUP
    rows = GROUPS * GROUP
    return pl.pallas_call(
        band_kernel,
        grid=(count // rows,),
        in_specs=[SMEM, SMEM, pl.BlockSpec((rows, values), lambda i: (i, 0))],
        out_specs=VMEM,
        scratch_shapes=[
            pltpu.VMEM((2 * rows * rows, rows * rows), kblocks.dtype),
            pltpu.VMEM((rows, NNZB * BS, 2 * BS), kblocks.dtype),
        ],
        out_shape=jax.ShapeDtypeStruct((groups, GROUP * BS, REACH), jnp.bfloat16),
        compiler_params=pltpu.CompilerParams(vmem_limit_bytes=28 << 20),
        cost_estimate=pl.CostEstimate(flops=0, bytes_accessed=40 << 20, transcendentals=0),
        name="banded",
    )(first_block, blk_index.T, pltpu.with_memory_space_constraint(kblocks, pltpu.HBM))


def residual_kernel(peers, first, low, keep, parts, me_ref, *refs):
    pieces = [refs[j * (peers - 1) : (j + 1) * (peers - 1)] for j in range(parts)]
    refs = refs[parts * (peers - 1) :]
    if keep:
        ends, refs = refs[: peers - 1], refs[peers - 1 :]
    rows_ref, band_ref, sigma_ref = refs[:3]
    out_ref, token_ref, panel, swap, own, own_sem = refs[3 if keep == 0 else 4 :]
    cols, span = own.shape
    columns = panel.shape[0]
    step = pl.program_id(0)
    width = GROUPS * GROUP * BS
    me = me_ref[0]

    @pl.when(step == 0)
    def _():
        token_ref[...] = jnp.zeros_like(token_ref)
        at = start_of(me, peers, rows_ref.shape[1]) + (low - keep)
        copy = pltpu.make_async_copy(
            rows_ref.at[:, pl.ds(pl.multiple_of(at, RIM), span)], own, own_sem
        )
        copy.start()
        panel[:, :RIM] = jnp.zeros((columns, RIM), panel.dtype)
        panel[:, RIM + span :] = jnp.zeros((columns, RIM), panel.dtype)
        row = lax.broadcasted_iota(jnp.int32, (columns, columns), 0)
        col = lax.broadcasted_iota(jnp.int32, (columns, columns), 1)
        sign = jnp.where(row % 2 == 0, -1.0, 1.0)
        swap[...] = jnp.where(row + 1 - 2 * (row % 2) == col, sign, 0.0).astype(swap.dtype)
        for s in range(1, peers):
            at = pl.ds(pl.multiple_of(lax.rem(me + peers - s, peers) * cols, cols), cols)
            if keep:
                panel[at, RIM : RIM + keep] = ends[s - 1][:, ends[s - 1].shape[1] - keep :]
            lane = RIM + keep
            for part in pieces:
                width_of = part[s - 1].shape[1]
                panel[at, lane : lane + width_of] = part[s - 1][...]
                lane += width_of
        copy.wait()
        panel[pl.ds(pl.multiple_of(me * cols, cols), cols), RIM : RIM + span] = own[...]

    moved = jnp.where(me == 0, -RIM, jnp.where(me == peers - 1, RIM, 0))
    start = (step + first) * width + RIM + moved - (low - keep)

    def window(at, size):
        return panel[:, pl.ds(pl.multiple_of(start + at, RIM), size)]

    swapped = jnp.dot(swap[...], window(RIM, width), preferred_element_type=jnp.float32)
    at = pl.multiple_of((step + first) * width, width)
    turned = swapped * sigma_ref[:, pl.ds(at, width)]
    for t in range(GROUPS):
        at = slice(t * GROUP * BS, (t + 1) * GROUP * BS)
        stiff = lax.dot_general(
            window(t * GROUP * BS, REACH),
            band_ref[(step + first) * GROUPS + t],
            (((1,), (1,)), ((), ())),
            preferred_element_type=jnp.float32,
        )
        out_ref[:, at] = (stiff + turned[:, at]).astype(out_ref.dtype)


def residual_of(rows, parts, band, sigma, me, peers):
    cols = rows.shape[0]
    edge_count = sigma.shape[0]
    columns = peers * cols
    width = GROUPS * GROUP * BS
    sigma = sigma.reshape(1, edge_count)
    out, before = None, None
    calls = [parts[:-1], parts[-1:]]
    for call in calls:
        first, low = call[0][0], call[0][2]
        steps = sum(part[1] for part in call)
        keep = KEEP if low else 0
        span = keep + sum(part[3][0].shape[1] for part in call)
        given = [x for part in call for x in part[3]]
        given += (list(before) if keep else []) + [rows, band, sigma]
        specs = [VMEM] * (len(given) - 3) + [HBM, VMEM, VMEM]
        if out is not None:
            given.append(out)
            specs.append(pl.BlockSpec(memory_space=pl.ANY))
        out, token = pl.pallas_call(
            functools.partial(residual_kernel, peers, first, low, keep, len(call)),
            grid_spec=pltpu.PrefetchScalarGridSpec(
                num_scalar_prefetch=1,
                grid=(steps,),
                in_specs=specs,
                out_specs=[
                    pl.BlockSpec((columns, width), lambda i, me, first=first: (0, i + first)),
                    pl.BlockSpec((8, LANE), lambda i, me: (0, 0)),
                ],
                scratch_shapes=[
                    pltpu.VMEM((columns, span + 2 * RIM), jnp.bfloat16),
                    pltpu.VMEM((columns, columns), jnp.bfloat16),
                    pltpu.VMEM((cols, span), rows.dtype),
                    pltpu.SemaphoreType.DMA,
                ],
            ),
            out_shape=[
                jax.ShapeDtypeStruct((columns, edge_count), jnp.bfloat16),
                jax.ShapeDtypeStruct((8, LANE), jnp.float32),
            ],
            input_output_aliases={len(given): 0} if out is not None else {},
            compiler_params=pltpu.CompilerParams(vmem_limit_bytes=24 << 20),
            cost_estimate=pl.CostEstimate(
                flops=2 * columns * steps * width * 384,
                bytes_accessed=(21 << 20) * steps * width // edge_count,
                transcendentals=0,
            ),
        )(me, *given)
        before = call[-1][3]
    return out, token


def on_device(fields, kblocks, blk_index, sigma, rec_edge, rec_weight, rec_owner, rec_slot):
    return ordered(
        fields, kblocks, blk_index, sigma, rec_edge, rec_weight, rec_owner, rec_slot
    )


def ordered(fields, kblocks, blk_index, sigma, rec_edge, rec_weight, rec_owner, rec_slot):
    peers = lax.axis_size("edge")
    shares = lax.axis_size("tx") * lax.axis_size("rcv")
    me = jnp.stack([lax.axis_index("edge"), lax.axis_index(("tx", "rcv"))])
    rows = fields[0]
    edge_count = sigma.shape[0]
    shifts = range(1, peers)

    length = edge_count + 2 * RIM
    width = GROUPS * GROUP * BS
    steps = edge_count // width
    marks = [0, 1, steps // 2, steps - 2, steps]
    lanes = [0] + [m * width + KEEP - RIM for m in marks[1:-1]] + [length]

    rows = pltpu.with_memory_space_constraint(rows, pltpu.HBM)
    mine, blocks = packed(me, rec_edge, rec_weight, rec_owner, rec_slot, rows, peers, lanes, shares)
    parts = []
    for j in range(len(lanes) - 1):
        pieces = [shifted(blocks[j * (peers - 1) + s - 1], s, peers) for s in shifts]
        parts.append((marks[j], marks[j + 1] - marks[j], lanes[j], pieces))
    lists = [mine] + [shifted(mine, s, peers) for s in shifts]
    lists = jnp.concatenate(lists, axis=0)
    lists = [lists] + [
        lax.ppermute(lists, ("tx", "rcv"), [(i, (i + k) % shares) for i in range(shares)])
        for k in range(1, shares)
    ]
    band = banded(kblocks, blk_index, me[:1] * (edge_count // BS))
    own, sent = site_sums(me, turned_rows(me, rows, peers), rows.shape[0], lists, peers)
    got = [own] + [shifted(sent[s - 1], s, peers) for s in shifts]
    residual, token = residual_of(rows, parts, band, sigma, me, peers)
    site_out = placed_rows(me, token, got, peers)
    return residual[None], site_out[None]


def fits(mesh, fields, sigma, rec_edge):
    peers = mesh.shape["edge"]
    cols = fields.shape[1] // peers
    edge_count = sigma.shape[0] // (mesh.shape["grp"] * peers)
    recs = rec_edge.shape[0] // (mesh.shape["grp"] * peers)
    return (
        cols % 16 == 0
        and cols * peers == LANE
        and peers * IW <= LANE
        and edge_count % (GROUPS * GROUP * BS) == 0
        and edge_count >= 8 * GROUPS * GROUP * BS
        and recs % (LANE * mesh.shape["tx"] * mesh.shape["rcv"]) == 0
        and peers > 1
    )


def solution(mesh):
    placed = (
        P(("grp", "tx", "rcv"), "edge", None),
        P("edge", None),
        P("edge", None),
        P(("grp", "edge")),
        P(("grp", "edge"), None),
        P(("grp", "edge"), None),
        P(("grp", "edge"), None),
        P(("grp", "edge")),
    )

    def run(fields, kblocks, blk_index, sigma, rec_edge, rec_weight, rec_owner, rec_slot):
        body = on_device if fits(mesh, fields, sigma, rec_edge) else plain_device
        return jax.shard_map(
            body,
            mesh=mesh,
            in_specs=placed,
            out_specs=(P(("grp", "tx", "rcv"), None, "edge"), P(("grp", "tx", "rcv"), None, "edge")),
            check_vma=False,
        )(fields, kblocks, blk_index, sigma, rec_edge, rec_weight, rec_owner, rec_slot)

    return run
```

```python
import functools
import math

import jax
import jax.numpy as jnp
from jax import lax
from jax.experimental import pallas as pl
from jax.experimental.pallas import tpu as pltpu
from jax.sharding import PartitionSpec as P


BS = 64
NNZB = 3
HB = 2
IW = 8
SDEV = 1024

LANE = 128
GROUP = 4
GROUPS = 4
REACH = GROUP * BS + 2 * BS * HB
RIM = BS * HB
KEEP = 4 * RIM
LINES = 2 * IW + 8
TOP = 32000.0


def padded_2(shard, sides, width):
    for axis, dim in sides:
        peers, length = (lax.axis_size(axis), shard.shape[dim])
        up = [(i, (i + 1) % peers) for i in range(peers - 1)]
        down = [(j, i) for i, j in up]
        last = lax.slice_in_dim(shard, length - width, length, axis=dim)
        initial = lax.slice_in_dim(shard, 0, width, axis=dim)
        before = lax.ppermute(last, axis, up)
        after = lax.ppermute(initial, axis, down)
        shard = jnp.concatenate([before, shard, after], axis=dim)
    return shard


def plain_device(fields, kblocks, blk_index, sigma, rec_edge, rec_weight, rec_owner, rec_slot):
    peers = lax.axis_size("edge")
    edge_count = sigma.shape[0]
    block_count = edge_count // BS
    rec_count = rec_edge.shape[0]
    rim_width = BS * HB
    tx_local = fields.shape[1] // 2
    first_block = lax.axis_index("edge") * block_count
    local_index = blk_index - first_block + HB
    flat_edges = rec_edge.reshape(-1)
    block_vals = kblocks.reshape(block_count, NNZB, BS, BS)
    source = fields.reshape(1, tx_local, 2, fields.shape[2])
    moved = lax.all_to_all(source, "edge", split_axis=3, concat_axis=0, tiled=True)
    item_count = moved.shape[1]
    columns = peers * item_count * 2
    flat_rows = moved.reshape(columns, edge_count)
    padded = padded_2(flat_rows, (("edge", 1),), rim_width)
    blocks = padded.reshape(columns, block_count + 2 * HB, BS)
    picked = jnp.take(blocks, local_index, axis=1)
    stiffness = jnp.einsum("cbkj,bkij->cbi", picked, block_vals, preferred_element_type=jnp.float32)
    stiffness = stiffness.reshape(columns, edge_count)
    paired = flat_rows.reshape(columns // 2, 2, edge_count).astype(jnp.float32)
    diagonal = jnp.stack([-sigma * paired[:, 1], sigma * paired[:, 0]], axis=1).reshape(
        columns, edge_count
    )
    residual = (stiffness + diagonal).astype(jnp.bfloat16).reshape(1, columns, edge_count)
    interp_vals = (
        jnp.take(flat_rows, flat_edges, axis=1).reshape(columns, rec_count, IW).astype(jnp.float32)
    )
    predicted = jnp.sum(interp_vals * rec_weight[None], axis=2)
    site_ids = rec_owner[:, 0] * SDEV + rec_slot
    local_sums = jax.ops.segment_sum(predicted.T, site_ids, num_segments=peers * SDEV)
    site_table = lax.psum_scatter(local_sums.T, "edge", scatter_dimension=1, tiled=True)
    return (residual, site_table.reshape(1, columns, SDEV))


def shifted(x, shift, peers):
    return lax.ppermute(x, "edge", [(i, (i + shift) % peers) for i in range(peers)])


HBM = pl.BlockSpec(memory_space=pltpu.HBM)
VMEM = pl.BlockSpec(memory_space=pltpu.VMEM)
SMEM = pl.BlockSpec(memory_space=pltpu.SMEM)


def pack_kernel(peers, lanes, me_ref, edge_ref, weight_ref, owner_ref, slot_ref, rows_ref, *refs):
    parts = len(lanes) - 1
    count = parts * (peers - 1)
    list_ref, pieces, refs = refs[0], refs[1 : 1 + count], refs[1 + count :]
    edges, weights, owners, slots, list_sems, sems = refs
    recs = list_ref.shape[1]
    share = pl.ds(pl.multiple_of(me_ref[1] * recs, recs), recs)
    small = [
        pltpu.make_async_copy(source.at[:, share], target, list_sems.at[i])
        for i, (source, target) in enumerate(
            [(edge_ref, edges), (weight_ref, weights), (owner_ref, owners), (slot_ref, slots)]
        )
    ]
    for copy in small:
        copy.start()
    taken = []
    for j in range(parts):
        for s in range(1, peers):
            target = lax.rem(me_ref[0] + s, peers)
            start = start_of(target, peers, rows_ref.shape[1]) + lanes[j]
            n = len(taken)
            taken.append(
                pltpu.make_async_copy(
                    rows_ref.at[:, pl.ds(pl.multiple_of(start, RIM), lanes[j + 1] - lanes[j])],
                    pieces[n],
                    sems.at[n],
                )
            )
    for copy in taken:
        copy.start()
    for copy in small:
        copy.wait()
    list_ref[:IW, :] = edges[...].astype(jnp.float32)
    list_ref[IW : 2 * IW, :] = weights[...]
    sites = (owners[...] * SDEV + slots[...]).astype(jnp.float32)
    list_ref[2 * IW :, :] = jnp.broadcast_to(sites, (LINES - 2 * IW, recs))
    for copy in taken:
        copy.wait()


def start_of(target, peers, all_edges):
    edge_count = all_edges // peers
    return jnp.clip(target * edge_count - RIM, 0, all_edges - edge_count - 2 * RIM)


def packed(me, rec_edge, rec_weight, rec_owner, rec_slot, rows, peers, lanes, shares):
    recs = rec_slot.shape[0]
    share = recs // shares
    cols = rows.shape[0]
    shapes = [
        (cols, high - low) for low, high in zip(lanes, lanes[1:]) for _ in range(1, peers)
    ]
    small = [rec_edge.T, rec_weight.T, rec_owner.T, rec_slot.reshape(1, recs)]
    out = pl.pallas_call(
        functools.partial(pack_kernel, peers, lanes),
        in_specs=[SMEM] + [HBM] * 5,
        out_specs=[VMEM] * (1 + len(shapes)),
        out_shape=[jax.ShapeDtypeStruct((LINES, share), jnp.float32)]
        + [jax.ShapeDtypeStruct(shape, rows.dtype) for shape in shapes],
        scratch_shapes=[pltpu.VMEM((x.shape[0], share), x.dtype) for x in small]
        + [
            pltpu.SemaphoreType.DMA((len(small),)),
            pltpu.SemaphoreType.DMA((len(shapes),)),
        ],
        compiler_params=pltpu.CompilerParams(vmem_limit_bytes=8 << 20),
        cost_estimate=pl.CostEstimate(flops=0, bytes_accessed=8 << 20, transcendentals=0),
        name="packed",
    )(me, *[pltpu.with_memory_space_constraint(x, pltpu.HBM) for x in small], rows)
    return out[0], out[1:]


def site_kernel(peers, shares, me_ref, rows_ref, *refs):
    list_refs, refs = refs[:shares], refs[shares:]
    own_ref, sent_refs, refs = refs[0], refs[1:peers], refs[peers:]
    out_ref, rows, turned, picked, pred, ints, scale, row_sems, int_sems = refs[:9]
    refs = refs[9:]
    edge_refs = [refs[s * (IW + 1) : (s + 1) * (IW + 1)] for s in range(peers)]
    tables = refs[peers * (IW + 1) :]
    cols = own_ref.shape[0]
    share = list_refs[0].shape[1]
    recs = shares * share
    per = picked.shape[1]
    edge_count = turned.shape[0]
    parts = row_sems.shape[0]
    width = edge_count // parts

    def fetch(part, s):
        start = lax.rem(me_ref[0] + peers - s, peers) * edge_count + part * width
        return pltpu.make_async_copy(
            rows_ref.at[:, pl.ds(pl.multiple_of(start, LANE), width)],
            rows.at[pl.ds(s * cols, cols), pl.ds(part * width, width)],
            row_sems.at[part, s],
        )

    for part in range(parts):
        for s in range(peers):
            fetch(part, s).start()
    lists = []
    for s in range(peers):
        for j, ref in enumerate(list_refs):
            at = slice(j * share, (j + 1) * share)
            edges = ref[s * LINES : s * LINES + IW, :]
            ints[s, :IW, at] = edges.astype(jnp.int32)
            scale[s * IW : (s + 1) * IW, at] = ref[s * LINES + IW : s * LINES + 2 * IW, :]
            sites = ref[s * LINES + 2 * IW : (s + 1) * LINES, :]
            ints[s, IW:, at] = sites.astype(jnp.int32)
        for k in range(IW + 1):
            copy = pltpu.make_async_copy(
                ints.at[s, pl.ds(k, 1)], edge_refs[s][k], int_sems.at[s, k]
            )
            copy.start()
            lists.append(copy)
    scale[peers * IW :, :] = jnp.zeros((LANE - peers * IW, recs), jnp.float32)
    for table in tables:
        table[...] = jnp.zeros_like(table)

    for part in range(parts):
        for s in range(peers):
            fetch(part, s).wait()

        def turn(t, _, part=part):
            at = pl.multiple_of(part * width + t * LANE, LANE)
            turned[pl.ds(at, LANE), :] = rows[:, pl.ds(at, LANE)].T.astype(jnp.float32)
            return 0

        lax.fori_loop(0, width // LANE, turn, 0, unroll=2)
    lane = lax.broadcasted_iota(jnp.int32, (1, LANE), 1) // cols
    lanes = lax.broadcasted_iota(jnp.int32, (per, LANE), 1) // cols
    for copy in lists:
        copy.wait()

    def receivers(g, _):
        first = pl.multiple_of(g * per, per)

        def gather(r, _):
            for k in range(IW):
                row = turned[pl.ds(edge_refs[0][k][0, first + r], 1), :]
                for q in range(1, peers):
                    other = turned[pl.ds(edge_refs[q][k][0, first + r], 1), :]
                    row = jnp.where(lane == q, other, row)
                picked[k, pl.ds(r, 1), :] = row
            return 0

        lax.fori_loop(0, per, gather, 0, unroll=4)
        weights = scale[:, pl.ds(first, per)].T
        total = jnp.zeros((per, LANE), jnp.float32)
        for k in range(IW):
            total += picked[k] * jnp.take_along_axis(weights, lanes * IW + k, axis=1)
        pred[...] = total

        def scatter(r, _):
            row = pred[pl.ds(r, 1), :]
            for q in range(peers):
                at = pl.ds(edge_refs[q][IW][0, first + r], 1)
                tables[q][at, :] = tables[q][at, :] + row
            return 0

        lax.fori_loop(0, per, scatter, 0, unroll=8)
        return 0

    lax.fori_loop(0, recs // per, receivers, 0)
    owned = out_ref.shape[2]
    per_owner = owned // LANE

    def back(t, _):
        at = pl.ds(pl.multiple_of(t * LANE, LANE), LANE)
        tile = tables[0][at, :]
        for q in range(1, peers):
            tile = jnp.where(lane == q, tables[q][at, :], tile)
        tile = tile.T
        total = tile[:cols]
        for q in range(1, peers):
            total += tile[q * cols : (q + 1) * cols]
        out_ref[t // per_owner, :, pl.ds(pl.multiple_of((t % per_owner) * LANE, LANE), LANE)] = total
        return 0

    lax.fori_loop(0, peers * per_owner, back, 0)
    own_ref[...] = out_ref[me_ref[0]]
    for s in range(1, peers):
        block = out_ref[lax.rem(me_ref[0] + s, peers)]
        most = jnp.max(jnp.abs(block), axis=1, keepdims=True)
        power = jnp.floor(jnp.log(jnp.maximum(most, 1e-36)) * (1 / math.log(2.0))) + 1.0
        coded = jnp.round(block * (TOP * jnp.exp2(-power)))
        sent_refs[s - 1][:, :owned] = coded.astype(jnp.int32).astype(jnp.int16)
        power = jnp.broadcast_to(power, (cols, LANE))
        sent_refs[s - 1][:, owned:] = power.astype(jnp.int32).astype(jnp.int16)


def site_sums(me, rows, lists, peers):
    cols, all_edges = rows.shape
    edge_count = all_edges // peers
    per = LANE
    parts = 4
    shares = len(lists)
    recs = lists[0].shape[1] * shares
    sent = jax.ShapeDtypeStruct((cols, SDEV + LANE), jnp.int16)
    out = pl.pallas_call(
        functools.partial(site_kernel, peers, shares),
        in_specs=[SMEM, HBM] + [VMEM] * shares,
        out_specs=[VMEM] * peers,
        out_shape=[jax.ShapeDtypeStruct((cols, SDEV), jnp.float32)] + [sent] * (peers - 1),
        scratch_shapes=[
            pltpu.VMEM((peers, cols, SDEV), jnp.float32),
            pltpu.VMEM((peers * cols, edge_count), rows.dtype),
            pltpu.VMEM((edge_count, LANE), jnp.float32),
            pltpu.VMEM((IW, per, LANE), jnp.float32),
            pltpu.VMEM((per, LANE), jnp.float32),
            pltpu.VMEM((peers, IW + 8, recs), jnp.int32),
            pltpu.VMEM((LANE, recs), jnp.float32),
            pltpu.SemaphoreType.DMA((parts, peers)),
            pltpu.SemaphoreType.DMA((peers, IW + 1)),
        ]
        + [pltpu.SMEM((1, recs), jnp.int32)] * (peers * (IW + 1))
        + [pltpu.VMEM((peers * SDEV, LANE), jnp.float32)] * peers,
        compiler_params=pltpu.CompilerParams(vmem_limit_bytes=24 << 20),
        cost_estimate=pl.CostEstimate(
            flops=2 * recs * peers * IW * 8 * LANE, bytes_accessed=64 << 20, transcendentals=0
        ),
        name="site_sums",
    )(me, rows, *lists)
    return out[0], out[1:]


def place_kernel(peers, me_ref, _, *refs):
    out_ref = refs[peers]
    cols, width = refs[0].shape
    for s in range(peers):
        at = lax.rem(me_ref[0] + peers - s, peers) * cols
        block = refs[s][:, :width].astype(jnp.int32) if s else refs[s][...]
        if s:
            power = refs[s][:, width:].astype(jnp.int32).astype(jnp.float32)
            block = block.astype(jnp.float32) * (jnp.exp2(power[:, :1]) * (1 / TOP))
        out_ref[pl.ds(pl.multiple_of(at, 8), cols), :] = block


def placed_rows(me, after, got, peers):
    cols, width = got[0].shape
    return pl.pallas_call(
        functools.partial(place_kernel, peers),
        in_specs=[SMEM] + [VMEM] * (peers + 1),
        out_specs=VMEM,
        out_shape=jax.ShapeDtypeStruct((peers * cols, width), got[0].dtype),
        compiler_params=pltpu.CompilerParams(vmem_limit_bytes=4 << 20),
        name="placed_rows",
    )(me, after, *got)


def band_kernel(first_ref, index_ref, values_ref, band_ref, pick, lines):
    step = pl.program_id(0)
    rows = values_ref.shape[0]
    deep = rows * rows
    half = lax.broadcasted_iota(jnp.int32, (1, 2 * BS), 1) // BS

    @pl.when(step == 0)
    def _():
        line = lax.broadcasted_iota(jnp.int32, pick.shape, 0)
        wanted = (line % (2 * rows)) // 2 * rows + line // (2 * rows)
        same = wanted == lax.broadcasted_iota(jnp.int32, pick.shape, 1)
        pick[...] = jnp.where(same, 1.0, 0.0).astype(pick.dtype)

    odd = lax.broadcasted_iota(jnp.int32, (2 * deep, 1), 0) % 2
    parts = lines.shape[1] // (2 * rows)

    def stacked(part):
        at = [(part * rows + j) * 2 * BS for j in range(rows)]
        return jnp.concatenate([values_ref[:, i : i + 2 * BS] for i in at], axis=0)

    for first in range(0, parts, 2):
        pair = jnp.concatenate([stacked(first), stacked(first + 1)], axis=1)
        picked = jnp.dot(pick[...], pair, preferred_element_type=jnp.float32)
        for part in range(first, first + 2):
            at = (part - first) * 2 * BS
            both = picked[:, at : at + 2 * BS]
            crossed = pltpu.roll(both, BS, 1)
            twice = jnp.where(half == odd, both, crossed).astype(lines.dtype)
            for row in range(rows):
                lines[row, part * 2 * rows : (part + 1) * 2 * rows, :] = twice[
                    row * 2 * rows : (row + 1) * 2 * rows
                ]

    def group(trip, _):
        p = step * GROUPS + trip
        base = GROUP * p - HB + first_ref[0]
        for row in range(GROUP):
            offs = [index_ref[k, GROUP * p + row] - base for k in range(NNZB)]
            blocks = [
                lines[trip * GROUP + row, k * BS : (k + 1) * BS, :] for k in range(NNZB)
            ]
            for tile in range(REACH // (2 * BS)):
                at = slice(tile * 2 * BS, (tile + 1) * 2 * BS)
                if row // 2 <= tile <= (row + 2 * HB) // 2:
                    masks = [
                        jnp.where(half + 2 * tile == off, 1.0, 0.0).astype(band_ref.dtype)
                        for off in offs
                    ]
                    total = blocks[0] * masks[0]
                    for k in range(1, NNZB):
                        total += blocks[k] * masks[k]
                else:
                    total = jnp.zeros((BS, 2 * BS), band_ref.dtype)
                band_ref[p, row * BS : (row + 1) * BS, at] = total
        return 0

    lax.fori_loop(0, GROUPS, group, 0)


def banded(kblocks, blk_index, first_block):
    count, values = kblocks.shape
    groups = count // GROUP
    rows = GROUPS * GROUP
    return pl.pallas_call(
        band_kernel,
        grid=(count // rows,),
        in_specs=[SMEM, SMEM, pl.BlockSpec((rows, values), lambda i: (i, 0))],
        out_specs=VMEM,
        scratch_shapes=[
            pltpu.VMEM((2 * rows * rows, rows * rows), kblocks.dtype),
            pltpu.VMEM((rows, NNZB * BS, 2 * BS), kblocks.dtype),
        ],
        out_shape=jax.ShapeDtypeStruct((groups, GROUP * BS, REACH), jnp.bfloat16),
        compiler_params=pltpu.CompilerParams(vmem_limit_bytes=28 << 20),
        cost_estimate=pl.CostEstimate(flops=0, bytes_accessed=40 << 20, transcendentals=0),
        name="banded",
    )(first_block, blk_index.T, pltpu.with_memory_space_constraint(kblocks, pltpu.HBM))


def residual_kernel(peers, first, low, keep, parts, me_ref, *refs):
    pieces = [refs[j * (peers - 1) : (j + 1) * (peers - 1)] for j in range(parts)]
    refs = refs[parts * (peers - 1) :]
    if keep:
        ends, refs = refs[: peers - 1], refs[peers - 1 :]
    rows_ref, band_ref, sigma_ref = refs[:3]
    out_ref, token_ref, panel, swap, own, own_sem = refs[3 if keep == 0 else 4 :]
    cols, span = own.shape
    columns = panel.shape[0]
    step = pl.program_id(0)
    width = GROUPS * GROUP * BS
    me = me_ref[0]

    @pl.when(step == 0)
    def _():
        token_ref[...] = jnp.zeros_like(token_ref)
        at = start_of(me, peers, rows_ref.shape[1]) + (low - keep)
        copy = pltpu.make_async_copy(
            rows_ref.at[:, pl.ds(pl.multiple_of(at, RIM), span)], own, own_sem
        )
        copy.start()
        panel[:, :RIM] = jnp.zeros((columns, RIM), panel.dtype)
        panel[:, RIM + span :] = jnp.zeros((columns, RIM), panel.dtype)
        row = lax.broadcasted_iota(jnp.int32, (columns, columns), 0)
        col = lax.broadcasted_iota(jnp.int32, (columns, columns), 1)
        sign = jnp.where(row % 2 == 0, -1.0, 1.0)
        swap[...] = jnp.where(row + 1 - 2 * (row % 2) == col, sign, 0.0).astype(swap.dtype)
        for s in range(1, peers):
            at = pl.ds(pl.multiple_of(lax.rem(me + peers - s, peers) * cols, cols), cols)
            if keep:
                panel[at, RIM : RIM + keep] = ends[s - 1][:, ends[s - 1].shape[1] - keep :]
            lane = RIM + keep
            for part in pieces:
                width_of = part[s - 1].shape[1]
                panel[at, lane : lane + width_of] = part[s - 1][...]
                lane += width_of
        copy.wait()
        panel[pl.ds(pl.multiple_of(me * cols, cols), cols), RIM : RIM + span] = own[...]

    moved = jnp.where(me == 0, -RIM, jnp.where(me == peers - 1, RIM, 0))
    start = (step + first) * width + RIM + moved - (low - keep)

    def window(at, size):
        return panel[:, pl.ds(pl.multiple_of(start + at, RIM), size)]

    swapped = jnp.dot(swap[...], window(RIM, width), preferred_element_type=jnp.float32)
    at = pl.multiple_of((step + first) * width, width)
    turned = swapped * sigma_ref[:, pl.ds(at, width)]
    for t in range(GROUPS):
        at = slice(t * GROUP * BS, (t + 1) * GROUP * BS)
        stiff = lax.dot_general(
            window(t * GROUP * BS, REACH),
            band_ref[(step + first) * GROUPS + t],
            (((1,), (1,)), ((), ())),
            preferred_element_type=jnp.float32,
        )
        out_ref[:, at] = (stiff + turned[:, at]).astype(out_ref.dtype)


def residual_of(rows, parts, band, sigma, me, peers):
    cols = rows.shape[0]
    edge_count = sigma.shape[0]
    columns = peers * cols
    width = GROUPS * GROUP * BS
    sigma = sigma.reshape(1, edge_count)
    out, before = None, None
    calls = [parts[:3], parts[3:]]
    for call in calls:
        first, low = call[0][0], call[0][2]
        steps = sum(part[1] for part in call)
        keep = KEEP if low else 0
        span = keep + sum(part[3][0].shape[1] for part in call)
        given = [x for part in call for x in part[3]]
        given += (list(before) if keep else []) + [rows, band, sigma]
        specs = [VMEM] * (len(given) - 3) + [HBM, VMEM, VMEM]
        if out is not None:
            given.append(out)
            specs.append(pl.BlockSpec(memory_space=pl.ANY))
        out, token = pl.pallas_call(
            functools.partial(residual_kernel, peers, first, low, keep, len(call)),
            grid_spec=pltpu.PrefetchScalarGridSpec(
                num_scalar_prefetch=1,
                grid=(steps,),
                in_specs=specs,
                out_specs=[
                    pl.BlockSpec((columns, width), lambda i, me, first=first: (0, i + first)),
                    pl.BlockSpec((8, LANE), lambda i, me: (0, 0)),
                ],
                scratch_shapes=[
                    pltpu.VMEM((columns, span + 2 * RIM), jnp.bfloat16),
                    pltpu.VMEM((columns, columns), jnp.bfloat16),
                    pltpu.VMEM((cols, span), rows.dtype),
                    pltpu.SemaphoreType.DMA,
                ],
            ),
            out_shape=[
                jax.ShapeDtypeStruct((columns, edge_count), jnp.bfloat16),
                jax.ShapeDtypeStruct((8, LANE), jnp.float32),
            ],
            input_output_aliases={len(given): 0} if out is not None else {},
            compiler_params=pltpu.CompilerParams(vmem_limit_bytes=24 << 20),
            cost_estimate=pl.CostEstimate(
                flops=2 * columns * steps * width * 384,
                bytes_accessed=(21 << 20) * steps * width // edge_count,
                transcendentals=0,
            ),
        )(me, *given)
        before = call[-1][3]
    return out, token


def on_device(fields, kblocks, blk_index, sigma, rec_edge, rec_weight, rec_owner, rec_slot):
    return ordered(
        fields, kblocks, blk_index, sigma, rec_edge, rec_weight, rec_owner, rec_slot
    )


def ordered(fields, kblocks, blk_index, sigma, rec_edge, rec_weight, rec_owner, rec_slot):
    peers = lax.axis_size("edge")
    shares = lax.axis_size("tx") * lax.axis_size("rcv")
    me = jnp.stack([lax.axis_index("edge"), lax.axis_index(("tx", "rcv"))])
    rows = fields[0]
    edge_count = sigma.shape[0]
    shifts = range(1, peers)

    length = edge_count + 2 * RIM
    width = GROUPS * GROUP * BS
    marks = [0, 1, 7, 12, 16]
    lanes = [0] + [m * width + KEEP - RIM for m in marks[1:-1]] + [length]

    rows = pltpu.with_memory_space_constraint(rows, pltpu.HBM)
    mine, blocks = packed(me, rec_edge, rec_weight, rec_owner, rec_slot, rows, peers, lanes, shares)
    parts = []
    for j in range(len(lanes) - 1):
        pieces = [shifted(blocks[j * (peers - 1) + s - 1], s, peers) for s in shifts]
        parts.append((marks[j], marks[j + 1] - marks[j], lanes[j], pieces))
    lists = [mine] + [shifted(mine, s, peers) for s in shifts]
    lists = jnp.concatenate(lists, axis=0)
    lists = [lists] + [
        lax.ppermute(lists, ("tx", "rcv"), [(i, (i + k) % shares) for i in range(shares)])
        for k in range(1, shares)
    ]
    band = banded(kblocks, blk_index, me[:1] * (edge_count // BS))
    own, sent = site_sums(me, rows, lists, peers)
    got = [own] + [shifted(sent[s - 1], s, peers) for s in shifts]
    residual, token = residual_of(rows, parts, band, sigma, me, peers)
    site_out = placed_rows(me, token, got, peers)
    return residual[None], site_out[None]


def fits(mesh, fields, sigma, rec_edge):
    peers = mesh.shape["edge"]
    cols = fields.shape[1] // peers
    edge_count = sigma.shape[0] // (mesh.shape["grp"] * peers)
    recs = rec_edge.shape[0] // (mesh.shape["grp"] * peers)
    return (
        cols % 16 == 0
        and cols * peers == LANE
        and peers * IW <= LANE
        and edge_count % (GROUPS * GROUP * BS) == 0
        and edge_count >= 8 * GROUPS * GROUP * BS
        and recs % (LANE * mesh.shape["tx"] * mesh.shape["rcv"]) == 0
        and peers > 1
    )


def solution(mesh):
    placed = (
        P(("grp", "tx", "rcv"), "edge", None),
        P("edge", None),
        P("edge", None),
        P(("grp", "edge")),
        P(("grp", "edge"), None),
        P(("grp", "edge"), None),
        P(("grp", "edge"), None),
        P(("grp", "edge")),
    )

    def run(fields, kblocks, blk_index, sigma, rec_edge, rec_weight, rec_owner, rec_slot):
        body = on_device if fits(mesh, fields, sigma, rec_edge) else plain_device
        return jax.shard_map(
            body,
            mesh=mesh,
            in_specs=placed,
            out_specs=(P(("grp", "tx", "rcv"), None, "edge"), P(("grp", "tx", "rcv"), None, "edge")),
            check_vma=False,
        )(fields, kblocks, blk_index, sigma, rec_edge, rec_weight, rec_owner, rec_slot)

    return run
```

```python
import functools
import math

import jax
import jax.numpy as jnp
from jax import lax
from jax.experimental import pallas as pl
from jax.experimental.pallas import tpu as pltpu
from jax.sharding import PartitionSpec as P


BS = 64
NNZB = 3
HB = 2
IW = 8
SDEV = 1024

LANE = 128
GROUP = 4
GROUPS = 4
REACH = GROUP * BS + 2 * BS * HB
RIM = BS * HB
KEEP = 4 * RIM
LINES = 2 * IW + 8
TOP = 32000.0


def padded_2(shard, sides, width):
    for axis, dim in sides:
        peers, length = (lax.axis_size(axis), shard.shape[dim])
        up = [(i, (i + 1) % peers) for i in range(peers - 1)]
        down = [(j, i) for i, j in up]
        last = lax.slice_in_dim(shard, length - width, length, axis=dim)
        initial = lax.slice_in_dim(shard, 0, width, axis=dim)
        before = lax.ppermute(last, axis, up)
        after = lax.ppermute(initial, axis, down)
        shard = jnp.concatenate([before, shard, after], axis=dim)
    return shard


def plain_device(fields, kblocks, blk_index, sigma, rec_edge, rec_weight, rec_owner, rec_slot):
    peers = lax.axis_size("edge")
    edge_count = sigma.shape[0]
    block_count = edge_count // BS
    rec_count = rec_edge.shape[0]
    rim_width = BS * HB
    tx_local = fields.shape[1] // 2
    first_block = lax.axis_index("edge") * block_count
    local_index = blk_index - first_block + HB
    flat_edges = rec_edge.reshape(-1)
    block_vals = kblocks.reshape(block_count, NNZB, BS, BS)
    source = fields.reshape(1, tx_local, 2, fields.shape[2])
    moved = lax.all_to_all(source, "edge", split_axis=3, concat_axis=0, tiled=True)
    item_count = moved.shape[1]
    columns = peers * item_count * 2
    flat_rows = moved.reshape(columns, edge_count)
    padded = padded_2(flat_rows, (("edge", 1),), rim_width)
    blocks = padded.reshape(columns, block_count + 2 * HB, BS)
    picked = jnp.take(blocks, local_index, axis=1)
    stiffness = jnp.einsum("cbkj,bkij->cbi", picked, block_vals, preferred_element_type=jnp.float32)
    stiffness = stiffness.reshape(columns, edge_count)
    paired = flat_rows.reshape(columns // 2, 2, edge_count).astype(jnp.float32)
    diagonal = jnp.stack([-sigma * paired[:, 1], sigma * paired[:, 0]], axis=1).reshape(
        columns, edge_count
    )
    residual = (stiffness + diagonal).astype(jnp.bfloat16).reshape(1, columns, edge_count)
    interp_vals = (
        jnp.take(flat_rows, flat_edges, axis=1).reshape(columns, rec_count, IW).astype(jnp.float32)
    )
    predicted = jnp.sum(interp_vals * rec_weight[None], axis=2)
    site_ids = rec_owner[:, 0] * SDEV + rec_slot
    local_sums = jax.ops.segment_sum(predicted.T, site_ids, num_segments=peers * SDEV)
    site_table = lax.psum_scatter(local_sums.T, "edge", scatter_dimension=1, tiled=True)
    return (residual, site_table.reshape(1, columns, SDEV))


def shifted(x, shift, peers):
    return lax.ppermute(x, "edge", [(i, (i + shift) % peers) for i in range(peers)])


HBM = pl.BlockSpec(memory_space=pltpu.HBM)
VMEM = pl.BlockSpec(memory_space=pltpu.VMEM)
SMEM = pl.BlockSpec(memory_space=pltpu.SMEM)


def pack_kernel(peers, lanes, me_ref, edge_ref, weight_ref, owner_ref, slot_ref, rows_ref, *refs):
    parts = len(lanes) - 1
    count = parts * (peers - 1)
    list_ref, pieces, refs = refs[0], refs[1 : 1 + count], refs[1 + count :]
    edges, weights, owners, slots, list_sems, sems = refs
    recs = list_ref.shape[1]
    share = pl.ds(pl.multiple_of(me_ref[1] * recs, recs), recs)
    small = [
        pltpu.make_async_copy(source.at[:, share], target, list_sems.at[i])
        for i, (source, target) in enumerate(
            [(edge_ref, edges), (weight_ref, weights), (owner_ref, owners), (slot_ref, slots)]
        )
    ]
    for copy in small:
        copy.start()
    taken = []
    for j in range(parts):
        for s in range(1, peers):
            target = lax.rem(me_ref[0] + s, peers)
            start = start_of(target, peers, rows_ref.shape[1]) + lanes[j]
            n = len(taken)
            taken.append(
                pltpu.make_async_copy(
                    rows_ref.at[:, pl.ds(pl.multiple_of(start, RIM), lanes[j + 1] - lanes[j])],
                    pieces[n],
                    sems.at[n],
                )
            )
    for copy in taken:
        copy.start()
    for copy in small:
        copy.wait()
    list_ref[:IW, :] = edges[...].astype(jnp.float32)
    list_ref[IW : 2 * IW, :] = weights[...]
    sites = (owners[...] * SDEV + slots[...]).astype(jnp.float32)
    list_ref[2 * IW :, :] = jnp.broadcast_to(sites, (LINES - 2 * IW, recs))
    for copy in taken:
        copy.wait()


def start_of(target, peers, all_edges):
    edge_count = all_edges // peers
    return jnp.clip(target * edge_count - RIM, 0, all_edges - edge_count - 2 * RIM)


def packed(me, rec_edge, rec_weight, rec_owner, rec_slot, rows, peers, lanes, shares):
    recs = rec_slot.shape[0]
    share = recs // shares
    cols = rows.shape[0]
    shapes = [
        (cols, high - low) for low, high in zip(lanes, lanes[1:]) for _ in range(1, peers)
    ]
    small = [rec_edge.T, rec_weight.T, rec_owner.T, rec_slot.reshape(1, recs)]
    out = pl.pallas_call(
        functools.partial(pack_kernel, peers, lanes),
        in_specs=[SMEM] + [HBM] * 5,
        out_specs=[VMEM] * (1 + len(shapes)),
        out_shape=[jax.ShapeDtypeStruct((LINES, share), jnp.float32)]
        + [jax.ShapeDtypeStruct(shape, rows.dtype) for shape in shapes],
        scratch_shapes=[pltpu.VMEM((x.shape[0], share), x.dtype) for x in small]
        + [
            pltpu.SemaphoreType.DMA((len(small),)),
            pltpu.SemaphoreType.DMA((len(shapes),)),
        ],
        compiler_params=pltpu.CompilerParams(vmem_limit_bytes=8 << 20),
        cost_estimate=pl.CostEstimate(flops=0, bytes_accessed=8 << 20, transcendentals=0),
        name="packed",
    )(me, *[pltpu.with_memory_space_constraint(x, pltpu.HBM) for x in small], rows)
    return out[0], out[1:]


def site_kernel(peers, shares, me_ref, rows_ref, *refs):
    list_refs, refs = refs[:shares], refs[shares:]
    own_ref, sent_refs, refs = refs[0], refs[1:peers], refs[peers:]
    out_ref, rows, turned, picked, pred, ints, scale, row_sems, int_sems = refs[:9]
    refs = refs[9:]
    edge_refs = [refs[s * (IW + 1) : (s + 1) * (IW + 1)] for s in range(peers)]
    tables = refs[peers * (IW + 1) :]
    cols = own_ref.shape[0]
    share = list_refs[0].shape[1]
    recs = shares * share
    per = picked.shape[1]
    edge_count = turned.shape[0]
    parts = row_sems.shape[0]
    width = edge_count // parts

    def fetch(part, s):
        start = lax.rem(me_ref[0] + peers - s, peers) * edge_count + part * width
        return pltpu.make_async_copy(
            rows_ref.at[:, pl.ds(pl.multiple_of(start, LANE), width)],
            rows.at[pl.ds(s * cols, cols), pl.ds(part * width, width)],
            row_sems.at[part, s],
        )

    for part in range(parts):
        for s in range(peers):
            fetch(part, s).start()
    lists = []
    for s in range(peers):
        for j, ref in enumerate(list_refs):
            at = slice(j * share, (j + 1) * share)
            edges = ref[s * LINES : s * LINES + IW, :]
            ints[s, :IW, at] = edges.astype(jnp.int32)
            scale[s * IW : (s + 1) * IW, at] = ref[s * LINES + IW : s * LINES + 2 * IW, :]
            sites = ref[s * LINES + 2 * IW : (s + 1) * LINES, :]
            ints[s, IW:, at] = sites.astype(jnp.int32)
        for k in range(IW + 1):
            copy = pltpu.make_async_copy(
                ints.at[s, pl.ds(k, 1)], edge_refs[s][k], int_sems.at[s, k]
            )
            copy.start()
            lists.append(copy)
    scale[peers * IW :, :] = jnp.zeros((LANE - peers * IW, recs), jnp.float32)
    for table in tables:
        table[...] = jnp.zeros_like(table)

    for part in range(parts):
        for s in range(peers):
            fetch(part, s).wait()

        def turn(t, _, part=part):
            at = pl.multiple_of(part * width + t * LANE, LANE)
            turned[pl.ds(at, LANE), :] = rows[:, pl.ds(at, LANE)].T.astype(jnp.float32)
            return 0

        lax.fori_loop(0, width // LANE, turn, 0, unroll=2)
    lane = lax.broadcasted_iota(jnp.int32, (1, LANE), 1) // cols
    lanes = lax.broadcasted_iota(jnp.int32, (per, LANE), 1) // cols
    for copy in lists:
        copy.wait()

    def receivers(g, _):
        first = pl.multiple_of(g * per, per)

        def gather(r, _):
            for k in range(IW):
                row = turned[pl.ds(edge_refs[0][k][0, first + r], 1), :]
                for q in range(1, peers):
                    other = turned[pl.ds(edge_refs[q][k][0, first + r], 1), :]
                    row = jnp.where(lane == q, other, row)
                picked[k, pl.ds(r, 1), :] = row
            return 0

        lax.fori_loop(0, per, gather, 0, unroll=4)
        weights = scale[:, pl.ds(first, per)].T
        total = jnp.zeros((per, LANE), jnp.float32)
        for k in range(IW):
            total += picked[k] * jnp.take_along_axis(weights, lanes * IW + k, axis=1)
        pred[...] = total

        def scatter(r, _):
            row = pred[pl.ds(r, 1), :]
            for q in range(peers):
                at = pl.ds(edge_refs[q][IW][0, first + r], 1)
                tables[q][at, :] = tables[q][at, :] + row
            return 0

        lax.fori_loop(0, per, scatter, 0, unroll=8)
        return 0

    lax.fori_loop(0, recs // per, receivers, 0)
    owned = out_ref.shape[2]
    per_owner = owned // LANE

    def back(t, _):
        at = pl.ds(pl.multiple_of(t * LANE, LANE), LANE)
        tile = tables[0][at, :]
        for q in range(1, peers):
            tile = jnp.where(lane == q, tables[q][at, :], tile)
        tile = tile.T
        total = tile[:cols]
        for q in range(1, peers):
            total += tile[q * cols : (q + 1) * cols]
        out_ref[t // per_owner, :, pl.ds(pl.multiple_of((t % per_owner) * LANE, LANE), LANE)] = total
        return 0

    lax.fori_loop(0, peers * per_owner, back, 0)
    own_ref[...] = out_ref[me_ref[0]]
    for s in range(1, peers):
        block = out_ref[lax.rem(me_ref[0] + s, peers)]
        most = jnp.max(jnp.abs(block), axis=1, keepdims=True)
        power = jnp.floor(jnp.log(jnp.maximum(most, 1e-36)) * (1 / math.log(2.0))) + 1.0
        coded = jnp.round(block * (TOP * jnp.exp2(-power)))
        sent_refs[s - 1][:, :owned] = coded.astype(jnp.int32).astype(jnp.int16)
        power = jnp.broadcast_to(power, (cols, LANE))
        sent_refs[s - 1][:, owned:] = power.astype(jnp.int32).astype(jnp.int16)


def site_sums(me, rows, lists, peers):
    cols, all_edges = rows.shape
    edge_count = all_edges // peers
    per = LANE
    parts = 4
    shares = len(lists)
    recs = lists[0].shape[1] * shares
    sent = jax.ShapeDtypeStruct((cols, SDEV + LANE), jnp.int16)
    out = pl.pallas_call(
        functools.partial(site_kernel, peers, shares),
        in_specs=[SMEM, HBM] + [VMEM] * shares,
        out_specs=[VMEM] * peers,
        out_shape=[jax.ShapeDtypeStruct((cols, SDEV), jnp.float32)] + [sent] * (peers - 1),
        scratch_shapes=[
            pltpu.VMEM((peers, cols, SDEV), jnp.float32),
            pltpu.VMEM((peers * cols, edge_count), rows.dtype),
            pltpu.VMEM((edge_count, LANE), jnp.float32),
            pltpu.VMEM((IW, per, LANE), jnp.float32),
            pltpu.VMEM((per, LANE), jnp.float32),
            pltpu.VMEM((peers, IW + 8, recs), jnp.int32),
            pltpu.VMEM((LANE, recs), jnp.float32),
            pltpu.SemaphoreType.DMA((parts, peers)),
            pltpu.SemaphoreType.DMA((peers, IW + 1)),
        ]
        + [pltpu.SMEM((1, recs), jnp.int32)] * (peers * (IW + 1))
        + [pltpu.VMEM((peers * SDEV, LANE), jnp.float32)] * peers,
        compiler_params=pltpu.CompilerParams(vmem_limit_bytes=24 << 20),
        cost_estimate=pl.CostEstimate(
            flops=2 * recs * peers * IW * 8 * LANE, bytes_accessed=64 << 20, transcendentals=0
        ),
        name="site_sums",
    )(me, rows, *lists)
    return out[0], out[1:]


def place_kernel(peers, me_ref, _, *refs):
    out_ref = refs[peers]
    cols, width = refs[0].shape
    for s in range(peers):
        at = lax.rem(me_ref[0] + peers - s, peers) * cols
        block = refs[s][:, :width].astype(jnp.int32) if s else refs[s][...]
        if s:
            power = refs[s][:, width:].astype(jnp.int32).astype(jnp.float32)
            block = block.astype(jnp.float32) * (jnp.exp2(power[:, :1]) * (1 / TOP))
        out_ref[pl.ds(pl.multiple_of(at, 8), cols), :] = block


def placed_rows(me, after, got, peers):
    cols, width = got[0].shape
    return pl.pallas_call(
        functools.partial(place_kernel, peers),
        in_specs=[SMEM] + [VMEM] * (peers + 1),
        out_specs=VMEM,
        out_shape=jax.ShapeDtypeStruct((peers * cols, width), got[0].dtype),
        compiler_params=pltpu.CompilerParams(vmem_limit_bytes=4 << 20),
        name="placed_rows",
    )(me, after, *got)


def band_kernel(first_ref, index_ref, values_ref, band_ref, pick, lines):
    step = pl.program_id(0)
    rows = values_ref.shape[0]
    deep = rows * rows
    half = lax.broadcasted_iota(jnp.int32, (1, 2 * BS), 1) // BS

    @pl.when(step == 0)
    def _():
        line = lax.broadcasted_iota(jnp.int32, pick.shape, 0)
        wanted = (line % (2 * rows)) // 2 * rows + line // (2 * rows)
        same = wanted == lax.broadcasted_iota(jnp.int32, pick.shape, 1)
        pick[...] = jnp.where(same, 1.0, 0.0).astype(pick.dtype)

    odd = lax.broadcasted_iota(jnp.int32, (2 * deep, 1), 0) % 2
    parts = lines.shape[1] // (2 * rows)

    def stacked(part):
        at = [(part * rows + j) * 2 * BS for j in range(rows)]
        return jnp.concatenate([values_ref[:, i : i + 2 * BS] for i in at], axis=0)

    for first in range(0, parts, 2):
        pair = jnp.concatenate([stacked(first), stacked(first + 1)], axis=1)
        picked = jnp.dot(pick[...], pair, preferred_element_type=jnp.float32)
        for part in range(first, first + 2):
            at = (part - first) * 2 * BS
            both = picked[:, at : at + 2 * BS]
            crossed = pltpu.roll(both, BS, 1)
            twice = jnp.where(half == odd, both, crossed).astype(lines.dtype)
            for row in range(rows):
                lines[row, part * 2 * rows : (part + 1) * 2 * rows, :] = twice[
                    row * 2 * rows : (row + 1) * 2 * rows
                ]

    def group(trip, _):
        p = step * GROUPS + trip
        base = GROUP * p - HB + first_ref[0]
        for row in range(GROUP):
            offs = [index_ref[k, GROUP * p + row] - base for k in range(NNZB)]
            blocks = [
                lines[trip * GROUP + row, k * BS : (k + 1) * BS, :] for k in range(NNZB)
            ]
            for tile in range(REACH // (2 * BS)):
                at = slice(tile * 2 * BS, (tile + 1) * 2 * BS)
                if row // 2 <= tile <= (row + 2 * HB) // 2:
                    masks = [
                        jnp.where(half + 2 * tile == off, 1.0, 0.0).astype(band_ref.dtype)
                        for off in offs
                    ]
                    total = blocks[0] * masks[0]
                    for k in range(1, NNZB):
                        total += blocks[k] * masks[k]
                else:
                    total = jnp.zeros((BS, 2 * BS), band_ref.dtype)
                band_ref[p, row * BS : (row + 1) * BS, at] = total
        return 0

    lax.fori_loop(0, GROUPS, group, 0)


def banded(kblocks, blk_index, first_block):
    count, values = kblocks.shape
    groups = count // GROUP
    rows = GROUPS * GROUP
    return pl.pallas_call(
        band_kernel,
        grid=(count // rows,),
        in_specs=[SMEM, SMEM, pl.BlockSpec((rows, values), lambda i: (i, 0))],
        out_specs=VMEM,
        scratch_shapes=[
            pltpu.VMEM((2 * rows * rows, rows * rows), kblocks.dtype),
            pltpu.VMEM((rows, NNZB * BS, 2 * BS), kblocks.dtype),
        ],
        out_shape=jax.ShapeDtypeStruct((groups, GROUP * BS, REACH), jnp.bfloat16),
        compiler_params=pltpu.CompilerParams(vmem_limit_bytes=28 << 20),
        cost_estimate=pl.CostEstimate(flops=0, bytes_accessed=40 << 20, transcendentals=0),
        name="banded",
    )(first_block, blk_index.T, pltpu.with_memory_space_constraint(kblocks, pltpu.HBM))


def residual_kernel(peers, first, low, keep, parts, ready, me_ref, *refs):
    pieces = [refs[j * (peers - 1) : (j + 1) * (peers - 1)] for j in range(parts)]
    refs = refs[parts * (peers - 1) :]
    if keep:
        ends, refs = refs[: peers - 1], refs[peers - 1 :]
    rows_ref, band_ref, sigma_ref = refs[:3]
    out_ref, token_ref, panel, swap, *refs = refs[3 if keep == 0 else 4 :]
    if not ready:
        own, own_sem = refs
    cols, span = rows_ref.shape if ready else own.shape
    columns = panel.shape[0]
    step = pl.program_id(0)
    width = GROUPS * GROUP * BS
    me = me_ref[0]

    @pl.when(step == 0)
    def _():
        token_ref[...] = jnp.zeros_like(token_ref)
        if not ready:
            at = start_of(me, peers, rows_ref.shape[1]) + (low - keep)
            copy = pltpu.make_async_copy(
                rows_ref.at[:, pl.ds(pl.multiple_of(at, RIM), span)], own, own_sem
            )
            copy.start()
        panel[:, :RIM] = jnp.zeros((columns, RIM), panel.dtype)
        panel[:, RIM + span :] = jnp.zeros((columns, RIM), panel.dtype)
        row = lax.broadcasted_iota(jnp.int32, (columns, columns), 0)
        col = lax.broadcasted_iota(jnp.int32, (columns, columns), 1)
        sign = jnp.where(row % 2 == 0, -1.0, 1.0)
        swap[...] = jnp.where(row + 1 - 2 * (row % 2) == col, sign, 0.0).astype(swap.dtype)
        for s in range(1, peers):
            at = pl.ds(pl.multiple_of(lax.rem(me + peers - s, peers) * cols, cols), cols)
            if keep:
                panel[at, RIM : RIM + keep] = ends[s - 1][:, ends[s - 1].shape[1] - keep :]
            lane = RIM + keep
            for part in pieces:
                width_of = part[s - 1].shape[1]
                panel[at, lane : lane + width_of] = part[s - 1][...]
                lane += width_of
        if not ready:
            copy.wait()
        mine = pl.ds(pl.multiple_of(me * cols, cols), cols)
        panel[mine, RIM : RIM + span] = rows_ref[...] if ready else own[...]

    moved = jnp.where(me == 0, -RIM, jnp.where(me == peers - 1, RIM, 0))
    start = (step + first) * width + RIM + moved - (low - keep)

    def window(at, size):
        return panel[:, pl.ds(pl.multiple_of(start + at, RIM), size)]

    swapped = jnp.dot(swap[...], window(RIM, width), preferred_element_type=jnp.float32)
    at = pl.multiple_of((step + first) * width, width)
    turned = swapped * sigma_ref[:, pl.ds(at, width)]
    for t in range(GROUPS):
        at = slice(t * GROUP * BS, (t + 1) * GROUP * BS)
        stiff = lax.dot_general(
            window(t * GROUP * BS, REACH),
            band_ref[(step + first) * GROUPS + t],
            (((1,), (1,)), ((), ())),
            preferred_element_type=jnp.float32,
        )
        out_ref[:, at] = (stiff + turned[:, at]).astype(out_ref.dtype)


def own_kernel(peers, low, me_ref, rows_ref, out_ref, sem):
    at = start_of(me_ref[0], peers, rows_ref.shape[1]) + low
    copy = pltpu.make_async_copy(
        rows_ref.at[:, pl.ds(pl.multiple_of(at, RIM), out_ref.shape[1])], out_ref, sem
    )
    copy.start()
    copy.wait()


def own_piece(me, rows, peers, low):
    cols, all_edges = rows.shape
    width = all_edges // peers + 2 * RIM - low
    return pl.pallas_call(
        functools.partial(own_kernel, peers, low),
        in_specs=[SMEM, HBM],
        out_specs=VMEM,
        out_shape=jax.ShapeDtypeStruct((cols, width), rows.dtype),
        scratch_shapes=[pltpu.SemaphoreType.DMA],
        compiler_params=pltpu.CompilerParams(vmem_limit_bytes=2 << 20),
        cost_estimate=pl.CostEstimate(flops=0, bytes_accessed=1 << 20, transcendentals=0),
        name="own_piece",
    )(me, rows)


def residual_of(rows, ready, parts, band, sigma, me, peers):
    cols = rows.shape[0]
    edge_count = sigma.shape[0]
    columns = peers * cols
    width = GROUPS * GROUP * BS
    sigma = sigma.reshape(1, edge_count)
    out, before = None, None
    calls = [parts[:3], parts[3:]]
    for call in calls:
        first, low = call[0][0], call[0][2]
        steps = sum(part[1] for part in call)
        keep = KEEP if low else 0
        span = keep + sum(part[3][0].shape[1] for part in call)
        given = [x for part in call for x in part[3]]
        last = call is calls[-1]
        given += (list(before) if keep else []) + [ready if last else rows, band, sigma]
        specs = [VMEM] * (len(given) - 3) + [VMEM if last else HBM, VMEM, VMEM]
        if out is not None:
            given.append(out)
            specs.append(pl.BlockSpec(memory_space=pl.ANY))
        out, token = pl.pallas_call(
            functools.partial(residual_kernel, peers, first, low, keep, len(call), last),
            grid_spec=pltpu.PrefetchScalarGridSpec(
                num_scalar_prefetch=1,
                grid=(steps,),
                in_specs=specs,
                out_specs=[
                    pl.BlockSpec((columns, width), lambda i, me, first=first: (0, i + first)),
                    pl.BlockSpec((8, LANE), lambda i, me: (0, 0)),
                ],
                scratch_shapes=[
                    pltpu.VMEM((columns, span + 2 * RIM), jnp.bfloat16),
                    pltpu.VMEM((columns, columns), jnp.bfloat16),
                ]
                + ([] if last else [pltpu.VMEM((cols, span), rows.dtype), pltpu.SemaphoreType.DMA]),
            ),
            out_shape=[
                jax.ShapeDtypeStruct((columns, edge_count), jnp.bfloat16),
                jax.ShapeDtypeStruct((8, LANE), jnp.float32),
            ],
            input_output_aliases={len(given): 0} if out is not None else {},
            compiler_params=pltpu.CompilerParams(vmem_limit_bytes=24 << 20),
            cost_estimate=pl.CostEstimate(
                flops=2 * columns * steps * width * 384,
                bytes_accessed=(21 << 20) * steps * width // edge_count,
                transcendentals=0,
            ),
        )(me, *given)
        before = call[-1][3]
    return out, token


def on_device(fields, kblocks, blk_index, sigma, rec_edge, rec_weight, rec_owner, rec_slot):
    return ordered(
        fields, kblocks, blk_index, sigma, rec_edge, rec_weight, rec_owner, rec_slot
    )


def ordered(fields, kblocks, blk_index, sigma, rec_edge, rec_weight, rec_owner, rec_slot):
    peers = lax.axis_size("edge")
    shares = lax.axis_size("tx") * lax.axis_size("rcv")
    me = jnp.stack([lax.axis_index("edge"), lax.axis_index(("tx", "rcv"))])
    rows = fields[0]
    edge_count = sigma.shape[0]
    shifts = range(1, peers)

    length = edge_count + 2 * RIM
    width = GROUPS * GROUP * BS
    marks = [0, 1, 7, 12, 16]
    lanes = [0] + [m * width + KEEP - RIM for m in marks[1:-1]] + [length]

    rows = pltpu.with_memory_space_constraint(rows, pltpu.HBM)
    mine, blocks = packed(me, rec_edge, rec_weight, rec_owner, rec_slot, rows, peers, lanes, shares)
    parts = []
    for j in range(len(lanes) - 1):
        pieces = [shifted(blocks[j * (peers - 1) + s - 1], s, peers) for s in shifts]
        parts.append((marks[j], marks[j + 1] - marks[j], lanes[j], pieces))
    lists = [mine] + [shifted(mine, s, peers) for s in shifts]
    lists = jnp.concatenate(lists, axis=0)
    lists = [lists] + [
        lax.ppermute(lists, ("tx", "rcv"), [(i, (i + k) % shares) for i in range(shares)])
        for k in range(1, shares)
    ]
    band = banded(kblocks, blk_index, me[:1] * (edge_count // BS))
    own, sent = site_sums(me, rows, lists, peers)
    got = [own] + [shifted(sent[s - 1], s, peers) for s in shifts]
    low = lanes[-2] - KEEP
    ready = own_piece(me, rows, peers, low)
    residual, token = residual_of(rows, ready, parts, band, sigma, me, peers)
    site_out = placed_rows(me, token, got, peers)
    return residual[None], site_out[None]


def fits(mesh, fields, sigma, rec_edge):
    peers = mesh.shape["edge"]
    cols = fields.shape[1] // peers
    edge_count = sigma.shape[0] // (mesh.shape["grp"] * peers)
    recs = rec_edge.shape[0] // (mesh.shape["grp"] * peers)
    return (
        cols % 16 == 0
        and cols * peers == LANE
        and peers * IW <= LANE
        and edge_count % (GROUPS * GROUP * BS) == 0
        and edge_count >= 8 * GROUPS * GROUP * BS
        and recs % (LANE * mesh.shape["tx"] * mesh.shape["rcv"]) == 0
        and peers > 1
    )


def solution(mesh):
    placed = (
        P(("grp", "tx", "rcv"), "edge", None),
        P("edge", None),
        P("edge", None),
        P(("grp", "edge")),
        P(("grp", "edge"), None),
        P(("grp", "edge"), None),
        P(("grp", "edge"), None),
        P(("grp", "edge")),
    )

    def run(fields, kblocks, blk_index, sigma, rec_edge, rec_weight, rec_owner, rec_slot):
        body = on_device if fits(mesh, fields, sigma, rec_edge) else plain_device
        return jax.shard_map(
            body,
            mesh=mesh,
            in_specs=placed,
            out_specs=(P(("grp", "tx", "rcv"), None, "edge"), P(("grp", "tx", "rcv"), None, "edge")),
            check_vma=False,
        )(fields, kblocks, blk_index, sigma, rec_edge, rec_weight, rec_owner, rec_slot)

    return run
```
